32 devices in a mesh: grp: 8 (over z, y), dp: 4 (over x, core).
Axes of the slice: x: 2, y: 2, z: 4, core: 2. Of those that a mesh axis runs over, the one named last changes fastest.
Arguments:
- hidden: bfloat16 [32768, 768], P(('grp', 'dp')), may hold values from -6 to 6
- lengths: int32 [32], P(('grp', 'dp')), may hold values from 512 to 1024, as said below
- subnet: int32 [8, 3], replicated, may hold values from 0 to 2
- qkv_weight: bfloat16 [768, 2304], P(('grp', 'dp')), may hold values from -0.21875 to 0.21875
- qv_bias: bfloat16 [2, 768], P(None, ('grp', 'dp')), may hold values from -3 to 3
- out_weight: bfloat16 [768, 768], P(('grp', 'dp')), may hold values from -3.5 to 3.5
- up_weight: bfloat16 [768, 3072], P(('grp', 'dp')), may hold values from -0.21875 to 0.21875
- up_bias: bfloat16 [3072], P(('grp', 'dp')), may hold values from -3 to 3
- down_weight: bfloat16 [3072, 768], P(('grp', 'dp')), may hold values from -0.109375 to 0.109375
- norm_gains: bfloat16 [2, 768], P(None, ('grp', 'dp')), may hold values from 0.25 to 1.75
- bias_rows: bfloat16 [4, 768], P(None, ('grp', 'dp')), may hold values from -3 to 3
- cotangent: bfloat16 [32768, 768], P(('grp', 'dp')), may hold values from -6 to 6
Outputs:
- output: bfloat16 [32768, 768], P(('grp', 'dp'))
- grad_hidden: bfloat16 [32768, 768], P(('grp', 'dp'))
- grad_qkv_weight: float32 [768, 2304], P(('grp', 'dp'))
- grad_qv_bias: float32 [2, 768], P(None, ('grp', 'dp'))
- grad_out_weight: float32 [768, 768], P(('grp', 'dp'))
- grad_up_weight: float32 [768, 3072], P(('grp', 'dp'))
- grad_up_bias: float32 [3072], P(('grp', 'dp'))
- grad_down_weight: float32 [3072, 768], P(('grp', 'dp'))
- grad_norm_gains: float32 [2, 768], P(None, ('grp', 'dp'))
- grad_bias_rows: float32 [4, 768], P(None, ('grp', 'dp'))
The draws below stay inside these ranges and needn't reach their ends.
Inputs may be any that keep to these rules, and one draw needn't show every extreme that they name: `lengths`: the sequences of one device come from one of four length buckets; some sequence has exactly 1024 frames.
All inputs are finite; a program needn't handle non-finite values.
Results may differ from the reference program's by a relative error of at most 0.015.
Values may be sent and summed in bfloat16 or wider, within the bound.
No kernel may reach another device: no remote copies, remote signals or barrier semaphores. Data moves between devices by JAX's collectives and lax.ppermute only.
A program may use at most 192 MiB of HBM per device.

```python
import jax
import jax.numpy as jnp
from jax import lax

D = 768
HEADS = 12
HDIM = 64
FF = 3072
LEN = 1024
SEQ_DEV = 1
ATT = 768
GROUPS = 8
SEQ_GRP = 4
SEQS = 32
TOKENS = 32768


def draw_lengths(key, part):
    bucket_key, extra_key, full_key = jax.random.split(jax.random.fold_in(key, 17), 3)
    devices_count = SEQS // SEQ_DEV
    bucket = jax.random.randint(bucket_key, (devices_count, 1), 0, 4)
    bucket = jnp.broadcast_to(bucket, (devices_count, SEQ_DEV)).reshape(SEQS)
    extra = jax.random.randint(extra_key, (SEQS,), 0, LEN // 8 + 1)
    drawn = LEN // 2 + bucket * (LEN // 8) + extra
    longest = jax.random.randint(full_key, (), 0, SEQS)
    drawn = jnp.where(jnp.arange(SEQS) == longest, LEN, drawn)
    return drawn.astype(jnp.int32)


def with_ends(values, rng, low, high):
    longest = values.shape.index(max(values.shape))
    spots = []
    for shift in (0, 1):
        where = [jax.random.randint(jax.random.fold_in(rng, axis), (), 0, length) for axis, length in enumerate(values.shape)]
        where[longest] = (where[longest] + shift) % values.shape[longest]
        spots.append(tuple(where))
    return values.at[spots[0]].set(low).at[spots[1]].set(high)


def with_spikes(values, rng, source, target, parts, factor):
    def block_of(position):
        return (jnp.arange(values.shape[position]) // (values.shape[position] // parts)).reshape((-1,) + (1,) * (values.ndim - 1 - position))

    near = jax.random.permutation(rng, parts)[block_of(target)]
    far = (block_of(target) + parts // 2) % parts
    return jnp.where((block_of(source) == near) | (block_of(source) == far), factor * values, values)


def levels(key, dims, cuts, low, largest):
    def one(axis_at, parts):
        draws = jax.random.uniform(jax.random.fold_in(jax.random.fold_in(key, 6), axis_at), (parts,), jnp.float32, low / len(cuts), largest / len(cuts))
        return jnp.repeat(jnp.exp(draws), dims[axis_at] // parts).reshape((-1,) + (1,) * (len(dims) - axis_at - 1))

    level = one(*cuts[0])
    for cut in cuts[1:]:
        level = level * one(*cut)
    return level


def normal_values(rng, shape, width, limit, pieces=(), held_as=jnp.bfloat16):
    array = jax.random.normal(rng, shape, jnp.float32) * width
    if len(pieces) > 0:
        array = levels(rng, shape, pieces, -0.22, 0.18) * array
    return jnp.clip(array, min=-limit, max=limit).astype(held_as)


def gaussian_with(own_key, extent, width, bound, pieces, heavy, dtype=jnp.bfloat16):
    array = width * jax.random.normal(own_key, extent, jnp.float32)
    if pieces:
        array = array * levels(own_key, extent, pieces, -0.22, 0.18)
    return jnp.clip(with_spikes(array, jax.random.fold_in(own_key, 3), *heavy), -bound, bound).astype(dtype)


def setup_inputs(seed: int = 0) -> dict:
    arg_keys = jax.random.split(jax.random.key(seed), 13)
    hidden = gaussian_with(arg_keys[0], (TOKENS, D), 1.0, 6.0, ((0, 32),), (0, 1, 32, 2.75))
    lengths = draw_lengths(jax.random.fold_in(arg_keys[12], 71), 0)
    subnet = with_ends(jax.random.randint(arg_keys[2], (GROUPS, 3), 0, 3), jax.random.fold_in(arg_keys[2], 1), 0, 2).astype(jnp.int32)
    qkv_weight = normal_values(arg_keys[3], (D, 3 * ATT), D ** -0.5, 0.21875, ((0, 32),))
    qv_bias = normal_values(arg_keys[4], (2, ATT), 0.5, 3.0, ((1, 32),))
    out_weight = normal_values(arg_keys[5], (ATT, D), (max(1, 4 * D // LEN)) ** -0.5, 3.5, ((0, 32),))
    up_weight = normal_values(arg_keys[6], (D, FF), D ** -0.5, 0.21875, ((0, 32),))
    up_bias = normal_values(arg_keys[7], (FF,), 0.5, 3.0, ((0, 32),))
    down_weight = normal_values(arg_keys[8], (FF, D), FF ** -0.5, 0.109375, ((0, 32),))
    norm_gains = jnp.clip(1.0 + 0.15 * jax.random.normal(arg_keys[9], (2, D), jnp.float32), 0.25, 1.75).astype(jnp.bfloat16)
    bias_rows = normal_values(arg_keys[10], (4, D), 0.5, 3.0, ((1, 32),))
    cotangent = normal_values(arg_keys[11], (TOKENS, D), 1.0, 6.0, ((0, 32),))
    return dict(hidden=hidden, lengths=lengths, subnet=subnet, qkv_weight=qkv_weight, qv_bias=qv_bias, out_weight=out_weight, up_weight=up_weight, up_bias=up_bias, down_weight=down_weight, norm_gains=norm_gains, bias_rows=bias_rows, cotangent=cotangent)


EPSILON = 1e-05
NEGATIVE = -1e+30
HIGHEST = lax.Precision.HIGHEST

@jax.custom_vjp
def low(v):
    return lax.optimization_barrier(v.astype(jnp.bfloat16)).astype(jnp.float32)

@jax.custom_vjp
def low_back(v):
    return v

def low_keep(v):
    return (low(v), None)

def low_pass(kept, grad):
    return (grad,)

def back_keep(v):
    return (v, None)

def back_low(kept, grad):
    return (low(grad),)
low.defvjp(low_keep, low_pass)
low_back.defvjp(back_keep, back_low)

def norm_apply(values, colmask, feat_count, norm_gain, norm_shift):
    row_mean = lax.optimization_barrier(jnp.sum(values * colmask, axis=-1, keepdims=True)) / feat_count
    centred = (values - row_mean) * colmask
    variance = lax.optimization_barrier(jnp.sum(centred * centred, axis=-1, keepdims=True)) / feat_count
    return (centred * lax.rsqrt(variance + EPSILON) * norm_gain + norm_shift) * colmask

def one_sequence(params, sequence, length, picks):
    qkv_weight, qv_bias, out_weight, up_weight, up_bias, down_weight, norm_gains, bias_rows = params
    sub_width = D - (2 - picks[0]) * (D // 6)
    sub_heads = HEADS - (2 - picks[1]) * (HEADS // 6)
    sub_inner = sub_width * (6 + picks[2]) // 2
    feat_count = sub_width.astype(jnp.float32)
    colmask = (jnp.arange(D) < sub_width).astype(jnp.float32)
    attmask = (jnp.arange(3 * ATT) % ATT < sub_heads * HDIM).astype(jnp.float32)
    ffmask = (jnp.arange(FF) < sub_inner).astype(jnp.float32)
    key_valid = jnp.arange(LEN) < length
    rowmask = key_valid.astype(jnp.float32)[:, None]
    masked_in = sequence * colmask
    bias_row = jnp.concatenate([qv_bias[0], jnp.zeros((ATT,), jnp.float32), qv_bias[1]])
    projected = jnp.dot(low(masked_in), qkv_weight, precision=HIGHEST)
    qkv_low = low(low_back((projected + bias_row) * attmask))
    queries = qkv_low[:, :ATT].reshape(LEN, HEADS, HDIM)
    key_heads = qkv_low[:, ATT:2 * ATT].reshape(LEN, HEADS, HDIM)
    value_heads = qkv_low[:, 2 * ATT:].reshape(LEN, HEADS, HDIM)
    scores = jnp.einsum('qhd,khd->hqk', queries, key_heads, precision=HIGHEST) * HDIM ** (-0.5)
    scores = jnp.where(key_valid[None, None, :], low_back(scores), NEGATIVE)
    row_top = lax.optimization_barrier(jnp.max(scores, axis=2, keepdims=True))
    exponent = jnp.exp(scores - row_top)
    softmaxed = exponent / lax.optimization_barrier(jnp.sum(exponent, axis=2, keepdims=True))
    context = jnp.einsum('hqk,khd->qhd', low(softmaxed), value_heads, precision=HIGHEST).reshape(LEN, ATT)
    context = low(low_back(context))
    attn_out = low_back((jnp.dot(context, out_weight, precision=HIGHEST) + bias_rows[0]) * colmask)
    first_sum = masked_in + attn_out
    first_norm = norm_apply(first_sum, colmask, feat_count, norm_gains[0], bias_rows[1])
    ffn_pre = low_back((jnp.dot(low(first_norm), up_weight, precision=HIGHEST) + up_bias) * ffmask)
    ffn_act = low(jax.nn.gelu(ffn_pre, approximate=False))
    ffn_out = low_back((jnp.dot(ffn_act, down_weight, precision=HIGHEST) + bias_rows[2]) * colmask)
    second_sum = first_norm + ffn_out
    return norm_apply(second_sum, colmask, feat_count, norm_gains[1], bias_rows[3]) * rowmask

def reference(hidden, lengths, subnet, qkv_weight, qv_bias, out_weight, up_weight, up_bias, down_weight, norm_gains, bias_rows, cotangent):
    params = (qkv_weight.astype(jnp.float32), qv_bias.astype(jnp.float32), out_weight.astype(jnp.float32), up_weight.astype(jnp.float32), up_bias.astype(jnp.float32), down_weight.astype(jnp.float32), norm_gains.astype(jnp.float32), bias_rows.astype(jnp.float32))
    inputs = hidden.astype(jnp.float32).reshape(SEQS, LEN, D)
    group_rows = subnet[(jnp.arange(SEQS) // SEQ_GRP).astype(jnp.int32)]
    checked = jax.checkpoint(one_sequence)

    def forward(weights, frames):

        def apply_one(packed):
            return checked(weights, packed[0], packed[1], packed[2])
        return lax.map(apply_one, (frames, lengths, group_rows))
    result, pull_back = jax.vjp(forward, params, inputs)
    weight_grads, input_grad = pull_back(cotangent.astype(jnp.float32).reshape(SEQS, LEN, D))
    output = result.reshape(TOKENS, D).astype(jnp.bfloat16)
    grad_hidden = (0.1 * input_grad.reshape(TOKENS, D)).astype(jnp.bfloat16)
    return (output, grad_hidden, weight_grads[0], weight_grads[1], weight_grads[2], weight_grads[3], weight_grads[4], weight_grads[5], weight_grads[6], weight_grads[7])
```

```python
import functools

import jax
import jax.numpy as jnp
from jax import lax
from jax.experimental import pallas as pl
from jax.experimental.pallas import tpu as pltpu
from jax.sharding import PartitionSpec as P

D = 768
HEADS = 12
HDIM = 64
FF = 3072
LEN = 1024
ATT = 768
PAIRS = HEADS // 2

EPSILON = 1e-05
NEGATIVE = -1e30

UNITS = 32
ROWS = D // UNITS
FROWS = FF // UNITS
PAIR = 2 * ROWS
CHIPS = UNITS // 2
EXTRA = 128
QCOLS = 3 * ATT + 2 * EXTRA
UCOLS = D + FF

BF = jnp.bfloat16
F32 = jnp.float32
SEND = jnp.bfloat16

NN = (((1,), (0,)), ((), ()))
NT = (((1,), (1,)), ((), ()))
TN = (((0,), (0,)), ((), ()))

CORE, AX, AY, Z1, Z2 = 1, 2, 4, 8, 16


def mm(a, b, dims, precision=None):
    return lax.dot_general(a, b, dims, precision=precision, preferred_element_type=F32)


def params(megabytes):
    return pltpu.CompilerParams(vmem_limit_bytes=megabytes << 20)


def cost(micros):
    return pl.CostEstimate(
        flops=int(micros * 1.1e9), transcendentals=0, bytes_accessed=int(micros * 1e6)
    )


def owner(position, masks):
    offset = 0
    for bit, mask in enumerate(masks):
        if (position >> bit) & 1:
            offset ^= mask
    return offset


GATHER = ((Z2, Z1, AX, AY), (Z2, Z1, AY, AX))
SCATTER = ((Z2, Z1, AY, AX), (Z2, Z1, AX, AY))


def held(me, position, orders, sibling=False):
    even, odd = owner(position, orders[0]), owner(position, orders[1])
    parity = me & 1
    if sibling:
        me, parity = me ^ CORE, 1 - parity
    return me ^ jnp.where(parity == 0, even, odd)


def after(x, *others):
    return lax.optimization_barrier((x,) + others)


def iota(shape, axis):
    return lax.broadcasted_iota(jnp.int32, shape, axis)


def spread(width, period, columns):
    col = iota((width, columns), 1)
    turn = jnp.floor((col.astype(F32) + 0.5) * (1.0 / period)).astype(jnp.int32)
    return jnp.where(col - turn * period == iota((width, columns), 0), 1.0, 0.0)


QKV_BLOCK = 256


def qkv_kernel(sc, x_ref, own, other, qkv_ref, w_ref, small_ref, upb_ref, sem):
    me, width, att = sc[0], sc[1], sc[2]

    @pl.when(pl.program_id(0) == 0)
    def _():
        copies = []
        half = QCOLS // 2
        for source, sibling in ((own, False), (other, True)):
            side = (me & 1) ^ 1 if sibling else me & 1
            col = pl.multiple_of(side * half, 128)
            for position in range(CHIPS):
                chip = held(me, position, GATHER, sibling) >> 1
                row = pl.multiple_of(chip * PAIR, 16)
                copies.append(
                    pltpu.make_async_copy(
                        source.at[position],
                        w_ref.at[pl.ds(row, PAIR), pl.ds(col, half)],
                        sem.at[len(copies)],
                    )
                )
                copies[-1].start()
        for copy in copies:
            copy.wait()
        extra = w_ref[:, 3 * ATT : 3 * ATT + EXTRA]
        wide = mm(extra, spread(EXTRA, ROWS, D).astype(BF), NN).reshape(UNITS, ROWS, D)
        shape = (UNITS, ROWS, D)
        start = iota(shape, 0) * ROWS
        lane = iota(shape, 2)
        mine = (lane >= start) & (lane < start + ROWS)
        small_ref[...] = jnp.sum(jnp.where(mine, wide, 0.0), axis=0)
        row8 = extra.reshape(UNITS, ROWS, EXTRA)[:, 8, :]
        wide = mm(row8, spread(EXTRA, FROWS, FF).astype(BF), NN)
        start = iota((UNITS, FF), 0) * FROWS
        lane = iota((UNITS, FF), 1)
        mine = (lane >= start) & (lane < start + FROWS)
        upb_ref[...] = jnp.sum(jnp.where(mine, wide, 0.0), axis=0, keepdims=True)

    x = x_ref[...]
    x = jnp.where(iota(x.shape, 1) < width, x, jnp.zeros_like(x))
    on = iota((1, ATT), 1) < att
    for third in range(3):
        part = mm(x, w_ref[:, third * ATT : (third + 1) * ATT], NN)
        if third == 0:
            part = part + small_ref[0:1, :]
        if third == 2:
            part = part + small_ref[1:2, :]
        part = jnp.where(on, part, 0.0).astype(BF)
        if third == 0:
            part = part * jnp.asarray(HDIM ** (-0.5), BF)
        qkv_ref[:, third * ATT : (third + 1) * ATT] = part


def qkv_call(sc, hidden, own, other):
    hbm = pl.BlockSpec(memory_space=pl.ANY)
    return pl.pallas_call(
        qkv_kernel,
        out_shape=(
            jax.ShapeDtypeStruct((LEN, 3 * ATT), BF),
            jax.ShapeDtypeStruct((D, QCOLS), BF),
            jax.ShapeDtypeStruct((ROWS, D), F32),
            jax.ShapeDtypeStruct((1, FF), F32),
        ),
        grid_spec=pltpu.PrefetchScalarGridSpec(
            num_scalar_prefetch=1,
            grid=(LEN // QKV_BLOCK,),
            in_specs=[pl.BlockSpec((QKV_BLOCK, D), lambda i, s: (i, 0)), hbm, hbm],
            out_specs=[
                pl.BlockSpec((QKV_BLOCK, 3 * ATT), lambda i, s: (i, 0)),
                pl.BlockSpec((D, QCOLS), lambda i, s: (0, 0)),
                pl.BlockSpec((ROWS, D), lambda i, s: (0, 0)),
                pl.BlockSpec((1, FF), lambda i, s: (0, 0)),
            ],
            scratch_shapes=[pltpu.SemaphoreType.DMA((UNITS,))],
        ),
        compiler_params=params(48),
        cost_estimate=cost(10),
        name="qkv",
    )(sc, hidden, own, other)


FWD_BLOCK = 512


def attend_kernel(sc, q_ref, k_ref, v_ref, o_ref, e_ref, inv_ref):
    length = sc[4]
    half = LEN // 2
    lane = iota((LEN, 128), 1)
    edge = jnp.where(iota((1, half), 1) + half < length, 0.0, NEGATIVE)
    k = k_ref[...]
    v = v_ref[...]
    heads = []
    for h in range(2):
        mine = (lane // HDIM) == h
        heads.append(
            (jnp.where(mine, k, jnp.zeros_like(k)), jnp.where(mine, v, jnp.ones_like(v)))
        )
    left = iota((FWD_BLOCK, 128), 1) < HDIM
    for b in range(LEN // FWD_BLOCK):
        rows = slice(b * FWD_BLOCK, (b + 1) * FWD_BLOCK)
        q = q_ref[rows, :]
        outs, invs = [], []
        for h in range(2):
            keys, values = heads[h]
            scores = mm(q, keys, NT)
            sa = scores[:, :half]
            sb = scores[:, half:] + edge
            top = jnp.maximum(
                jnp.max(sa, axis=1, keepdims=True), jnp.max(sb, axis=1, keepdims=True)
            )
            ea = jnp.exp(sa - top).astype(BF)
            eb = jnp.exp(sb - top).astype(BF)
            e_ref[h, rows, :half] = ea
            e_ref[h, rows, half:] = eb
            o = mm(ea, values[:half], NN) + mm(eb, values[half:], NN)
            inv = 1.0 / pltpu.roll(o, HDIM, 1)
            outs.append(o * inv)
            invs.append(inv)
        o_ref[rows, :] = jnp.where(left, outs[0], outs[1]).astype(BF)
        inv_ref[rows, :] = jnp.where(left, invs[0], invs[1])


def attend_call(sc, qkv, first, pairs):
    def spec(offset):
        return pl.BlockSpec((LEN, 128), lambda i, s: (0, offset + first + i))

    out = pl.BlockSpec((LEN, 128), lambda i, s: (0, i))

    return pl.pallas_call(
        attend_kernel,
        out_shape=(
            jax.ShapeDtypeStruct((LEN, pairs * 128), BF),
            jax.ShapeDtypeStruct((2 * pairs, LEN, LEN), BF),
            jax.ShapeDtypeStruct((LEN, pairs * 128), F32),
        ),
        grid_spec=pltpu.PrefetchScalarGridSpec(
            num_scalar_prefetch=1,
            grid=(pairs,),
            in_specs=[spec(0), spec(PAIRS), spec(2 * PAIRS)],
            out_specs=[out, pl.BlockSpec((2, LEN, LEN), lambda i, s: (i, 0, 0)), out],
        ),
        compiler_params=params(56),
        cost_estimate=cost(4 * pairs),
        name="attend",
    )(sc, qkv, qkv, qkv)


CHAIN_BLOCK = 256
HALF = ATT // 2
CHUNK = 768


def normal_parts(x):
    z = jnp.abs(x) * 0.7071067811865476
    t = 1.0 / (1.0 + 0.3275911 * z)
    gauss = jnp.exp(-0.5 * x * x)
    poly = t * (
        0.254829592
        + t * (-0.284496736 + t * (1.421413741 + t * (-1.453152027 + t * 1.061405429)))
    )
    tail = 0.5 * poly * gauss
    return jnp.where(x >= 0, 1.0 - tail, tail), gauss * 0.3989422804014327


def normalise(v, cm, count):
    mean = jnp.sum(v, axis=1, keepdims=True) / count
    centred = (v - mean) * cm
    var = jnp.sum(centred * centred, axis=1, keepdims=True) / count
    r = lax.rsqrt(var + EPSILON)
    return centred * r, r


def normalise_back(e, yhat, r, gain, cm, count):
    t = e * gain * cm
    s1 = jnp.sum(t, axis=1, keepdims=True) / count
    s2 = jnp.sum(t * yhat, axis=1, keepdims=True) / count
    return r * cm * (t - s1 - yhat * s2)


def width_mask(width):
    return jnp.where(iota((1, D), 1) < width, 1.0, 0.0)


def column_sum(x):
    return jnp.sum(x.astype(F32), axis=0, keepdims=True)


def rise_kernel(
    sc,
    ctx0_ref,
    ctx1_ref,
    hid_ref,
    small_ref,
    upb_ref,
    u0,
    u1,
    first_ref,
    nlow_ref,
    act_ref,
    slope_ref,
    wu_ref,
    sem,
):
    me, width, inner = sc[0], sc[1], sc[3]

    @pl.when(pl.program_id(0) == 0)
    def _():
        copies = []
        half = UCOLS // 2
        for source, sibling in ((u0, False), (u1, True)):
            side = (me & 1) ^ 1 if sibling else me & 1
            col = pl.multiple_of(side * half, 128)
            for position in range(CHIPS):
                chip = held(me, position, GATHER, sibling) >> 1
                row = pl.multiple_of(chip * PAIR, 16)
                copies.append(
                    pltpu.make_async_copy(
                        source.at[position],
                        wu_ref.at[pl.ds(row, PAIR), pl.ds(col, half)],
                        sem.at[len(copies)],
                    )
                )
                copies[-1].start()
        for copy in copies:
            copy.wait()

    cm = width_mask(width)
    gain1, bias0, shift1 = small_ref[2:3, :], small_ref[4:5, :], small_ref[5:6, :]
    x = hid_ref[...].astype(F32) * cm
    projected = mm(ctx0_ref[...], wu_ref[:HALF, :D], NN) + mm(
        ctx1_ref[...], wu_ref[HALF:, :D], NN
    )
    first = x + (projected + bias0) * cm
    first_ref[...] = first
    yhat, _ = normalise(first, cm, width.astype(F32))
    nlow = ((yhat * gain1 + shift1) * cm).astype(BF)
    nlow_ref[...] = nlow
    for j in range(FF // CHUNK):
        cols = slice(j * CHUNK, (j + 1) * CHUNK)
        up_cols = slice(D + j * CHUNK, D + (j + 1) * CHUNK)
        fm = jnp.where(iota((1, CHUNK), 1) + j * CHUNK < inner, 1.0, 0.0)
        pre = (mm(nlow, wu_ref[:, up_cols], NN) + upb_ref[:, cols]) * fm
        cdf, pdf = normal_parts(pre)
        act_ref[:, cols] = (pre * cdf).astype(BF)
        slope_ref[:, cols] = (cdf + pre * pdf) * fm


def row_spec(cols):
    return pl.BlockSpec((CHAIN_BLOCK, cols), lambda i, s: (i, 0))


def whole_spec(*shape):
    return pl.BlockSpec(shape, lambda i, s: (0,) * len(shape))


def row_shape(cols, dtype=BF):
    return jax.ShapeDtypeStruct((LEN, cols), dtype)


def rise_call(sc, ctx0, ctx1, hidden, small, upb, u0, u1):
    hbm = pl.BlockSpec(memory_space=pl.ANY)
    return pl.pallas_call(
        rise_kernel,
        out_shape=(
            row_shape(D, F32),
            row_shape(D),
            row_shape(FF),
            row_shape(FF, F32),
            jax.ShapeDtypeStruct((D, UCOLS), BF),
        ),
        grid_spec=pltpu.PrefetchScalarGridSpec(
            num_scalar_prefetch=1,
            grid=(LEN // CHAIN_BLOCK,),
            in_specs=[row_spec(HALF)] * 2
            + [row_spec(D), whole_spec(ROWS, D), whole_spec(1, FF), hbm, hbm],
            out_specs=[
                row_spec(D),
                row_spec(D),
                row_spec(FF),
                row_spec(FF),
                whole_spec(D, UCOLS),
            ],
            scratch_shapes=[pltpu.SemaphoreType.DMA((UNITS,))],
        ),
        compiler_params=params(56),
        cost_estimate=cost(18),
        name="rise",
    )(sc, ctx0, ctx1, hidden, small, upb, u0, u1)


def fall_kernel(
    sc,
    first_ref,
    act_ref,
    slope_ref,
    cot_ref,
    small_ref,
    wu_ref,
    d0,
    d1,
    out_ref,
    fgrad_ref,
    pgrad_ref,
    agrad_ref,
    igrad_ref,
    cgrad_ref,
    sums_ref,
    usum_ref,
    wd_ref,
    sem,
):
    me, width, length = sc[0], sc[1], sc[4]
    step = pl.program_id(0)

    @pl.when(step == 0)
    def _():
        copies = []
        for source, sibling in ((d0, False), (d1, True)):
            for position in range(CHIPS):
                unit = held(me, position, GATHER, sibling)
                row = pl.multiple_of(unit * FROWS, 16)
                copies.append(
                    pltpu.make_async_copy(
                        source.at[position],
                        wd_ref.at[pl.ds(row, FROWS), :],
                        sem.at[len(copies)],
                    )
                )
                copies[-1].start()
        sums_ref[...] = jnp.zeros_like(sums_ref)
        usum_ref[...] = jnp.zeros_like(usum_ref)
        for copy in copies:
            copy.wait()

    cm = width_mask(width)
    count = width.astype(F32)
    rowpos = step * CHAIN_BLOCK + iota((CHAIN_BLOCK, 1), 0)
    rm = jnp.where(rowpos < length, 1.0, 0.0)
    gain1, gain2 = small_ref[2:3, :], small_ref[3:4, :]
    shift1, bias2, shift3 = small_ref[5:6, :], small_ref[6:7, :], small_ref[7:8, :]

    yhat1, r1 = normalise(first_ref[...], cm, count)
    normed1 = (yhat1 * gain1 + shift1) * cm
    second = normed1 + (mm(act_ref[...], wd_ref[...], NN) + bias2) * cm
    yhat2, r2 = normalise(second, cm, count)
    out_ref[...] = ((yhat2 * gain2 + shift3) * cm * rm).astype(BF)
    e2 = cot_ref[...].astype(F32) * rm
    sums_ref[3:4, :] += column_sum(e2 * yhat2)
    sums_ref[7:8, :] += column_sum(e2 * cm)
    second_grad = normalise_back(e2, yhat2, r2, gain2, cm, count)
    fgrad = second_grad.astype(BF)
    fgrad_ref[...] = fgrad
    sums_ref[6:7, :] += column_sum(fgrad)
    total = second_grad
    for j in range(FF // CHUNK):
        cols = slice(j * CHUNK, (j + 1) * CHUNK)
        up_cols = slice(D + j * CHUNK, D + (j + 1) * CHUNK)
        pgrad = (mm(fgrad, wd_ref[cols, :], NT) * slope_ref[:, cols]).astype(BF)
        pgrad_ref[:, cols] = pgrad
        usum_ref[:, cols] += column_sum(pgrad)
        total = total + mm(pgrad, wu_ref[:, up_cols], NT)
    sums_ref[2:3, :] += column_sum(total * yhat1)
    sums_ref[5:6, :] += column_sum(total * cm)
    first_grad = normalise_back(total, yhat1, r1, gain1, cm, count)
    igrad_ref[...] = first_grad
    agrad = first_grad.astype(BF)
    agrad_ref[...] = agrad
    sums_ref[4:5, :] += column_sum(agrad)
    cgrad_ref[...] = mm(agrad, wu_ref[:, :D], NT).astype(BF)


def fall_call(sc, first, act, slope, cotangent, small, wu, d0, d1):
    hbm = pl.BlockSpec(memory_space=pl.ANY)
    return pl.pallas_call(
        fall_kernel,
        out_shape=(
            row_shape(D),
            row_shape(D),
            row_shape(FF),
            row_shape(D),
            row_shape(D, F32),
            row_shape(ATT),
            jax.ShapeDtypeStruct((8, D), F32),
            jax.ShapeDtypeStruct((1, FF), F32),
        ),
        grid_spec=pltpu.PrefetchScalarGridSpec(
            num_scalar_prefetch=1,
            grid=(LEN // CHAIN_BLOCK,),
            in_specs=[
                row_spec(D),
                row_spec(FF),
                row_spec(FF),
                row_spec(D),
                whole_spec(ROWS, D),
                whole_spec(D, UCOLS),
                hbm,
                hbm,
            ],
            out_specs=[
                row_spec(D),
                row_spec(D),
                row_spec(FF),
                row_spec(D),
                row_spec(D),
                row_spec(ATT),
                whole_spec(8, D),
                whole_spec(1, FF),
            ],
            scratch_shapes=[pltpu.VMEM((FF, D), BF), pltpu.SemaphoreType.DMA((UNITS,))],
        ),
        compiler_params=params(58),
        cost_estimate=cost(30),
        name="fall",
    )(sc, first, act, slope, cotangent, small, wu, d0, d1)


def place(acc_ref, keep_ref, send_ref, me, rows):
    for ref, sibling in ((keep_ref, False), (send_ref, True)):
        for position in range(CHIPS):
            unit = held(me, position, SCATTER, sibling)
            row = pl.multiple_of(unit * rows, 8)
            ref[position] = acc_ref[pl.ds(row, rows), :].astype(ref.dtype)


DOWN_TILE = 384


def down_kernel(sc, act_ref, g_ref, keep_ref, send_ref, acc_ref):
    acc_ref[...] = mm(act_ref[...], g_ref[...], TN)
    place(acc_ref, keep_ref, send_ref, sc[0], FROWS)


def down_call(sc, act, fgrad):
    out = pl.BlockSpec((16, FROWS, DOWN_TILE), lambda i, s: (0, 0, i))
    return pl.pallas_call(
        down_kernel,
        out_shape=(
            jax.ShapeDtypeStruct((16, FROWS, D), F32),
            jax.ShapeDtypeStruct((16, FROWS, D), SEND),
        ),
        grid_spec=pltpu.PrefetchScalarGridSpec(
            num_scalar_prefetch=1,
            grid=(D // DOWN_TILE,),
            in_specs=[
                pl.BlockSpec((LEN, FF), lambda i, s: (0, 0), pipeline_mode=pl.Buffered(1)),
                pl.BlockSpec((LEN, DOWN_TILE), lambda i, s: (0, i)),
            ],
            out_specs=[out, out],
            scratch_shapes=[pltpu.VMEM((FF, DOWN_TILE), F32)],
        ),
        compiler_params=params(56),
        cost_estimate=cost(14),
        name="down_term",
    )(sc, act, fgrad)


TILE = 256
OUT_TILES = D // TILE
UP_TILES = FF // TILE


def up_kernel(sc, ctx0_ref, ctx1_ref, ag_ref, nlow_ref, pg_ref, keep_ref, send_ref, acc_ref):
    tile = pl.program_id(0)

    @pl.when(tile < OUT_TILES)
    def _():
        acc_ref[:HALF, :] = mm(ctx0_ref[...], ag_ref[...], TN)
        acc_ref[HALF:, :] = mm(ctx1_ref[...], ag_ref[...], TN)

    @pl.when(tile >= OUT_TILES)
    def _():
        acc_ref[...] = mm(nlow_ref[...], pg_ref[...], TN)

    place(acc_ref, keep_ref, send_ref, sc[0], ROWS)


def up_call(sc, ctx0, ctx1, agrad, nlow, pgrad):
    out = pl.BlockSpec((16, ROWS, TILE), lambda i, s: (0, 0, i))
    cols = D + FF
    return pl.pallas_call(
        up_kernel,
        out_shape=(
            jax.ShapeDtypeStruct((16, ROWS, cols), F32),
            jax.ShapeDtypeStruct((16, ROWS, cols), SEND),
        ),
        grid_spec=pltpu.PrefetchScalarGridSpec(
            num_scalar_prefetch=1,
            grid=(OUT_TILES + UP_TILES,),
            in_specs=[
                pl.BlockSpec((LEN, HALF), lambda i, s: (0, 0)),
                pl.BlockSpec((LEN, HALF), lambda i, s: (0, 0)),
                pl.BlockSpec((LEN, TILE), lambda i, s: (0, jnp.minimum(i, OUT_TILES - 1))),
                pl.BlockSpec((LEN, D), lambda i, s: (0, 0)),
                pl.BlockSpec((LEN, TILE), lambda i, s: (0, jnp.maximum(i - OUT_TILES, 0))),
            ],
            out_specs=[out, out],
            scratch_shapes=[pltpu.VMEM((D, TILE), F32)],
        ),
        compiler_params=params(48),
        cost_estimate=cost(17),
        name="up_term",
    )(sc, ctx0, ctx1, agrad, nlow, pgrad)


QTILE = 384
QPART = 3 * QTILE


def qterm_kernel(last, sc, x_ref, g_ref, sums_ref, usum_ref, qv_in_ref, *rest):
    if last:
        keep_ref, send_ref, acc_ref, qv_ref = rest
    else:
        keep_ref, send_ref, qv_ref, acc_ref = rest
    tile = pl.program_id(0)

    @pl.when(tile < 3)
    def _():
        x = x_ref[...]
        x = jnp.where(iota(x.shape, 1) < sc[1], x, jnp.zeros_like(x))
        g = g_ref[0]
        acc_ref[...] = mm(x, g, TN)
        column = jnp.sum(g.astype(F32), axis=0, keepdims=True)
        for third in (0, 2):

            @pl.when(tile == third)
            def _():
                qv_ref[third // 2] = column

    if last:

        @pl.when(tile == 3)
        def _():
            high = lax.Precision.HIGHEST
            rows = sums_ref[...]
            pick = iota((8, D), 0)
            for k in range(2):
                row = jnp.concatenate([qv_in_ref[k], qv_ref[k]], axis=1)
                rows = jnp.where(pick == k, row, rows)
            shape = (UNITS, 8, D)
            start = iota(shape, 0) * ROWS
            lane = iota(shape, 2)
            mine = (lane >= start) & (lane < start + ROWS)
            wide = jnp.where(mine, rows[None], 0.0).reshape(UNITS * 8, D)
            small = mm(wide, spread(EXTRA, ROWS, D), NT, high).reshape(UNITS, 8, EXTRA)
            start = iota((UNITS, FF), 0) * FROWS
            lane = iota((UNITS, FF), 1)
            mine = (lane >= start) & (lane < start + FROWS)
            up = mm(jnp.where(mine, usum_ref[...], 0.0), spread(EXTRA, FROWS, FF), NT, high)
            acc_ref[...] = jnp.zeros_like(acc_ref)
            for unit in range(UNITS):
                acc_ref[unit * ROWS : unit * ROWS + 8, 0:EXTRA] = small[unit]
                acc_ref[unit * ROWS + 8 : unit * ROWS + 9, 0:EXTRA] = up[unit : unit + 1]

    place(acc_ref, keep_ref, send_ref, sc[0], ROWS)


def qterm_call(sc, hidden, qkv_grad, sums, usum, qv=None):
    last = qv is not None
    out = pl.BlockSpec((CHIPS, ROWS, QTILE), lambda i, s: (0, 0, i))
    pair = pl.BlockSpec((2, 1, QTILE), lambda i, s: (0, 0, 0))
    shape = jax.ShapeDtypeStruct((2, 1, QTILE), F32)
    if not last:
        qv = jnp.zeros(shape.shape, F32)
    cols = QPART + (QTILE if last else 0)
    return pl.pallas_call(
        functools.partial(qterm_kernel, last),
        out_shape=(
            jax.ShapeDtypeStruct((CHIPS, ROWS, cols), F32),
            jax.ShapeDtypeStruct((CHIPS, ROWS, cols), SEND),
        )
        + (() if last else (shape,)),
        grid_spec=pltpu.PrefetchScalarGridSpec(
            num_scalar_prefetch=1,
            grid=(cols // QTILE,),
            in_specs=[
                pl.BlockSpec((LEN, D), lambda i, s: (0, 0)),
                pl.BlockSpec((1, LEN, QTILE), lambda i, s: (jnp.minimum(i, 2), 0, 0)),
                pl.BlockSpec((8, D), lambda i, s: (0, 0)),
                pl.BlockSpec((1, FF), lambda i, s: (0, 0)),
                pair,
            ],
            out_specs=[out, out] + ([] if last else [pair]),
            scratch_shapes=[pltpu.VMEM((D, QTILE), F32)]
            + ([pltpu.VMEM((2, 1, QTILE), F32)] if last else []),
        ),
        compiler_params=params(48),
        cost_estimate=cost(7),
        name="qkv_term",
    )(sc, hidden, qkv_grad, sums, usum, qv)


BWD_BLOCK = 256


def attend_back_kernel(
    first, sc, q_ref, k_ref, v_ref, do_ref, o_ref, e_ref, inv_ref, g_ref, dk_acc, dv_acc
):
    k = k_ref[...]
    v = v_ref[...]
    lane = iota((LEN, 128), 1)
    keys = [jnp.where((lane // HDIM) == h, k, jnp.zeros_like(k)) for h in range(2)]
    lane_q = iota((BWD_BLOCK, 128), 1)
    on = iota((1, 128), 1) + (first + pl.program_id(0)) * 128 < sc[2]
    for b in range(LEN // BWD_BLOCK):
        rows = slice(b * BWD_BLOCK, (b + 1) * BWD_BLOCK)
        q = q_ref[rows, :]
        do = (do_ref[rows, :].astype(F32) * inv_ref[rows, :]).astype(BF)
        both = do.astype(F32) * o_ref[rows, :].astype(F32)
        dq = None
        for h in range(2):
            mine = (lane_q // HDIM) == h
            doh = jnp.where(mine, do, jnp.zeros_like(do))
            qh = jnp.where(mine, q, jnp.zeros_like(q))
            delta = jnp.sum(jnp.where(mine, both, 0.0), axis=1, keepdims=True)
            dp = mm(doh, v, NT)
            e = e_ref[h, rows, :]
            ds = (e.astype(F32) * (dp - delta)).astype(BF)
            part = mm(ds, keys[h], NN)
            dq = part if dq is None else dq + part
            dk = mm(ds, qh, TN)
            dv = mm(e, doh, TN)
            if b == 0 and h == 0:
                dk_acc[...] = dk
                dv_acc[...] = dv
            else:
                dk_acc[...] += dk
                dv_acc[...] += dv
        g_ref[0, rows, :] = jnp.where(on, dq * HDIM ** (-0.5), 0.0).astype(BF)
    g_ref[1] = jnp.where(on, dk_acc[...], 0.0).astype(BF)
    g_ref[2] = jnp.where(on, dv_acc[...], 0.0).astype(BF)


def attend_back_call(sc, qkv, cgrad, ctx, e, inv, first, pairs):
    def spec(offset):
        return pl.BlockSpec((LEN, 128), lambda i, s: (0, offset + first + i))

    own = pl.BlockSpec((LEN, 128), lambda i, s: (0, i))
    return pl.pallas_call(
        functools.partial(attend_back_kernel, first),
        out_shape=jax.ShapeDtypeStruct((3, LEN, pairs * 128), BF),
        grid_spec=pltpu.PrefetchScalarGridSpec(
            num_scalar_prefetch=1,
            grid=(pairs,),
            in_specs=[
                spec(0),
                spec(PAIRS),
                spec(2 * PAIRS),
                spec(0),
                own,
                pl.BlockSpec((2, LEN, LEN), lambda i, s: (i, 0, 0)),
                own,
            ],
            out_specs=pl.BlockSpec((3, LEN, 128), lambda i, s: (0, 0, i)),
            scratch_shapes=[pltpu.VMEM((LEN, 128), F32)] * 2,
        ),
        compiler_params=params(56),
        cost_estimate=cost(6 * pairs),
        name="attend_back",
    )(sc, qkv, qkv, qkv, cgrad, ctx, e, inv)


def input_kernel(sc, g0_ref, g1_ref, w_ref, first_ref, out_ref):
    total = first_ref[...]
    for third in range(3):
        for part, g_ref in enumerate((g0_ref, g1_ref)):
            col = third * ATT + part * HALF
            total = total + mm(g_ref[third], w_ref[:, col : col + HALF], NT)
    on = iota((1, D), 1) < sc[1]
    out_ref[...] = jnp.where(on, 0.1 * total, 0.0).astype(BF)


def input_call(sc, grad0, grad1, weight, first_grad):
    block = 256
    return pl.pallas_call(
        input_kernel,
        out_shape=jax.ShapeDtypeStruct((LEN, D), BF),
        grid_spec=pltpu.PrefetchScalarGridSpec(
            num_scalar_prefetch=1,
            grid=(LEN // block,),
            in_specs=[
                pl.BlockSpec((3, block, HALF), lambda i, s: (0, i, 0)),
                pl.BlockSpec((3, block, HALF), lambda i, s: (0, i, 0)),
                pl.BlockSpec((D, QCOLS), lambda i, s: (0, 0)),
                pl.BlockSpec((block, D), lambda i, s: (i, 0)),
            ],
            out_specs=pl.BlockSpec((block, D), lambda i, s: (i, 0)),
        ),
        compiler_params=params(48),
        cost_estimate=cost(9),
        name="input_grad",
    )(sc, grad0, grad1, weight, first_grad)


def make_local(groups, members):
    fine = groups * members == UNITS
    axes = ("grp", "dp") if fine else ("grp",)

    def swap(x, even, odd=None):
        pair = (even, even if odd is None else odd)
        return lax.ppermute(x, axes, [(i, i ^ pair[i & 1]) for i in range(UNITS)])

    class Gather:
        hops = tuple(zip(*GATHER)) + ((CORE, CORE),)

        def __init__(self, x):
            self.state, self.stage = [x[None]], 0

        def start(self):
            self.recv = swap(self.state[0], *self.hops[self.stage])
            self.stage += 1

        def finish(self, *beside):
            if beside:
                self.recv = after(self.recv, *beside)[0]
            if self.stage == 5:
                return self.state[0], self.recv
            self.state = [jnp.concatenate([self.state[0], self.recv], axis=0)]

    stages = ((CORE, CORE),) + tuple(zip(*SCATTER))[::-1]

    class Scatter:
        def __init__(self, keep, send):
            self.state, self.stage = [keep, send], 0

        def start(self):
            self.recv = swap(self.state[1], *stages[self.stage])
            self.stage += 1

        def finish(self, *beside):
            if beside:
                self.recv = after(self.recv, *beside)[0]
            x = self.state[0] + self.recv.astype(F32)
            if self.stage == 5:
                return x[0]
            n = x.shape[0] // 2
            self.state = [x[:n], x[n:].astype(SEND)]

    def tie(x, *movers):
        x, *flat = after(x, *(a for m in movers for a in m.state))
        for m in movers:
            m.state, flat = flat[: len(m.state)], flat[len(m.state) :]
        return x

    def local(
        hidden,
        lengths,
        subnet,
        qkv_weight,
        qv_bias,
        out_weight,
        up_weight,
        up_bias,
        down_weight,
        norm_gains,
        bias_rows,
        cotangent,
    ):
        group = lax.axis_index("grp")
        me = group * members + lax.axis_index("dp") if fine else group
        if not fine:
            qkv_weight, out_weight, up_weight, up_bias, down_weight = (
                lax.all_gather(w, "dp", axis=0, tiled=True)
                for w in (qkv_weight, out_weight, up_weight, up_bias, down_weight)
            )
            qv_bias, norm_gains, bias_rows = (
                lax.all_gather(w, "dp", axis=1, tiled=True)
                for w in (qv_bias, norm_gains, bias_rows)
            )
        picks = lax.dynamic_index_in_dim(subnet, group, 0, keepdims=False)
        width = D - (2 - picks[0]) * (D // 6)
        heads = HEADS - (2 - picks[1]) * (HEADS // 6)
        inner = width * (6 + picks[2]) // 2
        sc = jnp.stack([me.astype(jnp.int32), width, heads * HDIM, inner, lengths[0]])

        rows = jnp.concatenate([qv_bias, norm_gains, bias_rows], axis=0)
        extra = jnp.concatenate(
            [
                jnp.pad(rows, ((0, 0), (0, EXTRA - ROWS))),
                jnp.pad(up_bias[None], ((0, ROWS - 9), (0, EXTRA - FROWS))),
            ],
            axis=0,
        )
        zero = jnp.zeros((ROWS, EXTRA), BF)
        shard = jnp.concatenate([qkv_weight, extra, zero, out_weight, up_weight], axis=1)
        recv = swap(shard, CORE)
        side = me & 1
        pair = jnp.concatenate(
            [jnp.where(side == 0, shard, recv), jnp.where(side == 0, recv, shard)], axis=0
        )
        q = lax.dynamic_slice_in_dim(pair[:, :QCOLS], side * (QCOLS // 2), QCOLS // 2, 1)
        u = lax.dynamic_slice_in_dim(pair[:, QCOLS:], side * (UCOLS // 2), UCOLS // 2, 1)
        half = PAIRS // 2
        q = Gather(q)
        for _ in range(2):
            q.start()
            q.finish()
        u = Gather(tie(u, q))
        q.start()
        u.start()
        q.finish()
        u.finish()
        u.state = [tie(u.state[0], q)]
        q.start()
        u.start()
        q.finish()
        u.finish()
        u.state = [tie(u.state[0], q)]
        q.start()
        u.start()
        d = Gather(tie(down_weight, u))
        d.start()
        qkv, qkv_full, small, upb = qkv_call(sc, hidden, *q.finish())
        u.finish(small)
        d.finish(small)
        qkv = tie(qkv, u, d)
        u.start()
        d.start()
        ctx0, e0, inv0 = attend_call(sc, qkv, 0, half)
        u.finish(inv0)
        d.finish(inv0)
        qkv = tie(qkv, u, d)
        u.start()
        d.start()
        ctx1, e1, inv1 = attend_call(sc, qkv, half, half)
        d.finish(inv1)
        ctx1 = tie(ctx1, d)
        d.start()
        first, nlow, act, slope, wu = rise_call(
            sc, ctx0, ctx1, hidden, small, upb, *u.finish(inv1)
        )
        d.finish(first)
        d.start()
        output, fgrad, pgrad, agrad, first_grad, cgrad, sums, usum = fall_call(
            sc, first, act, slope, cotangent, small, wu, *d.finish()
        )

        dn = Scatter(*down_call(sc, act, fgrad))
        pgrad = tie(pgrad, dn)
        dn.start()
        up = Scatter(*up_call(sc, ctx0, ctx1, agrad, nlow, pgrad))
        dn.finish()
        cgrad = tie(cgrad, dn, up)
        dn.start()
        up.start()
        grad0 = attend_back_call(sc, qkv, cgrad, ctx0, e0, inv0, 0, half)
        dn.finish()
        up.finish()
        grad0 = tie(grad0, dn, up)
        dn.start()
        up.start()
        qk, qs, qv = qterm_call(sc, hidden, grad0, sums, usum)
        qa = Scatter(qk, qs)
        dn.finish()
        cgrad = tie(cgrad, dn, qa)
        dn.start()
        qa.start()
        grad1 = attend_back_call(sc, qkv, cgrad, ctx1, e1, inv1, half, half)
        up.finish()
        dn.finish()
        qa.finish()
        grad1 = tie(grad1, up, dn, qa)
        up.start()
        dn.start()
        qa.start()
        qb = Scatter(*qterm_call(sc, hidden, grad1, sums, usum, qv))
        up.finish()
        down = dn.finish()
        first_grad = tie(first_grad, up, qb)
        qb.start()
        up.start()
        grad_hidden = input_call(sc, grad0, grad1, qkv_full, first_grad)
        qa.finish()
        qb.finish()
        up.finish()
        for sc_ in (qb, qa, up):
            sc_.start()
        qa.finish()
        qb.finish()
        up = up.finish()
        for sc_ in (qb, qa):
            sc_.start()
        qa.finish()
        qb.finish()
        for sc_ in (qb, qa):
            sc_.start()
        qa = qa.finish()
        qb.finish()
        qb.start()
        qb = qb.finish()

        ex = qb[:, QPART:]
        qkv_sum = jnp.concatenate(
            [x[:, t * QTILE : (t + 1) * QTILE] for t in range(3) for x in (qa, qb)], axis=1
        )
        grads = (
            qkv_sum,
            ex[0:2, :ROWS],
            up[:, :D],
            up[:, D:],
            ex[8, :FROWS],
            down,
            ex[2:4, :ROWS],
            ex[4:8, :ROWS],
        )
        if not fine:
            dims = (0, 1, 0, 0, 0, 0, 1, 1)
            grads = tuple(
                lax.psum_scatter(g, "dp", scatter_dimension=d, tiled=True)
                for g, d in zip(grads, dims)
            )
        return (output, grad_hidden) + grads

    return local


def solution(mesh):
    both = ("grp", "dp")
    row, col, flat = P(both, None), P(None, both), P(both)
    placed = (row, flat, P(), row, col, row, row, flat, row, col, col, row)
    return jax.shard_map(
        make_local(mesh.shape["grp"], mesh.shape["dp"]),
        mesh=mesh,
        in_specs=placed,
        out_specs=(row, row, row, col, row, row, flat, row, col, col),
        check_vma=False,
    )
```

```python
import functools

import jax
import jax.numpy as jnp
from jax import lax
from jax.experimental import pallas as pl
from jax.experimental.pallas import tpu as pltpu
from jax.sharding import PartitionSpec as P

D = 768
HEADS = 12
HDIM = 64
FF = 3072
LEN = 1024
ATT = 768
PAIRS = HEADS // 2

EPSILON = 1e-05
NEGATIVE = -1e30

UNITS = 32
ROWS = D // UNITS
FROWS = FF // UNITS
PAIR = 2 * ROWS
CHIPS = UNITS // 2
EXTRA = 128
QCOLS = 3 * ATT + 2 * EXTRA
UCOLS = D + FF

BF = jnp.bfloat16
F32 = jnp.float32
SEND = jnp.bfloat16

NN = (((1,), (0,)), ((), ()))
NT = (((1,), (1,)), ((), ()))
TN = (((0,), (0,)), ((), ()))

CORE, AX, AY, Z1, Z2 = 1, 2, 4, 8, 16


def mm(a, b, dims, precision=None):
    return lax.dot_general(a, b, dims, precision=precision, preferred_element_type=F32)


def params(megabytes):
    return pltpu.CompilerParams(vmem_limit_bytes=megabytes << 20)


def cost(micros):
    return pl.CostEstimate(
        flops=int(micros * 1.1e9), transcendentals=0, bytes_accessed=int(micros * 1e6)
    )


def owner(position, masks):
    offset = 0
    for bit, mask in enumerate(masks):
        if (position >> bit) & 1:
            offset ^= mask
    return offset


GATHER = ((Z2, Z1, AX, AY), (Z2, Z1, AY, AX))
SCATTER = ((Z2, Z1, AY, AX), (Z2, Z1, AX, AY))


def held(me, position, orders, sibling=False):
    even, odd = owner(position, orders[0]), owner(position, orders[1])
    parity = me & 1
    if sibling:
        me, parity = me ^ CORE, 1 - parity
    return me ^ jnp.where(parity == 0, even, odd)


def after(x, *others):
    return lax.optimization_barrier((x,) + others)


def iota(shape, axis):
    return lax.broadcasted_iota(jnp.int32, shape, axis)


def spread(width, period, columns):
    col = iota((width, columns), 1)
    turn = jnp.floor((col.astype(F32) + 0.5) * (1.0 / period)).astype(jnp.int32)
    return jnp.where(col - turn * period == iota((width, columns), 0), 1.0, 0.0)


QKV_BLOCK = 256


def qkv_kernel(sc, x_ref, own, other, qkv_ref, w_ref, small_ref, upb_ref, sem):
    me, width, att = sc[0], sc[1], sc[2]

    @pl.when(pl.program_id(0) == 0)
    def _():
        copies = []
        half = QCOLS // 2
        for source, sibling in ((own, False), (other, True)):
            side = (me & 1) ^ 1 if sibling else me & 1
            col = pl.multiple_of(side * half, 128)
            for position in range(CHIPS):
                chip = held(me, position, GATHER, sibling) >> 1
                row = pl.multiple_of(chip * PAIR, 16)
                copies.append(
                    pltpu.make_async_copy(
                        source.at[position],
                        w_ref.at[pl.ds(row, PAIR), pl.ds(col, half)],
                        sem.at[len(copies)],
                    )
                )
                copies[-1].start()
        for copy in copies:
            copy.wait()
        extra = w_ref[:, 3 * ATT : 3 * ATT + EXTRA]
        wide = mm(extra, spread(EXTRA, ROWS, D).astype(BF), NN).reshape(UNITS, ROWS, D)
        shape = (UNITS, ROWS, D)
        start = iota(shape, 0) * ROWS
        lane = iota(shape, 2)
        mine = (lane >= start) & (lane < start + ROWS)
        small_ref[...] = jnp.sum(jnp.where(mine, wide, 0.0), axis=0)
        row8 = extra.reshape(UNITS, ROWS, EXTRA)[:, 8, :]
        wide = mm(row8, spread(EXTRA, FROWS, FF).astype(BF), NN)
        start = iota((UNITS, FF), 0) * FROWS
        lane = iota((UNITS, FF), 1)
        mine = (lane >= start) & (lane < start + FROWS)
        upb_ref[...] = jnp.sum(jnp.where(mine, wide, 0.0), axis=0, keepdims=True)

    x = x_ref[...]
    x = jnp.where(iota(x.shape, 1) < width, x, jnp.zeros_like(x))
    on = iota((1, ATT), 1) < att
    for third in range(3):
        part = mm(x, w_ref[:, third * ATT : (third + 1) * ATT], NN)
        if third == 0:
            part = part + small_ref[0:1, :]
        if third == 2:
            part = part + small_ref[1:2, :]
        part = jnp.where(on, part, 0.0).astype(BF)
        if third == 0:
            part = part * jnp.asarray(HDIM ** (-0.5), BF)
        qkv_ref[:, third * ATT : (third + 1) * ATT] = part


def qkv_call(sc, hidden, own, other):
    hbm = pl.BlockSpec(memory_space=pl.ANY)
    return pl.pallas_call(
        qkv_kernel,
        out_shape=(
            jax.ShapeDtypeStruct((LEN, 3 * ATT), BF),
            jax.ShapeDtypeStruct((D, QCOLS), BF),
            jax.ShapeDtypeStruct((ROWS, D), F32),
            jax.ShapeDtypeStruct((1, FF), F32),
        ),
        grid_spec=pltpu.PrefetchScalarGridSpec(
            num_scalar_prefetch=1,
            grid=(LEN // QKV_BLOCK,),
            in_specs=[pl.BlockSpec((QKV_BLOCK, D), lambda i, s: (i, 0)), hbm, hbm],
            out_specs=[
                pl.BlockSpec((QKV_BLOCK, 3 * ATT), lambda i, s: (i, 0)),
                pl.BlockSpec((D, QCOLS), lambda i, s: (0, 0)),
                pl.BlockSpec((ROWS, D), lambda i, s: (0, 0)),
                pl.BlockSpec((1, FF), lambda i, s: (0, 0)),
            ],
            scratch_shapes=[pltpu.SemaphoreType.DMA((UNITS,))],
        ),
        compiler_params=params(48),
        cost_estimate=cost(10),
        name="qkv",
    )(sc, hidden, own, other)


FWD_BLOCK = 512


def attend_kernel(sc, q_ref, k_ref, v_ref, o_ref, e_ref, inv_ref):
    length = sc[4]
    half = LEN // 2
    lane = iota((LEN, 128), 1)
    edge = jnp.where(iota((1, half), 1) + half < length, 0.0, NEGATIVE)
    k = k_ref[...]
    v = v_ref[...]
    heads = []
    for h in range(2):
        mine = (lane // HDIM) == h
        heads.append(
            (jnp.where(mine, k, jnp.zeros_like(k)), jnp.where(mine, v, jnp.ones_like(v)))
        )
    left = iota((FWD_BLOCK, 128), 1) < HDIM
    for b in range(LEN // FWD_BLOCK):
        rows = slice(b * FWD_BLOCK, (b + 1) * FWD_BLOCK)
        q = q_ref[rows, :]
        outs, invs = [], []
        for h in range(2):
            keys, values = heads[h]
            scores = mm(q, keys, NT)
            sa = scores[:, :half]
            sb = scores[:, half:] + edge
            top = jnp.maximum(
                jnp.max(sa, axis=1, keepdims=True), jnp.max(sb, axis=1, keepdims=True)
            )
            ea = jnp.exp(sa - top).astype(BF)
            eb = jnp.exp(sb - top).astype(BF)
            e_ref[h, rows, :half] = ea
            e_ref[h, rows, half:] = eb
            o = mm(ea, values[:half], NN) + mm(eb, values[half:], NN)
            inv = 1.0 / pltpu.roll(o, HDIM, 1)
            outs.append(o * inv)
            invs.append(inv)
        o_ref[rows, :] = jnp.where(left, outs[0], outs[1]).astype(BF)
        inv_ref[rows, :] = jnp.where(left, invs[0], invs[1])


def attend_call(sc, qkv, first, pairs):
    def spec(offset):
        return pl.BlockSpec((LEN, 128), lambda i, s: (0, offset + first + i))

    out = pl.BlockSpec((LEN, 128), lambda i, s: (0, i))

    return pl.pallas_call(
        attend_kernel,
        out_shape=(
            jax.ShapeDtypeStruct((LEN, pairs * 128), BF),
            jax.ShapeDtypeStruct((2 * pairs, LEN, LEN), BF),
            jax.ShapeDtypeStruct((LEN, pairs * 128), F32),
        ),
        grid_spec=pltpu.PrefetchScalarGridSpec(
            num_scalar_prefetch=1,
            grid=(pairs,),
            in_specs=[spec(0), spec(PAIRS), spec(2 * PAIRS)],
            out_specs=[out, pl.BlockSpec((2, LEN, LEN), lambda i, s: (i, 0, 0)), out],
        ),
        compiler_params=params(56),
        cost_estimate=cost(4 * pairs),
        name="attend",
    )(sc, qkv, qkv, qkv)


CHAIN_BLOCK = 256
HALF = ATT // 2
CHUNK = 768


def normal_parts(x):
    t = 1.0 / (1.0 + 0.23164189 * jnp.abs(x))
    gauss = jnp.exp2((x * x) * -0.7213475204444817)
    poly = t * (
        0.127414796
        + t * (-0.142248368 + t * (0.7107068705 + t * (-0.7265760135 + t * 0.5307027145)))
    )
    tail = poly * gauss
    return jnp.where(x >= 0, 1.0 - tail, tail), gauss * 0.3989422804014327


def normalise(v, cm, count):
    mean = jnp.sum(v, axis=1, keepdims=True) / count
    centred = (v - mean) * cm
    var = jnp.sum(centred * centred, axis=1, keepdims=True) / count
    r = lax.rsqrt(var + EPSILON)
    return centred * r, r


def normalise_back(e, yhat, r, gain, cm, count):
    t = e * gain * cm
    s1 = jnp.sum(t, axis=1, keepdims=True) / count
    s2 = jnp.sum(t * yhat, axis=1, keepdims=True) / count
    return r * cm * (t - s1 - yhat * s2)


def width_mask(width):
    return jnp.where(iota((1, D), 1) < width, 1.0, 0.0)


def column_sum(x):
    return jnp.sum(x.astype(F32), axis=0, keepdims=True)


def up_copies(me, own, other, w_ref, sem):
    copies = []
    half = UCOLS // 2
    for source, sibling in ((own, False), (other, True)):
        side = (me & 1) ^ 1 if sibling else me & 1
        col = pl.multiple_of(side * half, 128)
        for position in range(CHIPS):
            chip = held(me, position, GATHER, sibling) >> 1
            row = pl.multiple_of(chip * PAIR, 16)
            copies.append(
                pltpu.make_async_copy(
                    source.at[position],
                    w_ref.at[pl.ds(row, PAIR), pl.ds(col, half)],
                    sem.at[len(copies)],
                )
            )
    return copies


def down_copies(me, own, other, w_ref, sem):
    copies = []
    for source, sibling in ((own, False), (other, True)):
        for position in range(CHIPS):
            unit = held(me, position, GATHER, sibling)
            row = pl.multiple_of(unit * FROWS, 16)
            copies.append(
                pltpu.make_async_copy(
                    source.at[position],
                    w_ref.at[pl.ds(row, FROWS), :],
                    sem.at[len(copies)],
                )
            )
    return copies


def rise_kernel(
    sc,
    ctx0_ref,
    ctx1_ref,
    hid_ref,
    small_ref,
    upb_ref,
    u0,
    u1,
    first_ref,
    nlow_ref,
    act_ref,
    slope_ref,
    wu_ref,
    sem,
):
    me, width, inner = sc[0], sc[1], sc[3]

    @pl.when(pl.program_id(0) == 0)
    def _():
        copies = up_copies(me, u0, u1, wu_ref, sem)
        for copy in copies:
            copy.start()
        for copy in copies:
            copy.wait()

    cm = width_mask(width)
    gain1, bias0, shift1 = small_ref[2:3, :], small_ref[4:5, :], small_ref[5:6, :]
    x = hid_ref[...].astype(F32) * cm
    projected = mm(ctx0_ref[...], wu_ref[:HALF, :D], NN) + mm(
        ctx1_ref[...], wu_ref[HALF:, :D], NN
    )
    first = x + (projected + bias0) * cm
    first_ref[...] = first
    yhat, _ = normalise(first, cm, width.astype(F32))
    nlow = ((yhat * gain1 + shift1) * cm).astype(BF)
    nlow_ref[...] = nlow
    for j in range(FF // CHUNK):
        cols = slice(j * CHUNK, (j + 1) * CHUNK)
        up_cols = slice(D + j * CHUNK, D + (j + 1) * CHUNK)
        fm = jnp.where(iota((1, CHUNK), 1) + j * CHUNK < inner, 1.0, 0.0)
        pre = (mm(nlow, wu_ref[:, up_cols], NN) + upb_ref[:, cols]) * fm
        cdf, pdf = normal_parts(pre)
        act_ref[:, cols] = (pre * cdf).astype(BF)
        slope_ref[:, cols] = ((cdf + pre * pdf) * fm).astype(BF)


def row_spec(cols):
    return pl.BlockSpec((CHAIN_BLOCK, cols), lambda i, s: (i, 0))


def whole_spec(*shape):
    return pl.BlockSpec(shape, lambda i, s: (0,) * len(shape))


def row_shape(cols, dtype=BF):
    return jax.ShapeDtypeStruct((LEN, cols), dtype)


def rise_call(sc, ctx0, ctx1, hidden, small, upb, u0, u1):
    hbm = pl.BlockSpec(memory_space=pl.ANY)
    return pl.pallas_call(
        rise_kernel,
        out_shape=(
            row_shape(D, F32),
            row_shape(D),
            row_shape(FF),
            row_shape(FF),
        ),
        grid_spec=pltpu.PrefetchScalarGridSpec(
            num_scalar_prefetch=1,
            grid=(LEN // CHAIN_BLOCK,),
            in_specs=[row_spec(HALF)] * 2
            + [row_spec(D), whole_spec(ROWS, D), whole_spec(1, FF), hbm, hbm],
            out_specs=[
                row_spec(D),
                row_spec(D),
                row_spec(FF),
                row_spec(FF),
            ],
            scratch_shapes=[pltpu.VMEM((D, UCOLS), BF), pltpu.SemaphoreType.DMA((UNITS,))],
        ),
        compiler_params=params(56),
        cost_estimate=cost(18),
        name="rise",
    )(sc, ctx0, ctx1, hidden, small, upb, u0, u1)


def fall_kernel(
    sc,
    first_ref,
    act_ref,
    slope_ref,
    cot_ref,
    small_ref,
    u0,
    u1,
    d0,
    d1,
    out_ref,
    fgrad_ref,
    pgrad_ref,
    agrad_ref,
    igrad_ref,
    cgrad_ref,
    sums_ref,
    usum_ref,
    wu_ref,
    wd_ref,
    usem,
    dsem,
):
    me, width, length = sc[0], sc[1], sc[4]
    step = pl.program_id(0)

    @pl.when(step == 0)
    def _():
        down = down_copies(me, d0, d1, wd_ref, dsem)
        for copy in down + up_copies(me, u0, u1, wu_ref, usem):
            copy.start()
        sums_ref[...] = jnp.zeros_like(sums_ref)
        usum_ref[...] = jnp.zeros_like(usum_ref)
        for copy in down:
            copy.wait()

    cm = width_mask(width)
    count = width.astype(F32)
    rowpos = step * CHAIN_BLOCK + iota((CHAIN_BLOCK, 1), 0)
    rm = jnp.where(rowpos < length, 1.0, 0.0)
    gain1, gain2 = small_ref[2:3, :], small_ref[3:4, :]
    shift1, bias2, shift3 = small_ref[5:6, :], small_ref[6:7, :], small_ref[7:8, :]

    yhat1, r1 = normalise(first_ref[...], cm, count)
    normed1 = (yhat1 * gain1 + shift1) * cm
    second = normed1 + (mm(act_ref[...], wd_ref[...], NN) + bias2) * cm
    yhat2, r2 = normalise(second, cm, count)
    out_ref[...] = ((yhat2 * gain2 + shift3) * cm * rm).astype(BF)
    e2 = cot_ref[...].astype(F32) * rm
    sums_ref[3:4, :] += column_sum(e2 * yhat2)
    sums_ref[7:8, :] += column_sum(e2 * cm)
    second_grad = normalise_back(e2, yhat2, r2, gain2, cm, count)
    fgrad = second_grad.astype(BF)
    fgrad_ref[...] = fgrad
    sums_ref[6:7, :] += column_sum(fgrad)
    @pl.when(step == 0)
    def _():
        for copy in up_copies(me, u0, u1, wu_ref, usem):
            copy.wait()

    total = second_grad
    for j in range(FF // CHUNK):
        cols = slice(j * CHUNK, (j + 1) * CHUNK)
        up_cols = slice(D + j * CHUNK, D + (j + 1) * CHUNK)
        pgrad = (mm(fgrad, wd_ref[cols, :], NT) * slope_ref[:, cols].astype(F32)).astype(BF)
        pgrad_ref[:, cols] = pgrad
        usum_ref[:, cols] += column_sum(pgrad)
        total = total + mm(pgrad, wu_ref[:, up_cols], NT)
    sums_ref[2:3, :] += column_sum(total * yhat1)
    sums_ref[5:6, :] += column_sum(total * cm)
    first_grad = normalise_back(total, yhat1, r1, gain1, cm, count)
    igrad_ref[...] = first_grad
    agrad = first_grad.astype(BF)
    agrad_ref[...] = agrad
    sums_ref[4:5, :] += column_sum(agrad)
    cgrad_ref[...] = mm(agrad, wu_ref[:, :D], NT).astype(BF)


def fall_call(sc, first, act, slope, cotangent, small, u0, u1, d0, d1):
    hbm = pl.BlockSpec(memory_space=pl.ANY)
    return pl.pallas_call(
        fall_kernel,
        out_shape=(
            row_shape(D),
            row_shape(D),
            row_shape(FF),
            row_shape(D),
            row_shape(D, F32),
            row_shape(ATT),
            jax.ShapeDtypeStruct((8, D), F32),
            jax.ShapeDtypeStruct((1, FF), F32),
        ),
        grid_spec=pltpu.PrefetchScalarGridSpec(
            num_scalar_prefetch=1,
            grid=(LEN // CHAIN_BLOCK,),
            in_specs=[
                row_spec(D),
                row_spec(FF),
                row_spec(FF),
                row_spec(D),
                whole_spec(ROWS, D),
                hbm,
                hbm,
                hbm,
                hbm,
            ],
            out_specs=[
                row_spec(D),
                row_spec(D),
                row_spec(FF),
                row_spec(D),
                row_spec(D),
                row_spec(ATT),
                whole_spec(8, D),
                whole_spec(1, FF),
            ],
            scratch_shapes=[
                pltpu.VMEM((D, UCOLS), BF),
                pltpu.VMEM((FF, D), BF),
                pltpu.SemaphoreType.DMA((UNITS,)),
                pltpu.SemaphoreType.DMA((UNITS,)),
            ],
        ),
        compiler_params=params(58),
        cost_estimate=cost(30),
        name="fall",
    )(sc, first, act, slope, cotangent, small, u0, u1, d0, d1)


def place(acc_ref, keep_ref, send_ref, me, rows):
    for ref, sibling in ((keep_ref, False), (send_ref, True)):
        for position in range(CHIPS):
            unit = held(me, position, SCATTER, sibling)
            row = pl.multiple_of(unit * rows, 8)
            ref[position] = acc_ref[pl.ds(row, rows), :].astype(ref.dtype)


PLANE = 8
DOWN_ROWS = FF // 4


def down_kernel(sc, act_ref, g_ref, keep_ref, send_ref, acc_ref):
    acc_ref[...] = mm(act_ref[...], g_ref[...], TN)
    for ref, sibling in ((keep_ref, False), (send_ref, True)):
        for high in range(4):
            unit = held(sc[0], high * 4, SCATTER, sibling) & (PLANE - 1)
            row = pl.multiple_of(unit * FROWS, 8)
            ref[high, 0] = acc_ref[pl.ds(row, FROWS), :].astype(ref.dtype)


def down_call(sc, act, fgrad):
    def where(i, s):
        z = i ^ (s[0] // PLANE)
        return (0, (z & 1) * 2 + (z >> 1), 0, 0)

    out = pl.BlockSpec((4, 1, FROWS, D), where)
    keep, send = pl.pallas_call(
        down_kernel,
        out_shape=(
            jax.ShapeDtypeStruct((4, 4, FROWS, D), F32),
            jax.ShapeDtypeStruct((4, 4, FROWS, D), SEND),
        ),
        grid_spec=pltpu.PrefetchScalarGridSpec(
            num_scalar_prefetch=1,
            grid=(4,),
            in_specs=[
                pl.BlockSpec((LEN, DOWN_ROWS), lambda i, s: (0, i)),
                pl.BlockSpec((LEN, D), lambda i, s: (0, 0)),
            ],
            out_specs=[out, out],
            scratch_shapes=[pltpu.VMEM((DOWN_ROWS, D), F32)],
        ),
        compiler_params=params(56),
        cost_estimate=cost(14),
        name="down_term",
    )(sc, act, fgrad)
    return keep.reshape(CHIPS, FROWS, D), send.reshape(CHIPS, FROWS, D)


TILE = 768
OUT_TILES = D // TILE
UP_TILES = FF // TILE


def up_kernel(sc, ctx0_ref, ctx1_ref, ag_ref, nlow_ref, pg_ref, keep_ref, send_ref, acc_ref):
    tile = pl.program_id(0)

    @pl.when(tile < OUT_TILES)
    def _():
        acc_ref[:HALF, :] = mm(ctx0_ref[...], ag_ref[...], TN)
        acc_ref[HALF:, :] = mm(ctx1_ref[...], ag_ref[...], TN)

    @pl.when(tile >= OUT_TILES)
    def _():
        acc_ref[...] = mm(nlow_ref[...], pg_ref[...], TN)

    place(acc_ref, keep_ref, send_ref, sc[0], ROWS)


def up_call(sc, ctx0, ctx1, agrad, nlow, pgrad):
    out = pl.BlockSpec((16, ROWS, TILE), lambda i, s: (0, 0, i))
    cols = D + FF
    return pl.pallas_call(
        up_kernel,
        out_shape=(
            jax.ShapeDtypeStruct((16, ROWS, cols), F32),
            jax.ShapeDtypeStruct((16, ROWS, cols), SEND),
        ),
        grid_spec=pltpu.PrefetchScalarGridSpec(
            num_scalar_prefetch=1,
            grid=(OUT_TILES + UP_TILES,),
            in_specs=[
                pl.BlockSpec((LEN, HALF), lambda i, s: (0, 0)),
                pl.BlockSpec((LEN, HALF), lambda i, s: (0, 0)),
                pl.BlockSpec((LEN, TILE), lambda i, s: (0, jnp.minimum(i, OUT_TILES - 1))),
                pl.BlockSpec((LEN, D), lambda i, s: (0, 0)),
                pl.BlockSpec((LEN, TILE), lambda i, s: (0, jnp.maximum(i - OUT_TILES, 0))),
            ],
            out_specs=[out, out],
            scratch_shapes=[pltpu.VMEM((D, TILE), F32)],
        ),
        compiler_params=params(48),
        cost_estimate=cost(17),
        name="up_term",
    )(sc, ctx0, ctx1, agrad, nlow, pgrad)


QTILE = 384
QPART = 3 * QTILE


def qterm_kernel(last, sc, x_ref, g_ref, sums_ref, usum_ref, qv_in_ref, *rest):
    if last:
        keep_ref, send_ref, acc_ref, qv_ref = rest
    else:
        keep_ref, send_ref, qv_ref, acc_ref = rest
    tile = pl.program_id(0)

    @pl.when(tile < 3)
    def _():
        x = x_ref[...]
        x = jnp.where(iota(x.shape, 1) < sc[1], x, jnp.zeros_like(x))
        g = g_ref[0]
        acc_ref[...] = mm(x, g, TN)
        column = jnp.sum(g.astype(F32), axis=0, keepdims=True)
        for third in (0, 2):

            @pl.when(tile == third)
            def _():
                qv_ref[third // 2] = column

    if last:

        @pl.when(tile == 3)
        def _():
            high = lax.Precision.HIGHEST
            rows = sums_ref[...]
            pick = iota((8, D), 0)
            for k in range(2):
                row = jnp.concatenate([qv_in_ref[k], qv_ref[k]], axis=1)
                rows = jnp.where(pick == k, row, rows)
            shape = (UNITS, 8, D)
            start = iota(shape, 0) * ROWS
            lane = iota(shape, 2)
            mine = (lane >= start) & (lane < start + ROWS)
            wide = jnp.where(mine, rows[None], 0.0).reshape(UNITS * 8, D)
            small = mm(wide, spread(EXTRA, ROWS, D), NT, high).reshape(UNITS, 8, EXTRA)
            start = iota((UNITS, FF), 0) * FROWS
            lane = iota((UNITS, FF), 1)
            mine = (lane >= start) & (lane < start + FROWS)
            up = mm(jnp.where(mine, usum_ref[...], 0.0), spread(EXTRA, FROWS, FF), NT, high)
            acc_ref[...] = jnp.zeros_like(acc_ref)
            for unit in range(UNITS):
                acc_ref[unit * ROWS : unit * ROWS + 8, 0:EXTRA] = small[unit]
                acc_ref[unit * ROWS + 8 : unit * ROWS + 9, 0:EXTRA] = up[unit : unit + 1]

    place(acc_ref, keep_ref, send_ref, sc[0], ROWS)


def qterm_call(sc, hidden, qkv_grad, sums, usum, qv=None):
    last = qv is not None
    out = pl.BlockSpec((CHIPS, ROWS, QTILE), lambda i, s: (0, 0, i))
    pair = pl.BlockSpec((2, 1, QTILE), lambda i, s: (0, 0, 0))
    shape = jax.ShapeDtypeStruct((2, 1, QTILE), F32)
    if not last:
        qv = jnp.zeros(shape.shape, F32)
    cols = QPART + (QTILE if last else 0)
    return pl.pallas_call(
        functools.partial(qterm_kernel, last),
        out_shape=(
            jax.ShapeDtypeStruct((CHIPS, ROWS, cols), F32),
            jax.ShapeDtypeStruct((CHIPS, ROWS, cols), SEND),
        )
        + (() if last else (shape,)),
        grid_spec=pltpu.PrefetchScalarGridSpec(
            num_scalar_prefetch=1,
            grid=(cols // QTILE,),
            in_specs=[
                pl.BlockSpec((LEN, D), lambda i, s: (0, 0)),
                pl.BlockSpec((1, LEN, QTILE), lambda i, s: (jnp.minimum(i, 2), 0, 0)),
                pl.BlockSpec((8, D), lambda i, s: (0, 0)),
                pl.BlockSpec((1, FF), lambda i, s: (0, 0)),
                pair,
            ],
            out_specs=[out, out] + ([] if last else [pair]),
            scratch_shapes=[pltpu.VMEM((D, QTILE), F32)]
            + ([pltpu.VMEM((2, 1, QTILE), F32)] if last else []),
        ),
        compiler_params=params(48),
        cost_estimate=cost(7),
        name="qkv_term",
    )(sc, hidden, qkv_grad, sums, usum, qv)


BWD_BLOCK = 256


def attend_back_kernel(
    first, sc, q_ref, k_ref, v_ref, do_ref, o_ref, e_ref, inv_ref, g_ref, dk_acc, dv_acc
):
    k = k_ref[...]
    v = v_ref[...]
    lane = iota((LEN, 128), 1)
    keys = [jnp.where((lane // HDIM) == h, k, jnp.zeros_like(k)) for h in range(2)]
    lane_q = iota((BWD_BLOCK, 128), 1)
    on = iota((1, 128), 1) + (first + pl.program_id(0)) * 128 < sc[2]
    for b in range(LEN // BWD_BLOCK):
        rows = slice(b * BWD_BLOCK, (b + 1) * BWD_BLOCK)
        q = q_ref[rows, :]
        do = (do_ref[rows, :].astype(F32) * inv_ref[rows, :]).astype(BF)
        both = do.astype(F32) * o_ref[rows, :].astype(F32)
        dq = None
        for h in range(2):
            mine = (lane_q // HDIM) == h
            doh = jnp.where(mine, do, jnp.zeros_like(do))
            qh = jnp.where(mine, q, jnp.zeros_like(q))
            delta = jnp.sum(jnp.where(mine, both, 0.0), axis=1, keepdims=True)
            dp = mm(doh, v, NT)
            e = e_ref[h, rows, :]
            ds = (e.astype(F32) * (dp - delta)).astype(BF)
            part = mm(ds, keys[h], NN)
            dq = part if dq is None else dq + part
            dk = mm(ds, qh, TN)
            dv = mm(e, doh, TN)
            if b == 0 and h == 0:
                dk_acc[...] = dk
                dv_acc[...] = dv
            else:
                dk_acc[...] += dk
                dv_acc[...] += dv
        g_ref[0, rows, :] = jnp.where(on, dq * HDIM ** (-0.5), 0.0).astype(BF)
    g_ref[1] = jnp.where(on, dk_acc[...], 0.0).astype(BF)
    g_ref[2] = jnp.where(on, dv_acc[...], 0.0).astype(BF)


def attend_back_call(sc, qkv, cgrad, ctx, e, inv, first, pairs):
    def spec(offset):
        return pl.BlockSpec((LEN, 128), lambda i, s: (0, offset + first + i))

    own = pl.BlockSpec((LEN, 128), lambda i, s: (0, i))
    return pl.pallas_call(
        functools.partial(attend_back_kernel, first),
        out_shape=jax.ShapeDtypeStruct((3, LEN, pairs * 128), BF),
        grid_spec=pltpu.PrefetchScalarGridSpec(
            num_scalar_prefetch=1,
            grid=(pairs,),
            in_specs=[
                spec(0),
                spec(PAIRS),
                spec(2 * PAIRS),
                spec(0),
                own,
                pl.BlockSpec((2, LEN, LEN), lambda i, s: (i, 0, 0)),
                own,
            ],
            out_specs=pl.BlockSpec((3, LEN, 128), lambda i, s: (0, 0, i)),
            scratch_shapes=[pltpu.VMEM((LEN, 128), F32)] * 2,
        ),
        compiler_params=params(56),
        cost_estimate=cost(6 * pairs),
        name="attend_back",
    )(sc, qkv, qkv, qkv, cgrad, ctx, e, inv)


def input_kernel(sc, *refs):
    *parts, w_ref, first_ref, out_ref = refs
    total = first_ref[...]
    for third in range(3):
        grads = jnp.concatenate([g_ref[third] for g_ref in parts], axis=1)
        total = total + mm(grads, w_ref[:, third * ATT : (third + 1) * ATT], NT)
    on = iota((1, D), 1) < sc[1]
    out_ref[...] = jnp.where(on, 0.1 * total, 0.0).astype(BF)


def input_call(sc, parts, weight, first_grad):
    block = 512
    return pl.pallas_call(
        input_kernel,
        out_shape=jax.ShapeDtypeStruct((LEN, D), BF),
        grid_spec=pltpu.PrefetchScalarGridSpec(
            num_scalar_prefetch=1,
            grid=(LEN // block,),
            in_specs=[
                pl.BlockSpec((3, block, g.shape[2]), lambda i, s: (0, i, 0)) for g in parts
            ]
            + [whole_spec(D, QCOLS), pl.BlockSpec((block, D), lambda i, s: (i, 0))],
            out_specs=pl.BlockSpec((block, D), lambda i, s: (i, 0)),
        ),
        compiler_params=params(48),
        cost_estimate=cost(9),
        name="input_grad",
    )(sc, *parts, weight, first_grad)


def make_local(groups, members):
    fine = groups * members == UNITS
    axes = ("grp", "dp") if fine else ("grp",)

    def swap(x, even, odd=None):
        pair = (even, even if odd is None else odd)
        return lax.ppermute(x, axes, [(i, i ^ pair[i & 1]) for i in range(UNITS)])

    class Gather:
        hops = tuple(zip(*GATHER)) + ((CORE, CORE),)

        def __init__(self, x):
            self.state, self.stage = [x[None]], 0

        def start(self):
            self.recv = swap(self.state[0], *self.hops[self.stage])
            self.stage += 1

        def finish(self, *beside):
            if beside:
                self.recv = after(self.recv, *beside)[0]
            if self.stage == 5:
                return self.state[0], self.recv
            self.state = [jnp.concatenate([self.state[0], self.recv], axis=0)]

    stages = ((CORE, CORE),) + tuple(zip(*SCATTER))[::-1]

    class Scatter:
        def __init__(self, keep, send):
            self.state, self.stage = [keep, send], 0

        def start(self):
            self.recv = swap(self.state[1], *stages[self.stage])
            self.stage += 1

        def finish(self, *beside):
            if beside:
                self.recv = after(self.recv, *beside)[0]
            kept, recv = self.state[0], self.recv
            if self.stage == 5:
                return kept[0] + recv[0].astype(F32)
            n = kept.shape[0] // 2
            send = (kept[n:] + recv[n:].astype(F32)).astype(SEND)
            self.state = [kept[:n] + recv[:n].astype(F32), send]

    def tie(x, *movers):
        x, *flat = after(x, *(a for m in movers for a in m.state))
        for m in movers:
            m.state, flat = flat[: len(m.state)], flat[len(m.state) :]
        return x

    def local(
        hidden,
        lengths,
        subnet,
        qkv_weight,
        qv_bias,
        out_weight,
        up_weight,
        up_bias,
        down_weight,
        norm_gains,
        bias_rows,
        cotangent,
    ):
        group = lax.axis_index("grp")
        me = group * members + lax.axis_index("dp") if fine else group
        if not fine:
            qkv_weight, out_weight, up_weight, up_bias, down_weight = (
                lax.all_gather(w, "dp", axis=0, tiled=True)
                for w in (qkv_weight, out_weight, up_weight, up_bias, down_weight)
            )
            qv_bias, norm_gains, bias_rows = (
                lax.all_gather(w, "dp", axis=1, tiled=True)
                for w in (qv_bias, norm_gains, bias_rows)
            )
        picks = lax.dynamic_index_in_dim(subnet, group, 0, keepdims=False)
        width = D - (2 - picks[0]) * (D // 6)
        heads = HEADS - (2 - picks[1]) * (HEADS // 6)
        inner = width * (6 + picks[2]) // 2
        sc = jnp.stack([me.astype(jnp.int32), width, heads * HDIM, inner, lengths[0]])

        rows = jnp.concatenate([qv_bias, norm_gains, bias_rows], axis=0)
        extra = jnp.concatenate(
            [
                jnp.pad(rows, ((0, 0), (0, EXTRA - ROWS))),
                jnp.pad(up_bias[None], ((0, ROWS - 9), (0, EXTRA - FROWS))),
            ],
            axis=0,
        )
        side = me & 1

        def pair(shard, *beside):
            n = shard.shape[1] // 2
            mine = lax.dynamic_slice_in_dim(shard, side * n, n, 1)
            recv = swap(lax.dynamic_slice_in_dim(shard, (1 - side) * n, n, 1), CORE)
            ordered = [jnp.where(side == 0, mine, recv), jnp.where(side == 0, recv, mine)]
            return jnp.concatenate(ordered, axis=0)

        extra = jnp.pad(extra, ((0, 0), (0, EXTRA)))
        q = pair(jnp.concatenate([qkv_weight, extra], axis=1))
        half = PAIRS // 2
        q = Gather(q)
        q.start()
        q.finish()
        u = pair(jnp.concatenate([tie(out_weight, q), up_weight], axis=1))
        q.start()
        q.finish()
        u = Gather(tie(u, q))
        for _ in range(2):
            q.start()
            u.start()
            q.finish()
            u.finish()
            u.state = [tie(u.state[0], q)]
        q.start()
        u.start()
        d = Gather(tie(down_weight, u))
        d.start()
        qkv, qkv_full, small, upb = qkv_call(sc, hidden, *q.finish())
        u.finish(small)
        d.finish(small)
        qkv = tie(qkv, u, d)
        u.start()
        d.start()
        ctx0, e0, inv0 = attend_call(sc, qkv, 0, half)
        u.finish(inv0)
        d.finish(inv0)
        qkv = tie(qkv, u, d)
        u.start()
        d.start()
        ctx1, e1, inv1 = attend_call(sc, qkv, half, half)
        d.finish(inv1)
        ctx1 = tie(ctx1, d)
        d.start()
        u0, u1 = u.finish(inv1)
        first, nlow, act, slope = rise_call(sc, ctx0, ctx1, hidden, small, upb, u0, u1)
        d.finish(first)
        d.start()
        output, fgrad, pgrad, agrad, first_grad, cgrad, sums, usum = fall_call(
            sc, first, act, slope, cotangent, small, u0, u1, *d.finish()
        )
        def step(beside, *movers):
            for m in movers:
                m.finish(beside)
                m.start()

        dn = Scatter(*down_call(sc, act, fgrad))
        dn.start()
        uk, us = up_call(sc, ctx0, ctx1, agrad, nlow, tie(pgrad, dn))
        up = Scatter(uk, us)
        step(uk, dn)
        up.start()
        cgrad = tie(cgrad, dn, up)
        grad0 = attend_back_call(sc, qkv, cgrad, ctx0, e0, inv0, 0, half)
        step(grad0, dn, up)
        qk, qs, qv = qterm_call(sc, hidden, tie(grad0, dn, up), sums, usum)
        qa = Scatter(qk, qs)
        qa.start()
        step(qv, dn)
        grad1 = attend_back_call(sc, qkv, tie(cgrad, dn, qa), ctx1, e1, inv1, half, half)
        step(grad1, dn, up, qa)
        qk, qs = qterm_call(sc, hidden, tie(grad1, up, dn, qa), sums, usum, qv)
        qb = Scatter(qk, qs)
        qb.start()
        step(qk, qa)
        grad_hidden = input_call(
            sc, (grad0, grad1), qkv_full, tie(first_grad, qb, qa)
        )
        step(grad_hidden, qb, up)
        step(grad_hidden, qa)
        down = dn.finish(grad_hidden)
        step(grad_hidden, qb, up, qa)
        step(grad_hidden, qb)
        up = up.finish()
        qa = qa.finish()
        step(grad_hidden, qb)
        qb = qb.finish()

        ex = qb[:, QPART:]
        qkv_sum = jnp.concatenate(
            [x[:, t * QTILE : (t + 1) * QTILE] for t in range(3) for x in (qa, qb)], axis=1
        )
        grads = (
            qkv_sum,
            ex[0:2, :ROWS],
            up[:, :D],
            up[:, D:],
            ex[8, :FROWS],
            down,
            ex[2:4, :ROWS],
            ex[4:8, :ROWS],
        )
        if not fine:
            dims = (0, 1, 0, 0, 0, 0, 1, 1)
            grads = tuple(
                lax.psum_scatter(g, "dp", scatter_dimension=d, tiled=True)
                for g, d in zip(grads, dims)
            )
        return (output, grad_hidden) + grads

    return local


def solution(mesh):
    both = ("grp", "dp")
    row, col, flat = P(both, None), P(None, both), P(both)
    placed = (row, flat, P(), row, col, row, row, flat, row, col, col, row)
    return jax.shard_map(
        make_local(mesh.shape["grp"], mesh.shape["dp"]),
        mesh=mesh,
        in_specs=placed,
        out_specs=(row, row, row, col, row, row, flat, row, col, col),
        check_vma=False,
    )
```

```python
import functools

import jax
import jax.numpy as jnp
from jax import lax
from jax.experimental import pallas as pl
from jax.experimental.pallas import tpu as pltpu
from jax.sharding import PartitionSpec as P

D = 768
HEADS = 12
HDIM = 64
FF = 3072
LEN = 1024
ATT = 768
PAIRS = HEADS // 2
PARTS = (4, 2)
SPLIT = PARTS[0] * 128

EPSILON = 1e-05
NEGATIVE = -1e30

UNITS = 32
ROWS = D // UNITS
FROWS = FF // UNITS
PAIR = 2 * ROWS
CHIPS = UNITS // 2
EXTRA = 128
QCOLS = 3 * ATT + 2 * EXTRA
UCOLS = D + FF

BF = jnp.bfloat16
F32 = jnp.float32
SEND = jnp.bfloat16

NN = (((1,), (0,)), ((), ()))
NT = (((1,), (1,)), ((), ()))
TN = (((0,), (0,)), ((), ()))

CORE, AX, AY, Z1, Z2 = 1, 2, 4, 8, 16


def mm(a, b, dims, precision=None):
    return lax.dot_general(a, b, dims, precision=precision, preferred_element_type=F32)


def params(megabytes):
    return pltpu.CompilerParams(vmem_limit_bytes=megabytes << 20)


def cost(micros):
    return pl.CostEstimate(
        flops=int(micros * 1.1e9), transcendentals=0, bytes_accessed=int(micros * 1e6)
    )


def owner(position, masks):
    offset = 0
    for bit, mask in enumerate(masks):
        if (position >> bit) & 1:
            offset ^= mask
    return offset


GATHER = ((Z2, Z1, AX, AY), (Z2, Z1, AY, AX))
SCATTER = ((Z2, Z1, AY, AX), (Z2, Z1, AX, AY))


def held(me, position, orders, sibling=False):
    even, odd = owner(position, orders[0]), owner(position, orders[1])
    parity = me & 1
    if sibling:
        me, parity = me ^ CORE, 1 - parity
    return me ^ jnp.where(parity == 0, even, odd)


def after(x, *others):
    return lax.optimization_barrier((x,) + others)


def iota(shape, axis):
    return lax.broadcasted_iota(jnp.int32, shape, axis)


def spread(width, period, columns):
    col = iota((width, columns), 1)
    turn = jnp.floor((col.astype(F32) + 0.5) * (1.0 / period)).astype(jnp.int32)
    return jnp.where(col - turn * period == iota((width, columns), 0), 1.0, 0.0)


QKV_BLOCK = 512


def qkv_copies(me, own, other, w_ref, sem):
    copies = []
    half = QCOLS // 2
    for source, sibling in ((own, False), (other, True)):
        side = (me & 1) ^ 1 if sibling else me & 1
        col = pl.multiple_of(side * half, 128)
        for position in range(CHIPS):
            chip = held(me, position, GATHER, sibling) >> 1
            row = pl.multiple_of(chip * PAIR, 16)
            copies.append(
                pltpu.make_async_copy(
                    source.at[position],
                    w_ref.at[pl.ds(row, PAIR), pl.ds(col, half)],
                    sem.at[len(copies)],
                )
            )
    return copies


def qkv_kernel(sc, x_ref, own, other, qkv_ref, small_ref, upb_ref, w_ref, sem):
    me, width, att = sc[0], sc[1], sc[2]

    @pl.when(pl.program_id(0) == 0)
    def _():
        copies = qkv_copies(me, own, other, w_ref, sem)
        for copy in copies:
            copy.start()
        for copy in copies:
            copy.wait()
        extra = w_ref[:, 3 * ATT : 3 * ATT + EXTRA]
        wide = mm(extra, spread(EXTRA, ROWS, D).astype(BF), NN).reshape(UNITS, ROWS, D)
        shape = (UNITS, ROWS, D)
        start = iota(shape, 0) * ROWS
        lane = iota(shape, 2)
        mine = (lane >= start) & (lane < start + ROWS)
        small_ref[...] = jnp.sum(jnp.where(mine, wide, 0.0), axis=0)
        row8 = extra.reshape(UNITS, ROWS, EXTRA)[:, 8, :]
        wide = mm(row8, spread(EXTRA, FROWS, FF).astype(BF), NN)
        start = iota((UNITS, FF), 0) * FROWS
        lane = iota((UNITS, FF), 1)
        mine = (lane >= start) & (lane < start + FROWS)
        upb_ref[...] = jnp.sum(jnp.where(mine, wide, 0.0), axis=0, keepdims=True)

    x = x_ref[...]
    x = jnp.where(iota(x.shape, 1) < width, x, jnp.zeros_like(x))
    on = iota((1, ATT), 1) < att
    for third in range(3):
        part = mm(x, w_ref[:, third * ATT : (third + 1) * ATT], NN)
        if third == 0:
            part = part + small_ref[0:1, :]
        if third == 2:
            part = part + small_ref[1:2, :]
        part = jnp.where(on, part, 0.0).astype(BF)
        if third == 0:
            part = part * jnp.asarray(HDIM ** (-0.5), BF)
        qkv_ref[:, third * ATT : (third + 1) * ATT] = part


def qkv_call(sc, hidden, own, other):
    hbm = pl.BlockSpec(memory_space=pl.ANY)
    return pl.pallas_call(
        qkv_kernel,
        out_shape=(
            jax.ShapeDtypeStruct((LEN, 3 * ATT), BF),
            jax.ShapeDtypeStruct((ROWS, D), F32),
            jax.ShapeDtypeStruct((1, FF), F32),
        ),
        grid_spec=pltpu.PrefetchScalarGridSpec(
            num_scalar_prefetch=1,
            grid=(LEN // QKV_BLOCK,),
            in_specs=[pl.BlockSpec((QKV_BLOCK, D), lambda i, s: (i, 0)), hbm, hbm],
            out_specs=[
                pl.BlockSpec((QKV_BLOCK, 3 * ATT), lambda i, s: (i, 0)),
                pl.BlockSpec((ROWS, D), lambda i, s: (0, 0)),
                pl.BlockSpec((1, FF), lambda i, s: (0, 0)),
            ],
            scratch_shapes=[pltpu.VMEM((D, QCOLS), BF), pltpu.SemaphoreType.DMA((UNITS,))],
        ),
        compiler_params=params(48),
        cost_estimate=cost(10),
        name="qkv",
    )(sc, hidden, own, other)


FWD_BLOCK = 512


def attend_kernel(sc, q_ref, k_ref, v_ref, o_ref, e_ref, inv_ref):
    length = sc[4]
    half = LEN // 2
    lane = iota((LEN, 128), 1)
    edge = jnp.where(iota((1, half), 1) + half < length, 0.0, NEGATIVE)
    k = k_ref[...]
    v = v_ref[...]
    heads = []
    for h in range(2):
        mine = (lane // HDIM) == h
        heads.append(
            (jnp.where(mine, k, jnp.zeros_like(k)), jnp.where(mine, v, jnp.ones_like(v)))
        )
    left = iota((FWD_BLOCK, 128), 1) < HDIM
    for b in range(LEN // FWD_BLOCK):
        rows = slice(b * FWD_BLOCK, (b + 1) * FWD_BLOCK)
        q = q_ref[rows, :]
        outs, invs = [], []
        for h in range(2):
            keys, values = heads[h]
            scores = mm(q, keys, NT)
            sa = scores[:, :half]
            sb = scores[:, half:] + edge
            top = jnp.maximum(
                jnp.max(sa, axis=1, keepdims=True), jnp.max(sb, axis=1, keepdims=True)
            )
            ea = jnp.exp(sa - top).astype(BF)
            eb = jnp.exp(sb - top).astype(BF)
            e_ref[h, rows, :half] = ea
            e_ref[h, rows, half:] = eb
            o = mm(ea, values[:half], NN) + mm(eb, values[half:], NN)
            inv = 1.0 / pltpu.roll(o, HDIM, 1)
            outs.append(o * inv)
            invs.append(inv)
        o_ref[rows, :] = jnp.where(left, outs[0], outs[1]).astype(BF)
        inv_ref[rows, :] = jnp.where(left, invs[0], invs[1])


def attend_call(sc, qkv, first, pairs):
    def spec(offset):
        return pl.BlockSpec((LEN, 128), lambda i, s: (0, offset + first + i))

    out = pl.BlockSpec((LEN, 128), lambda i, s: (0, i))

    return pl.pallas_call(
        attend_kernel,
        out_shape=(
            jax.ShapeDtypeStruct((LEN, pairs * 128), BF),
            jax.ShapeDtypeStruct((2 * pairs, LEN, LEN), BF),
            jax.ShapeDtypeStruct((LEN, pairs * 128), F32),
        ),
        grid_spec=pltpu.PrefetchScalarGridSpec(
            num_scalar_prefetch=1,
            grid=(pairs,),
            in_specs=[spec(0), spec(PAIRS), spec(2 * PAIRS)],
            out_specs=[out, pl.BlockSpec((2, LEN, LEN), lambda i, s: (i, 0, 0)), out],
        ),
        compiler_params=params(56),
        cost_estimate=cost(4 * pairs),
        name="attend",
    )(sc, qkv, qkv, qkv)


CHAIN_BLOCK = 256
CHUNK = 768


def normal_parts(x):
    t = 1.0 / (1.0 + 0.23164189 * jnp.abs(x))
    gauss = jnp.exp2((x * x) * -0.7213475204444817)
    poly = t * (
        0.127414796
        + t * (-0.142248368 + t * (0.7107068705 + t * (-0.7265760135 + t * 0.5307027145)))
    )
    tail = poly * gauss
    return jnp.where(x >= 0, 1.0 - tail, tail), gauss * 0.3989422804014327


def normalise(v, cm, count):
    mean = jnp.sum(v, axis=1, keepdims=True) / count
    centred = (v - mean) * cm
    var = jnp.sum(centred * centred, axis=1, keepdims=True) / count
    r = lax.rsqrt(var + EPSILON)
    return centred * r, r


def normalise_back(e, yhat, r, gain, cm, count):
    t = e * gain * cm
    s1 = jnp.sum(t, axis=1, keepdims=True) / count
    s2 = jnp.sum(t * yhat, axis=1, keepdims=True) / count
    return r * cm * (t - s1 - yhat * s2)


def width_mask(width):
    return jnp.where(iota((1, D), 1) < width, 1.0, 0.0)


def column_sum(x):
    return jnp.sum(x.astype(F32), axis=0, keepdims=True)


def up_copies(me, own, other, w_ref, sem):
    copies = []
    half = UCOLS // 2
    for source, sibling in ((own, False), (other, True)):
        side = (me & 1) ^ 1 if sibling else me & 1
        col = pl.multiple_of(side * half, 128)
        for position in range(CHIPS):
            chip = held(me, position, GATHER, sibling) >> 1
            row = pl.multiple_of(chip * PAIR, 16)
            copies.append(
                pltpu.make_async_copy(
                    source.at[position],
                    w_ref.at[pl.ds(row, PAIR), pl.ds(col, half)],
                    sem.at[len(copies)],
                )
            )
    return copies


def down_copies(me, own, other, w_ref, sem):
    copies = []
    for source, sibling in ((own, False), (other, True)):
        for position in range(CHIPS):
            unit = held(me, position, GATHER, sibling)
            row = pl.multiple_of(unit * FROWS, 16)
            copies.append(
                pltpu.make_async_copy(
                    source.at[position],
                    w_ref.at[pl.ds(row, FROWS), :],
                    sem.at[len(copies)],
                )
            )
    return copies


def rise_kernel(
    sc,
    ctx0_ref,
    ctx1_ref,
    hid_ref,
    small_ref,
    upb_ref,
    u0,
    u1,
    first_ref,
    nlow_ref,
    act_ref,
    slope_ref,
    wu_ref,
    sem,
):
    me, width, inner = sc[0], sc[1], sc[3]

    @pl.when(pl.program_id(0) == 0)
    def _():
        copies = up_copies(me, u0, u1, wu_ref, sem)
        for copy in copies:
            copy.start()
        for copy in copies:
            copy.wait()

    cm = width_mask(width)
    gain1, bias0, shift1 = small_ref[2:3, :], small_ref[4:5, :], small_ref[5:6, :]
    x = hid_ref[...].astype(F32) * cm
    projected = mm(ctx0_ref[...], wu_ref[:SPLIT, :D], NN) + mm(
        ctx1_ref[...], wu_ref[SPLIT:, :D], NN
    )
    first = x + (projected + bias0) * cm
    first_ref[...] = first
    yhat, _ = normalise(first, cm, width.astype(F32))
    nlow = ((yhat * gain1 + shift1) * cm).astype(BF)
    nlow_ref[...] = nlow
    for j in range(FF // CHUNK):
        cols = slice(j * CHUNK, (j + 1) * CHUNK)
        up_cols = slice(D + j * CHUNK, D + (j + 1) * CHUNK)
        fm = jnp.where(iota((1, CHUNK), 1) + j * CHUNK < inner, 1.0, 0.0)
        pre = (mm(nlow, wu_ref[:, up_cols], NN) + upb_ref[:, cols]) * fm
        cdf, pdf = normal_parts(pre)
        act_ref[:, cols] = (pre * cdf).astype(BF)
        slope_ref[:, cols] = ((cdf + pre * pdf) * fm).astype(BF)


def row_spec(cols):
    return pl.BlockSpec((CHAIN_BLOCK, cols), lambda i, s: (i, 0))


def whole_spec(*shape):
    return pl.BlockSpec(shape, lambda i, s: (0,) * len(shape))


def row_shape(cols, dtype=BF):
    return jax.ShapeDtypeStruct((LEN, cols), dtype)


def rise_call(sc, ctx0, ctx1, hidden, small, upb, u0, u1):
    hbm = pl.BlockSpec(memory_space=pl.ANY)
    return pl.pallas_call(
        rise_kernel,
        out_shape=(
            row_shape(D, F32),
            row_shape(D),
            row_shape(FF),
            row_shape(FF),
        ),
        grid_spec=pltpu.PrefetchScalarGridSpec(
            num_scalar_prefetch=1,
            grid=(LEN // CHAIN_BLOCK,),
            in_specs=[row_spec(SPLIT), row_spec(ATT - SPLIT)]
            + [row_spec(D), whole_spec(ROWS, D), whole_spec(1, FF), hbm, hbm],
            out_specs=[
                row_spec(D),
                row_spec(D),
                row_spec(FF),
                row_spec(FF),
            ],
            scratch_shapes=[pltpu.VMEM((D, UCOLS), BF), pltpu.SemaphoreType.DMA((UNITS,))],
        ),
        compiler_params=params(56),
        cost_estimate=cost(18),
        name="rise",
    )(sc, ctx0, ctx1, hidden, small, upb, u0, u1)


def fall_kernel(
    sc,
    first_ref,
    act_ref,
    slope_ref,
    cot_ref,
    small_ref,
    u0,
    u1,
    d0,
    d1,
    out_ref,
    fgrad_ref,
    pgrad_ref,
    agrad_ref,
    igrad_ref,
    cgrad_ref,
    sums_ref,
    usum_ref,
    wu_ref,
    wd_ref,
    usem,
    dsem,
):
    me, width, length = sc[0], sc[1], sc[4]
    step = pl.program_id(0)

    @pl.when(step == 0)
    def _():
        down = down_copies(me, d0, d1, wd_ref, dsem)
        for copy in down + up_copies(me, u0, u1, wu_ref, usem):
            copy.start()
        sums_ref[...] = jnp.zeros_like(sums_ref)
        usum_ref[...] = jnp.zeros_like(usum_ref)
        for copy in down:
            copy.wait()

    cm = width_mask(width)
    count = width.astype(F32)
    rowpos = step * CHAIN_BLOCK + iota((CHAIN_BLOCK, 1), 0)
    rm = jnp.where(rowpos < length, 1.0, 0.0)
    gain1, gain2 = small_ref[2:3, :], small_ref[3:4, :]
    shift1, bias2, shift3 = small_ref[5:6, :], small_ref[6:7, :], small_ref[7:8, :]

    yhat1, r1 = normalise(first_ref[...], cm, count)
    normed1 = (yhat1 * gain1 + shift1) * cm
    second = normed1 + (mm(act_ref[...], wd_ref[...], NN) + bias2) * cm
    yhat2, r2 = normalise(second, cm, count)
    out_ref[...] = ((yhat2 * gain2 + shift3) * cm * rm).astype(BF)
    e2 = cot_ref[...].astype(F32) * rm
    sums_ref[3:4, :] += column_sum(e2 * yhat2)
    sums_ref[7:8, :] += column_sum(e2 * cm)
    second_grad = normalise_back(e2, yhat2, r2, gain2, cm, count)
    fgrad = second_grad.astype(BF)
    fgrad_ref[...] = fgrad
    sums_ref[6:7, :] += column_sum(fgrad)
    @pl.when(step == 0)
    def _():
        for copy in up_copies(me, u0, u1, wu_ref, usem):
            copy.wait()

    total = second_grad
    for j in range(FF // CHUNK):
        cols = slice(j * CHUNK, (j + 1) * CHUNK)
        up_cols = slice(D + j * CHUNK, D + (j + 1) * CHUNK)
        pgrad = (mm(fgrad, wd_ref[cols, :], NT) * slope_ref[:, cols].astype(F32)).astype(BF)
        pgrad_ref[:, cols] = pgrad
        usum_ref[:, cols] += column_sum(pgrad)
        total = total + mm(pgrad, wu_ref[:, up_cols], NT)
    sums_ref[2:3, :] += column_sum(total * yhat1)
    sums_ref[5:6, :] += column_sum(total * cm)
    first_grad = normalise_back(total, yhat1, r1, gain1, cm, count)
    igrad_ref[...] = first_grad
    agrad = first_grad.astype(BF)
    agrad_ref[...] = agrad
    sums_ref[4:5, :] += column_sum(agrad)
    cgrad_ref[...] = mm(agrad, wu_ref[:, :D], NT).astype(BF)


def fall_call(sc, first, act, slope, cotangent, small, u0, u1, d0, d1):
    hbm = pl.BlockSpec(memory_space=pl.ANY)
    return pl.pallas_call(
        fall_kernel,
        out_shape=(
            row_shape(D),
            row_shape(D),
            row_shape(FF),
            row_shape(D),
            row_shape(D, F32),
            row_shape(ATT),
            jax.ShapeDtypeStruct((8, D), F32),
            jax.ShapeDtypeStruct((1, FF), F32),
        ),
        grid_spec=pltpu.PrefetchScalarGridSpec(
            num_scalar_prefetch=1,
            grid=(LEN // CHAIN_BLOCK,),
            in_specs=[
                row_spec(D),
                row_spec(FF),
                row_spec(FF),
                row_spec(D),
                whole_spec(ROWS, D),
                hbm,
                hbm,
                hbm,
                hbm,
            ],
            out_specs=[
                row_spec(D),
                row_spec(D),
                row_spec(FF),
                row_spec(D),
                row_spec(D),
                row_spec(ATT),
                whole_spec(8, D),
                whole_spec(1, FF),
            ],
            scratch_shapes=[
                pltpu.VMEM((D, UCOLS), BF),
                pltpu.VMEM((FF, D), BF),
                pltpu.SemaphoreType.DMA((UNITS,)),
                pltpu.SemaphoreType.DMA((UNITS,)),
            ],
        ),
        compiler_params=params(58),
        cost_estimate=cost(30),
        name="fall",
    )(sc, first, act, slope, cotangent, small, u0, u1, d0, d1)


def place(acc_ref, keep_ref, send_ref, me, rows):
    for ref, sibling in ((keep_ref, False), (send_ref, True)):
        for position in range(CHIPS):
            unit = held(me, position, SCATTER, sibling)
            row = pl.multiple_of(unit * rows, 8)
            ref[position] = acc_ref[pl.ds(row, rows), :].astype(ref.dtype)


PLANE = 8
DOWN_ROWS = FF // 4


def down_kernel(sc, act_ref, g_ref, keep_ref, send_ref, acc_ref):
    acc_ref[...] = mm(act_ref[...], g_ref[...], TN)
    for ref, sibling in ((keep_ref, False), (send_ref, True)):
        for high in range(4):
            unit = held(sc[0], high * 4, SCATTER, sibling) & (PLANE - 1)
            row = pl.multiple_of(unit * FROWS, 8)
            ref[high, 0] = acc_ref[pl.ds(row, FROWS), :].astype(ref.dtype)


def down_call(sc, act, fgrad):
    def where(i, s):
        z = i ^ (s[0] // PLANE)
        return (0, (z & 1) * 2 + (z >> 1), 0, 0)

    out = pl.BlockSpec((4, 1, FROWS, D), where)
    keep, send = pl.pallas_call(
        down_kernel,
        out_shape=(
            jax.ShapeDtypeStruct((4, 4, FROWS, D), F32),
            jax.ShapeDtypeStruct((4, 4, FROWS, D), SEND),
        ),
        grid_spec=pltpu.PrefetchScalarGridSpec(
            num_scalar_prefetch=1,
            grid=(4,),
            in_specs=[
                pl.BlockSpec((LEN, DOWN_ROWS), lambda i, s: (0, i)),
                pl.BlockSpec((LEN, D), lambda i, s: (0, 0)),
            ],
            out_specs=[out, out],
            scratch_shapes=[pltpu.VMEM((DOWN_ROWS, D), F32)],
        ),
        compiler_params=params(56),
        cost_estimate=cost(14),
        name="down_term",
    )(sc, act, fgrad)
    return keep.reshape(CHIPS, FROWS, D), send.reshape(CHIPS, FROWS, D)


TILE = 768
OUT_TILES = D // TILE
UP_TILES = FF // TILE


def up_kernel(sc, ctx0_ref, ctx1_ref, ag_ref, nlow_ref, pg_ref, keep_ref, send_ref, acc_ref):
    tile = pl.program_id(0)

    @pl.when(tile < OUT_TILES)
    def _():
        acc_ref[:SPLIT, :] = mm(ctx0_ref[...], ag_ref[...], TN)
        acc_ref[SPLIT:, :] = mm(ctx1_ref[...], ag_ref[...], TN)

    @pl.when(tile >= OUT_TILES)
    def _():
        acc_ref[...] = mm(nlow_ref[...], pg_ref[...], TN)

    place(acc_ref, keep_ref, send_ref, sc[0], ROWS)


def up_call(sc, ctx0, ctx1, agrad, nlow, pgrad):
    out = pl.BlockSpec((16, ROWS, TILE), lambda i, s: (0, 0, i))
    cols = D + FF
    return pl.pallas_call(
        up_kernel,
        out_shape=(
            jax.ShapeDtypeStruct((16, ROWS, cols), F32),
            jax.ShapeDtypeStruct((16, ROWS, cols), SEND),
        ),
        grid_spec=pltpu.PrefetchScalarGridSpec(
            num_scalar_prefetch=1,
            grid=(OUT_TILES + UP_TILES,),
            in_specs=[
                pl.BlockSpec((LEN, SPLIT), lambda i, s: (0, 0)),
                pl.BlockSpec((LEN, ATT - SPLIT), lambda i, s: (0, 0)),
                pl.BlockSpec((LEN, TILE), lambda i, s: (0, jnp.minimum(i, OUT_TILES - 1))),
                pl.BlockSpec((LEN, D), lambda i, s: (0, 0)),
                pl.BlockSpec((LEN, TILE), lambda i, s: (0, jnp.maximum(i - OUT_TILES, 0))),
            ],
            out_specs=[out, out],
            scratch_shapes=[pltpu.VMEM((D, TILE), F32)],
        ),
        compiler_params=params(48),
        cost_estimate=cost(17),
        name="up_term",
    )(sc, ctx0, ctx1, agrad, nlow, pgrad)


def qterm_kernel(last, pieces, sc, x_ref, *rest):
    g_refs = rest[:pieces]
    sums_ref, usum_ref, qv_in_ref, *rest = rest[pieces:]
    if last:
        keep_ref, send_ref, acc_ref, qv_ref = rest
    else:
        keep_ref, send_ref, qv_ref, acc_ref = rest
    tile = pl.program_id(0)

    @pl.when(tile < 3)
    def _():
        x = x_ref[...]
        x = jnp.where(iota(x.shape, 1) < sc[1], x, jnp.zeros_like(x))
        g = jnp.concatenate([g_ref[0] for g_ref in g_refs], axis=1)
        acc_ref[...] = mm(x, g, TN)
        column = jnp.sum(g.astype(F32), axis=0, keepdims=True)
        for third in (0, 2):

            @pl.when(tile == third)
            def _():
                qv_ref[third // 2] = column

    if last:

        @pl.when(tile == 3)
        def _():
            high = lax.Precision.HIGHEST
            rows = sums_ref[...]
            pick = iota((8, D), 0)
            for k in range(2):
                row = jnp.concatenate([qv_in_ref[k], qv_ref[k]], axis=1)
                rows = jnp.where(pick == k, row, rows)
            shape = (UNITS, 8, D)
            start = iota(shape, 0) * ROWS
            lane = iota(shape, 2)
            mine = (lane >= start) & (lane < start + ROWS)
            wide = jnp.where(mine, rows[None], 0.0).reshape(UNITS * 8, D)
            small = mm(wide, spread(EXTRA, ROWS, D), NT, high).reshape(UNITS, 8, EXTRA)
            start = iota((UNITS, FF), 0) * FROWS
            lane = iota((UNITS, FF), 1)
            mine = (lane >= start) & (lane < start + FROWS)
            up = mm(jnp.where(mine, usum_ref[...], 0.0), spread(EXTRA, FROWS, FF), NT, high)
            acc_ref[...] = jnp.zeros_like(acc_ref)
            for unit in range(UNITS):
                acc_ref[unit * ROWS : unit * ROWS + 8, 0:EXTRA] = small[unit]
                acc_ref[unit * ROWS + 8 : unit * ROWS + 9, 0:EXTRA] = up[unit : unit + 1]

    place(acc_ref, keep_ref, send_ref, sc[0], ROWS)


def qterm_call(sc, hidden, grads, sums, usum, qv=None):
    last = qv is not None
    width = sum(g.shape[2] for g in grads)
    out = pl.BlockSpec((CHIPS, ROWS, width), lambda i, s: (0, 0, i))
    shape = jax.ShapeDtypeStruct((2, 1, width), F32)
    if not last:
        qv = jnp.zeros(shape.shape, F32)
    cols = width * (4 if last else 3)
    return pl.pallas_call(
        functools.partial(qterm_kernel, last, len(grads)),
        out_shape=(
            jax.ShapeDtypeStruct((CHIPS, ROWS, cols), F32),
            jax.ShapeDtypeStruct((CHIPS, ROWS, cols), SEND),
        )
        + (() if last else (shape,)),
        grid_spec=pltpu.PrefetchScalarGridSpec(
            num_scalar_prefetch=1,
            grid=(cols // width,),
            in_specs=[pl.BlockSpec((LEN, D), lambda i, s: (0, 0))]
            + [
                pl.BlockSpec((1, LEN, g.shape[2]), lambda i, s: (jnp.minimum(i, 2), 0, 0))
                for g in grads
            ]
            + [
                pl.BlockSpec((8, D), lambda i, s: (0, 0)),
                pl.BlockSpec((1, FF), lambda i, s: (0, 0)),
                whole_spec(*qv.shape),
            ],
            out_specs=[out, out] + ([] if last else [whole_spec(*shape.shape)]),
            scratch_shapes=[pltpu.VMEM((D, width), F32)]
            + ([pltpu.VMEM((2, 1, width), F32)] if last else []),
        ),
        compiler_params=params(48),
        cost_estimate=cost(7),
        name="qkv_term",
    )(sc, hidden, *grads, sums, usum, qv)


BWD_BLOCK = 256


def attend_back_kernel(
    first, sc, q_ref, k_ref, v_ref, do_ref, o_ref, e_ref, inv_ref, g_ref, dk_acc, dv_acc
):
    k = k_ref[...]
    v = v_ref[...]
    lane = iota((LEN, 128), 1)
    keys = [jnp.where((lane // HDIM) == h, k, jnp.zeros_like(k)) for h in range(2)]
    lane_q = iota((BWD_BLOCK, 128), 1)
    on = iota((1, 128), 1) + (first + pl.program_id(0)) * 128 < sc[2]
    for b in range(LEN // BWD_BLOCK):
        rows = slice(b * BWD_BLOCK, (b + 1) * BWD_BLOCK)
        q = q_ref[rows, :]
        do = (do_ref[rows, :].astype(F32) * inv_ref[rows, :]).astype(BF)
        both = do.astype(F32) * o_ref[rows, :].astype(F32)
        dq = None
        for h in range(2):
            mine = (lane_q // HDIM) == h
            doh = jnp.where(mine, do, jnp.zeros_like(do))
            qh = jnp.where(mine, q, jnp.zeros_like(q))
            delta = jnp.sum(jnp.where(mine, both, 0.0), axis=1, keepdims=True)
            dp = mm(doh, v, NT)
            e = e_ref[h, rows, :]
            ds = (e.astype(F32) * (dp - delta)).astype(BF)
            part = mm(ds, keys[h], NN)
            dq = part if dq is None else dq + part
            dk = mm(ds, qh, TN)
            dv = mm(e, doh, TN)
            if b == 0 and h == 0:
                dk_acc[...] = dk
                dv_acc[...] = dv
            else:
                dk_acc[...] += dk
                dv_acc[...] += dv
        g_ref[0, rows, :] = jnp.where(on, dq * HDIM ** (-0.5), 0.0).astype(BF)
    g_ref[1] = jnp.where(on, dk_acc[...], 0.0).astype(BF)
    g_ref[2] = jnp.where(on, dv_acc[...], 0.0).astype(BF)


def attend_back_call(sc, qkv, cgrad, part, skip, pairs):
    first, ctx, e, inv = part
    first += skip

    def spec(offset):
        return pl.BlockSpec((LEN, 128), lambda i, s: (0, offset + first + i))

    own = pl.BlockSpec((LEN, 128), lambda i, s: (0, skip + i))
    return pl.pallas_call(
        functools.partial(attend_back_kernel, first),
        out_shape=jax.ShapeDtypeStruct((3, LEN, pairs * 128), BF),
        grid_spec=pltpu.PrefetchScalarGridSpec(
            num_scalar_prefetch=1,
            grid=(pairs,),
            in_specs=[
                spec(0),
                spec(PAIRS),
                spec(2 * PAIRS),
                spec(0),
                own,
                pl.BlockSpec((2, LEN, LEN), lambda i, s: (skip + i, 0, 0)),
                own,
            ],
            out_specs=pl.BlockSpec((3, LEN, 128), lambda i, s: (0, 0, i)),
            scratch_shapes=[pltpu.VMEM((LEN, 128), F32)] * 2,
        ),
        compiler_params=params(56),
        cost_estimate=cost(6 * pairs),
        name="attend_back",
    )(sc, qkv, qkv, qkv, cgrad, ctx, e, inv)


def input_kernel(sc, *refs):
    *parts, own, other, first_ref, out_ref, w_ref, sem = refs

    @pl.when(pl.program_id(0) == 0)
    def _():
        copies = qkv_copies(sc[0], own, other, w_ref, sem)
        for copy in copies:
            copy.start()
        for copy in copies:
            copy.wait()

    total = first_ref[...]
    for third in range(3):
        grads = jnp.concatenate([g_ref[third] for g_ref in parts], axis=1)
        total = total + mm(grads, w_ref[:, third * ATT : (third + 1) * ATT], NT)
    on = iota((1, D), 1) < sc[1]
    out_ref[...] = jnp.where(on, 0.1 * total, 0.0).astype(BF)


def input_call(sc, parts, own, other, first_grad):
    block = 512
    return pl.pallas_call(
        input_kernel,
        out_shape=jax.ShapeDtypeStruct((LEN, D), BF),
        grid_spec=pltpu.PrefetchScalarGridSpec(
            num_scalar_prefetch=1,
            grid=(LEN // block,),
            in_specs=[
                pl.BlockSpec((3, block, g.shape[2]), lambda i, s: (0, i, 0)) for g in parts
            ]
            + [pl.BlockSpec(memory_space=pl.ANY)] * 2
            + [pl.BlockSpec((block, D), lambda i, s: (i, 0))],
            out_specs=pl.BlockSpec((block, D), lambda i, s: (i, 0)),
            scratch_shapes=[pltpu.VMEM((D, QCOLS), BF), pltpu.SemaphoreType.DMA((UNITS,))],
        ),
        compiler_params=params(48),
        cost_estimate=cost(9),
        name="input_grad",
    )(sc, *parts, own, other, first_grad)


def make_local(groups, members):
    fine = groups * members == UNITS
    axes = ("grp", "dp") if fine else ("grp",)

    def swap(x, even, odd=None):
        pair = (even, even if odd is None else odd)
        return lax.ppermute(x, axes, [(i, i ^ pair[i & 1]) for i in range(UNITS)])

    along_z = ((Z2, Z2), (Z1, Z1), (Z1 ^ Z2, Z1 ^ Z2))
    gather_hops = tuple((hop,) for hop in zip(*GATHER)) + (((CORE, CORE),),)
    scatter_hops = (
        (((CORE, CORE),),) + tuple((hop,) for hop in zip(*SCATTER))[:1:-1] + (along_z,)
    )

    class Gather:
        def __init__(self, x):
            self.state, self.stage = [x[None]], 0

        def start(self):
            self.recv = [swap(self.state[0], *hop) for hop in gather_hops[self.stage]]
            self.stage += 1

        def finish(self, *beside):
            if beside:
                self.recv = after(*self.recv, *beside)[: len(self.recv)]
            if self.stage == len(gather_hops):
                return self.state[0], self.recv[0]
            self.state = [jnp.concatenate([self.state[0], *self.recv], axis=0)]

    class Scatter:
        def __init__(self, keep, send):
            self.state, self.stage = [keep, send], 0

        def start(self):
            hops = scatter_hops[self.stage]
            self.recv = [swap(x, *hop) for x, hop in zip(self.state[1:], hops)]
            self.stage += 1

        def finish(self, *beside):
            if beside:
                self.recv = after(*self.recv, *beside)[: len(self.recv)]
            kept = self.state[0]
            if self.stage == len(scatter_hops):
                total = kept[0]
                for recv in self.recv:
                    total = total + recv[0].astype(F32)
                return total
            parts = len(scatter_hops[self.stage]) + 1
            n = kept.shape[0] // parts
            sums = [
                kept[p * n : (p + 1) * n] + self.recv[0][p * n : (p + 1) * n].astype(F32)
                for p in range(parts)
            ]
            self.state = sums[:1] + [x.astype(SEND) for x in sums[1:]]

    def tie(x, *movers):
        x, *flat = after(x, *(a for m in movers for a in m.state))
        for m in movers:
            m.state, flat = flat[: len(m.state)], flat[len(m.state) :]
        return x

    def local(
        hidden,
        lengths,
        subnet,
        qkv_weight,
        qv_bias,
        out_weight,
        up_weight,
        up_bias,
        down_weight,
        norm_gains,
        bias_rows,
        cotangent,
    ):
        group = lax.axis_index("grp")
        me = group * members + lax.axis_index("dp") if fine else group
        if not fine:
            qkv_weight, out_weight, up_weight, up_bias, down_weight = (
                lax.all_gather(w, "dp", axis=0, tiled=True)
                for w in (qkv_weight, out_weight, up_weight, up_bias, down_weight)
            )
            qv_bias, norm_gains, bias_rows = (
                lax.all_gather(w, "dp", axis=1, tiled=True)
                for w in (qv_bias, norm_gains, bias_rows)
            )
        picks = lax.dynamic_index_in_dim(subnet, group, 0, keepdims=False)
        width = D - (2 - picks[0]) * (D // 6)
        heads = HEADS - (2 - picks[1]) * (HEADS // 6)
        inner = width * (6 + picks[2]) // 2
        sc = jnp.stack([me.astype(jnp.int32), width, heads * HDIM, inner, lengths[0]])

        rows = jnp.concatenate([qv_bias, norm_gains, bias_rows], axis=0)
        extra = jnp.concatenate(
            [
                jnp.pad(rows, ((0, 0), (0, EXTRA - ROWS))),
                jnp.pad(up_bias[None], ((0, ROWS - 9), (0, EXTRA - FROWS))),
            ],
            axis=0,
        )
        side = me & 1

        def pair(shard, *beside):
            n = shard.shape[1] // 2
            mine = lax.dynamic_slice_in_dim(shard, side * n, n, 1)
            recv = swap(lax.dynamic_slice_in_dim(shard, (1 - side) * n, n, 1), CORE)
            ordered = [jnp.where(side == 0, mine, recv), jnp.where(side == 0, recv, mine)]
            return jnp.concatenate(ordered, axis=0)

        extra = jnp.pad(extra, ((0, 0), (0, EXTRA)))
        q = pair(jnp.concatenate([qkv_weight, extra], axis=1))
        half = PAIRS // 2
        q = Gather(q)
        q.start()
        q.finish()
        u = pair(jnp.concatenate([tie(out_weight, q), up_weight], axis=1))
        q.start()
        q.finish()
        u = Gather(tie(u, q))
        q.start()
        u.start()
        q.finish()
        u.finish()
        u.state = [tie(u.state[0], q)]
        q.start()
        u.start()
        q.finish()
        u.finish()
        u.state = [tie(u.state[0], q)]
        q.start()
        u.start()
        d = Gather(tie(down_weight, u))
        d.start()
        q0, q1 = q.finish()
        qkv, small, upb = qkv_call(sc, hidden, q0, q1)
        u.finish(small)
        d.finish(small)
        qkv = tie(qkv, u, d)
        u.start()
        d.start()
        ctx0, e0, inv0 = attend_call(sc, qkv, 0, PARTS[0])
        u.finish(inv0)
        d.finish(inv0)
        qkv = tie(qkv, u, d)
        u.start()
        d.start()
        ctx1, e1, inv1 = attend_call(sc, qkv, PARTS[0], PARTS[1])
        d.finish(inv1)
        ctx1 = tie(ctx1, d)
        d.start()
        u0, u1 = u.finish(inv1)
        first, nlow, act, slope = rise_call(sc, ctx0, ctx1, hidden, small, upb, u0, u1)
        d.finish(first)
        d.start()
        d0, d1 = d.finish()
        output, fgrad, pgrad, agrad, first_grad, cgrad, sums, usum = fall_call(
            sc, first, act, slope, cotangent, small, u0, u1, d0, d1
        )

        def step(beside, *movers):
            for m in movers:
                m.finish(beside)
                m.start()

        part0, part1 = (0, ctx0, e0, inv0), (PARTS[0], ctx1, e1, inv1)
        dn = Scatter(*down_call(sc, act, fgrad))
        dn.start()
        uk, us = up_call(sc, ctx0, ctx1, agrad, nlow, tie(pgrad, dn))
        up = Scatter(uk, us)
        step(uk, dn)
        up.start()
        g0 = attend_back_call(sc, qkv, tie(cgrad, dn, up), part0, 0, 2)
        step(g0, dn, up)
        g1 = attend_back_call(sc, qkv, tie(cgrad, dn, up), part0, 2, 2)
        step(g1, dn)
        qk, qs, qv = qterm_call(sc, hidden, (g0, tie(g1, dn)), sums, usum)
        qa = Scatter(qk, qs)
        step(qv, up)
        qa.start()
        g2 = attend_back_call(sc, qkv, tie(cgrad, qa, up), part1, 0, PARTS[1])
        step(g2, up, qa)
        down = dn.finish(g2)
        g2, down = after(tie(g2, up, qa), down)
        qk, qs = qterm_call(sc, hidden, (g2,), sums, usum, qv)
        qb = Scatter(qk, qs)
        qb.start()
        step(qk, qa)
        qb.finish(qa.state[1])
        qb.start()
        grad_hidden = input_call(sc, (g0, g1, g2), q0, q1, tie(first_grad, qb, qa))
        step(grad_hidden, qb)
        qa.finish(qb.state[1])
        up = up.finish(qa.state[1])
        qb.finish()
        both = Scatter(None, None)
        both.state = [jnp.concatenate(x, axis=2) for x in zip(qa.state, qb.state)]
        both.state[0], up = after(both.state[0], up)
        both.stage = qa.stage
        both.start()
        both = both.finish()
        split = 3 * 128 * PARTS[0]
        qa, qb = both[:, :split], both[:, split:]

        wide = tuple(128 * n for n in PARTS)
        ex = qb[:, 3 * wide[1] :]
        qkv_sum = jnp.concatenate(
            [x[:, t * w : (t + 1) * w] for t in range(3) for x, w in zip((qa, qb), wide)],
            axis=1,
        )
        grads = (
            qkv_sum,
            ex[0:2, :ROWS],
            up[:, :D],
            up[:, D:],
            ex[8, :FROWS],
            down,
            ex[2:4, :ROWS],
            ex[4:8, :ROWS],
        )
        if not fine:
            dims = (0, 1, 0, 0, 0, 0, 1, 1)
            grads = tuple(
                lax.psum_scatter(g, "dp", scatter_dimension=d, tiled=True)
                for g, d in zip(grads, dims)
            )
        return (output, grad_hidden) + grads

    return local


def solution(mesh):
    both = ("grp", "dp")
    row, col, flat = P(both, None), P(None, both), P(both)
    placed = (row, flat, P(), row, col, row, row, flat, row, col, col, row)
    return jax.shard_map(
        make_local(mesh.shape["grp"], mesh.shape["dp"]),
        mesh=mesh,
        in_specs=placed,
        out_specs=(row, row, row, col, row, row, flat, row, col, col),
        check_vma=False,
    )
```

```python
import functools

import jax
import jax.numpy as jnp
from jax import lax
from jax.experimental import pallas as pl
from jax.experimental.pallas import tpu as pltpu
from jax.sharding import PartitionSpec as P

D = 768
HEADS = 12
HDIM = 64
FF = 3072
LEN = 1024
ATT = 768
PAIRS = HEADS // 2
PARTS = (4, 2)
SPLIT = PARTS[0] * 128

EPSILON = 1e-05
NEGATIVE = -1e30

UNITS = 32
ROWS = D // UNITS
FROWS = FF // UNITS
PAIR = 2 * ROWS
CHIPS = UNITS // 2
EXTRA = 128
QCOLS = 3 * ATT + 2 * EXTRA
UCOLS = D + FF

BF = jnp.bfloat16
F32 = jnp.float32
SEND = jnp.bfloat16
KEEP = jnp.bfloat16

NN = (((1,), (0,)), ((), ()))
NT = (((1,), (1,)), ((), ()))
TN = (((0,), (0,)), ((), ()))

CORE, AX, AY, Z1, Z2 = 1, 2, 4, 8, 16


def mm(a, b, dims, precision=None):
    return lax.dot_general(a, b, dims, precision=precision, preferred_element_type=F32)


def params(megabytes):
    return pltpu.CompilerParams(vmem_limit_bytes=megabytes << 20)


def cost(micros):
    return pl.CostEstimate(
        flops=int(micros * 1.1e9), transcendentals=0, bytes_accessed=int(micros * 1e6)
    )


def owner(position, masks):
    offset = 0
    for bit, mask in enumerate(masks):
        if (position >> bit) & 1:
            offset ^= mask
    return offset


GATHER = ((Z2, Z1, AX, AY), (Z2, Z1, AY, AX))
SCATTER = ((Z2, Z1, AY, AX), (Z2, Z1, AX, AY))


def held(me, position, orders, sibling=False):
    even, odd = owner(position, orders[0]), owner(position, orders[1])
    parity = me & 1
    if sibling:
        me, parity = me ^ CORE, 1 - parity
    return me ^ jnp.where(parity == 0, even, odd)


def after(x, *others):
    return lax.optimization_barrier((x,) + others)


def iota(shape, axis):
    return lax.broadcasted_iota(jnp.int32, shape, axis)


def spread(width, period, columns):
    col = iota((width, columns), 1)
    turn = jnp.floor((col.astype(F32) + 0.5) * (1.0 / period)).astype(jnp.int32)
    return jnp.where(col - turn * period == iota((width, columns), 0), 1.0, 0.0)


QKV_BLOCK = 512


def qkv_copies(me, own, other, w_ref, sem):
    copies = []
    half = QCOLS // 2
    for source, sibling in ((own, False), (other, True)):
        side = (me & 1) ^ 1 if sibling else me & 1
        col = pl.multiple_of(side * half, 128)
        for position in range(CHIPS):
            chip = held(me, position, GATHER, sibling) >> 1
            row = pl.multiple_of(chip * PAIR, 16)
            copies.append(
                pltpu.make_async_copy(
                    source.at[position],
                    w_ref.at[pl.ds(row, PAIR), pl.ds(col, half)],
                    sem.at[len(copies)],
                )
            )
    return copies


def qkv_kernel(sc, x_ref, own, other, qkv_ref, small_ref, upb_ref, w_ref, sem):
    me, width, att = sc[0], sc[1], sc[2]

    @pl.when(pl.program_id(0) == 0)
    def _():
        copies = qkv_copies(me, own, other, w_ref, sem)
        for copy in copies:
            copy.start()
        for copy in copies:
            copy.wait()
        extra = w_ref[:, 3 * ATT : 3 * ATT + EXTRA]
        wide = mm(extra, spread(EXTRA, ROWS, D).astype(BF), NN).reshape(UNITS, ROWS, D)
        shape = (UNITS, ROWS, D)
        start = iota(shape, 0) * ROWS
        lane = iota(shape, 2)
        mine = (lane >= start) & (lane < start + ROWS)
        small_ref[...] = jnp.sum(jnp.where(mine, wide, 0.0), axis=0)
        row8 = extra.reshape(UNITS, ROWS, EXTRA)[:, 8, :]
        wide = mm(row8, spread(EXTRA, FROWS, FF).astype(BF), NN)
        start = iota((UNITS, FF), 0) * FROWS
        lane = iota((UNITS, FF), 1)
        mine = (lane >= start) & (lane < start + FROWS)
        upb_ref[...] = jnp.sum(jnp.where(mine, wide, 0.0), axis=0, keepdims=True)

    x = x_ref[...]
    x = jnp.where(iota(x.shape, 1) < width, x, jnp.zeros_like(x))
    on = iota((1, ATT), 1) < att
    for third in range(3):
        part = mm(x, w_ref[:, third * ATT : (third + 1) * ATT], NN)
        if third == 0:
            part = part + small_ref[0:1, :]
        if third == 2:
            part = part + small_ref[1:2, :]
        part = jnp.where(on, part, 0.0).astype(BF)
        if third == 0:
            part = part * jnp.asarray(HDIM ** (-0.5), BF)
        qkv_ref[:, third * ATT : (third + 1) * ATT] = part


def qkv_call(sc, hidden, own, other):
    hbm = pl.BlockSpec(memory_space=pl.ANY)
    return pl.pallas_call(
        qkv_kernel,
        out_shape=(
            jax.ShapeDtypeStruct((LEN, 3 * ATT), BF),
            jax.ShapeDtypeStruct((ROWS, D), F32),
            jax.ShapeDtypeStruct((1, FF), F32),
        ),
        grid_spec=pltpu.PrefetchScalarGridSpec(
            num_scalar_prefetch=1,
            grid=(LEN // QKV_BLOCK,),
            in_specs=[pl.BlockSpec((QKV_BLOCK, D), lambda i, s: (i, 0)), hbm, hbm],
            out_specs=[
                pl.BlockSpec((QKV_BLOCK, 3 * ATT), lambda i, s: (i, 0)),
                pl.BlockSpec((ROWS, D), lambda i, s: (0, 0)),
                pl.BlockSpec((1, FF), lambda i, s: (0, 0)),
            ],
            scratch_shapes=[pltpu.VMEM((D, QCOLS), BF), pltpu.SemaphoreType.DMA((UNITS,))],
        ),
        compiler_params=params(24),
        cost_estimate=cost(10),
        name="qkv",
    )(sc, hidden, own, other)


FWD_BLOCK = 512


def attend_kernel(sc, q_ref, k_ref, v_ref, o_ref, e_ref, inv_ref):
    length = sc[4]
    half = LEN // 2
    lane = iota((LEN, 128), 1)
    edge = jnp.where(iota((1, half), 1) + half < length, 0.0, NEGATIVE)
    k = k_ref[...]
    v = v_ref[...]
    heads = []
    for h in range(2):
        mine = (lane // HDIM) == h
        heads.append(
            (jnp.where(mine, k, jnp.zeros_like(k)), jnp.where(mine, v, jnp.ones_like(v)))
        )
    left = iota((FWD_BLOCK, 128), 1) < HDIM
    for b in range(LEN // FWD_BLOCK):
        rows = slice(b * FWD_BLOCK, (b + 1) * FWD_BLOCK)
        q = q_ref[rows, :]
        outs, invs = [], []
        for h in range(2):
            keys, values = heads[h]
            scores = mm(q, keys, NT)
            sa = scores[:, :half]
            sb = scores[:, half:] + edge
            top = jnp.maximum(
                jnp.max(sa, axis=1, keepdims=True), jnp.max(sb, axis=1, keepdims=True)
            )
            ea = jnp.exp(sa - top).astype(BF)
            eb = jnp.exp(sb - top).astype(BF)
            e_ref[h, rows, :half] = ea
            e_ref[h, rows, half:] = eb
            o = mm(ea, values[:half], NN) + mm(eb, values[half:], NN)
            inv = 1.0 / pltpu.roll(o, HDIM, 1)
            outs.append(o * inv)
            invs.append(inv)
        o_ref[rows, :] = jnp.where(left, outs[0], outs[1]).astype(BF)
        inv_ref[rows, :] = jnp.where(left, invs[0], invs[1])


def attend_call(sc, qkv, first, pairs):
    def spec(offset):
        return pl.BlockSpec((LEN, 128), lambda i, s: (0, offset + first + i))

    out = pl.BlockSpec((LEN, 128), lambda i, s: (0, i))

    return pl.pallas_call(
        attend_kernel,
        out_shape=(
            jax.ShapeDtypeStruct((LEN, pairs * 128), BF),
            jax.ShapeDtypeStruct((2 * pairs, LEN, LEN), BF),
            jax.ShapeDtypeStruct((LEN, pairs * 128), F32),
        ),
        grid_spec=pltpu.PrefetchScalarGridSpec(
            num_scalar_prefetch=1,
            grid=(pairs,),
            in_specs=[spec(0), spec(PAIRS), spec(2 * PAIRS)],
            out_specs=[out, pl.BlockSpec((2, LEN, LEN), lambda i, s: (i, 0, 0)), out],
        ),
        compiler_params=params(56),
        cost_estimate=cost(4 * pairs),
        name="attend",
    )(sc, qkv, qkv, qkv)


CHAIN_BLOCK = 256
CHUNK = 768


def normal_parts(x):
    t = 1.0 / (jnp.abs(x) + 4.317008465)
    gauss = jnp.exp2((x * x) * -0.7213475204444817)
    poly = t * (
        0.5500507529
        + t * (-2.651020542 + t * (57.17935007 + t * (-252.3554320 + t * 795.7301438)))
    )
    tail = poly * gauss
    return jnp.where(x >= 0, 1.0 - tail, tail), gauss * 0.3989422804014327


def normalise(v, cm, count):
    mean = jnp.sum(v, axis=1, keepdims=True) / count
    centred = (v - mean) * cm
    var = jnp.sum(centred * centred, axis=1, keepdims=True) / count
    r = lax.rsqrt(var + EPSILON)
    return centred * r, r


def normalise_back(e, yhat, r, gain, cm, count):
    t = e * gain * cm
    s1 = jnp.sum(t, axis=1, keepdims=True) / count
    s2 = jnp.sum(t * yhat, axis=1, keepdims=True) / count
    return r * cm * (t - s1 - yhat * s2)


def width_mask(width):
    return jnp.where(iota((1, D), 1) < width, 1.0, 0.0)


def column_sum(x):
    return jnp.sum(x.astype(F32), axis=0, keepdims=True)


def up_copies(me, own, other, w_ref, sem):
    copies = []
    half = UCOLS // 2
    for source, sibling in ((own, False), (other, True)):
        side = (me & 1) ^ 1 if sibling else me & 1
        col = pl.multiple_of(side * half, 128)
        for position in range(CHIPS):
            chip = held(me, position, GATHER, sibling) >> 1
            row = pl.multiple_of(chip * PAIR, 16)
            copies.append(
                pltpu.make_async_copy(
                    source.at[position],
                    w_ref.at[pl.ds(row, PAIR), pl.ds(col, half)],
                    sem.at[len(copies)],
                )
            )
    return copies


def down_copies(me, own, other, w_ref, sem):
    copies = []
    for source, sibling in ((own, False), (other, True)):
        for position in range(CHIPS):
            unit = held(me, position, GATHER, sibling)
            row = pl.multiple_of(unit * FROWS, 16)
            copies.append(
                pltpu.make_async_copy(
                    source.at[position],
                    w_ref.at[pl.ds(row, FROWS), :],
                    sem.at[len(copies)],
                )
            )
    return copies


def rise_kernel(
    sc,
    ctx0_ref,
    ctx1_ref,
    hid_ref,
    small_ref,
    upb_ref,
    u0,
    u1,
    first_ref,
    nlow_ref,
    act_ref,
    slope_ref,
    wu_ref,
    sem,
):
    me, width, inner = sc[0], sc[1], sc[3]

    @pl.when(pl.program_id(0) == 0)
    def _():
        copies = up_copies(me, u0, u1, wu_ref, sem)
        for copy in copies:
            copy.start()
        for copy in copies:
            copy.wait()

    cm = width_mask(width)
    gain1, bias0, shift1 = small_ref[2:3, :], small_ref[4:5, :], small_ref[5:6, :]
    x = hid_ref[...].astype(F32) * cm
    projected = mm(ctx0_ref[...], wu_ref[:SPLIT, :D], NN) + mm(
        ctx1_ref[...], wu_ref[SPLIT:, :D], NN
    )
    first = x + (projected + bias0) * cm
    first_ref[...] = first
    yhat, _ = normalise(first, cm, width.astype(F32))
    nlow = ((yhat * gain1 + shift1) * cm).astype(BF)
    nlow_ref[...] = nlow
    for j in range(FF // CHUNK):
        cols = slice(j * CHUNK, (j + 1) * CHUNK)
        up_cols = slice(D + j * CHUNK, D + (j + 1) * CHUNK)
        fm = jnp.where(iota((1, CHUNK), 1) + j * CHUNK < inner, 1.0, 0.0)
        pre = (mm(nlow, wu_ref[:, up_cols], NN) + upb_ref[:, cols]) * fm
        cdf, pdf = normal_parts(pre)
        act_ref[:, cols] = (pre * cdf).astype(BF)
        slope_ref[:, cols] = (cdf + pre * pdf).astype(BF)


def row_spec(cols):
    return pl.BlockSpec((CHAIN_BLOCK, cols), lambda i, s: (i, 0))


def whole_spec(*shape):
    return pl.BlockSpec(shape, lambda i, s: (0,) * len(shape))


def row_shape(cols, dtype=BF):
    return jax.ShapeDtypeStruct((LEN, cols), dtype)


def rise_call(sc, ctx0, ctx1, hidden, small, upb, u0, u1):
    hbm = pl.BlockSpec(memory_space=pl.ANY)
    return pl.pallas_call(
        rise_kernel,
        out_shape=(
            row_shape(D, F32),
            row_shape(D),
            row_shape(FF),
            row_shape(FF),
        ),
        grid_spec=pltpu.PrefetchScalarGridSpec(
            num_scalar_prefetch=1,
            grid=(LEN // CHAIN_BLOCK,),
            in_specs=[row_spec(SPLIT), row_spec(ATT - SPLIT)]
            + [row_spec(D), whole_spec(ROWS, D), whole_spec(1, FF), hbm, hbm],
            out_specs=[
                row_spec(D),
                row_spec(D),
                row_spec(FF),
                row_spec(FF),
            ],
            scratch_shapes=[pltpu.VMEM((D, UCOLS), BF), pltpu.SemaphoreType.DMA((UNITS,))],
        ),
        compiler_params=params(56),
        cost_estimate=cost(18),
        name="rise",
    )(sc, ctx0, ctx1, hidden, small, upb, u0, u1)


def fall_kernel(
    sc,
    first_ref,
    act_ref,
    slope_ref,
    cot_ref,
    small_ref,
    u0,
    u1,
    d0,
    d1,
    out_ref,
    fgrad_ref,
    pgrad_ref,
    agrad_ref,
    igrad_ref,
    cgrad_ref,
    sums_ref,
    usum_ref,
    wu_ref,
    wd_ref,
    usem,
    dsem,
):
    me, width, inner, length = sc[0], sc[1], sc[3], sc[4]
    step = pl.program_id(0)

    @pl.when(step == 0)
    def _():
        down = down_copies(me, d0, d1, wd_ref, dsem)
        for copy in down + up_copies(me, u0, u1, wu_ref, usem):
            copy.start()
        sums_ref[...] = jnp.zeros_like(sums_ref)
        usum_ref[...] = jnp.zeros_like(usum_ref)
        for copy in down:
            copy.wait()

    cm = width_mask(width)
    count = width.astype(F32)
    rowpos = step * CHAIN_BLOCK + iota((CHAIN_BLOCK, 1), 0)
    rm = jnp.where(rowpos < length, 1.0, 0.0)
    gain1, gain2 = small_ref[2:3, :], small_ref[3:4, :]
    shift1, bias2, shift3 = small_ref[5:6, :], small_ref[6:7, :], small_ref[7:8, :]

    yhat1, r1 = normalise(first_ref[...], cm, count)
    normed1 = (yhat1 * gain1 + shift1) * cm
    second = normed1 + (mm(act_ref[...], wd_ref[...], NN) + bias2) * cm
    yhat2, r2 = normalise(second, cm, count)
    out_ref[...] = ((yhat2 * gain2 + shift3) * cm * rm).astype(BF)
    e2 = cot_ref[...].astype(F32) * rm
    sums_ref[3:4, :] += column_sum(e2 * yhat2)
    sums_ref[7:8, :] += column_sum(e2 * cm)
    second_grad = normalise_back(e2, yhat2, r2, gain2, cm, count)
    fgrad = second_grad.astype(BF)
    fgrad_ref[...] = fgrad
    sums_ref[6:7, :] += column_sum(fgrad)
    @pl.when(step == 0)
    def _():
        for copy in up_copies(me, u0, u1, wu_ref, usem):
            copy.wait()

    total = second_grad
    for j in range(FF // CHUNK):
        cols = slice(j * CHUNK, (j + 1) * CHUNK)
        up_cols = slice(D + j * CHUNK, D + (j + 1) * CHUNK)
        fm = jnp.where(iota((1, CHUNK), 1) + j * CHUNK < inner, 1.0, 0.0).astype(BF)
        slope = (slope_ref[:, cols] * fm).astype(F32)
        pgrad = (mm(fgrad, wd_ref[cols, :], NT) * slope).astype(BF)
        pgrad_ref[:, cols] = pgrad
        usum_ref[:, cols] += column_sum(pgrad)
        total = total + mm(pgrad, wu_ref[:, up_cols], NT)
    sums_ref[2:3, :] += column_sum(total * yhat1)
    sums_ref[5:6, :] += column_sum(total * cm)
    first_grad = normalise_back(total, yhat1, r1, gain1, cm, count)
    igrad_ref[...] = first_grad
    agrad = first_grad.astype(BF)
    agrad_ref[...] = agrad
    sums_ref[4:5, :] += column_sum(agrad)
    cgrad_ref[...] = mm(agrad, wu_ref[:, :D], NT).astype(BF)


def fall_call(sc, first, act, slope, cotangent, small, u0, u1, d0, d1):
    hbm = pl.BlockSpec(memory_space=pl.ANY)
    return pl.pallas_call(
        fall_kernel,
        out_shape=(
            row_shape(D),
            row_shape(D),
            row_shape(FF),
            row_shape(D),
            row_shape(D, F32),
            row_shape(ATT),
            jax.ShapeDtypeStruct((8, D), F32),
            jax.ShapeDtypeStruct((1, FF), F32),
        ),
        grid_spec=pltpu.PrefetchScalarGridSpec(
            num_scalar_prefetch=1,
            grid=(LEN // CHAIN_BLOCK,),
            in_specs=[
                row_spec(D),
                row_spec(FF),
                row_spec(FF),
                row_spec(D),
                whole_spec(ROWS, D),
                hbm,
                hbm,
                hbm,
                hbm,
            ],
            out_specs=[
                row_spec(D),
                row_spec(D),
                row_spec(FF),
                row_spec(D),
                row_spec(D),
                row_spec(ATT),
                whole_spec(8, D),
                whole_spec(1, FF),
            ],
            scratch_shapes=[
                pltpu.VMEM((D, UCOLS), BF),
                pltpu.VMEM((FF, D), BF),
                pltpu.SemaphoreType.DMA((UNITS,)),
                pltpu.SemaphoreType.DMA((UNITS,)),
            ],
        ),
        compiler_params=params(58),
        cost_estimate=cost(30),
        name="fall",
    )(sc, first, act, slope, cotangent, small, u0, u1, d0, d1)


def place(acc_ref, keep_ref, send_ref, me, rows):
    for ref, sibling in ((keep_ref, False), (send_ref, True)):
        for position in range(CHIPS):
            unit = held(me, position, SCATTER, sibling)
            row = pl.multiple_of(unit * rows, 8)
            ref[position] = acc_ref[pl.ds(row, rows), :].astype(ref.dtype)


PLANE = 8
DOWN_ROWS = FF // 4


def down_kernel(sc, act_ref, g_ref, keep_ref, send_ref, acc_ref):
    acc_ref[...] = mm(act_ref[...], g_ref[...], TN)
    for ref, sibling in ((keep_ref, False), (send_ref, True)):
        for high in range(4):
            unit = held(sc[0], high * 4, SCATTER, sibling) & (PLANE - 1)
            row = pl.multiple_of(unit * FROWS, 8)
            ref[high, 0] = acc_ref[pl.ds(row, FROWS), :].astype(ref.dtype)


def down_call(sc, act, fgrad):
    def where(i, s):
        z = i ^ (s[0] // PLANE)
        return (0, (z & 1) * 2 + (z >> 1), 0, 0)

    out = pl.BlockSpec((4, 1, FROWS, D), where)
    keep, send = pl.pallas_call(
        down_kernel,
        out_shape=(
            jax.ShapeDtypeStruct((4, 4, FROWS, D), KEEP),
            jax.ShapeDtypeStruct((4, 4, FROWS, D), SEND),
        ),
        grid_spec=pltpu.PrefetchScalarGridSpec(
            num_scalar_prefetch=1,
            grid=(4,),
            in_specs=[
                pl.BlockSpec((LEN, DOWN_ROWS), lambda i, s: (0, i)),
                pl.BlockSpec((LEN, D), lambda i, s: (0, 0)),
            ],
            out_specs=[out, out],
            scratch_shapes=[pltpu.VMEM((DOWN_ROWS, D), F32)],
        ),
        compiler_params=params(56),
        cost_estimate=cost(14),
        name="down_term",
    )(sc, act, fgrad)
    return keep.reshape(CHIPS, FROWS, D), send.reshape(CHIPS, FROWS, D)


TILE = 768
OUT_TILES = D // TILE
UP_TILES = FF // TILE


def up_kernel(sc, ctx0_ref, ctx1_ref, ag_ref, nlow_ref, pg_ref, keep_ref, send_ref, acc_ref):
    tile = pl.program_id(0)

    @pl.when(tile < OUT_TILES)
    def _():
        acc_ref[:SPLIT, :] = mm(ctx0_ref[...], ag_ref[...], TN)
        acc_ref[SPLIT:, :] = mm(ctx1_ref[...], ag_ref[...], TN)

    @pl.when(tile >= OUT_TILES)
    def _():
        acc_ref[...] = mm(nlow_ref[...], pg_ref[...], TN)

    place(acc_ref, keep_ref, send_ref, sc[0], ROWS)


def up_call(sc, ctx0, ctx1, agrad, nlow, pgrad):
    out = pl.BlockSpec((16, ROWS, TILE), lambda i, s: (0, 0, i))
    cols = D + FF
    return pl.pallas_call(
        up_kernel,
        out_shape=(
            jax.ShapeDtypeStruct((16, ROWS, cols), KEEP),
            jax.ShapeDtypeStruct((16, ROWS, cols), SEND),
        ),
        grid_spec=pltpu.PrefetchScalarGridSpec(
            num_scalar_prefetch=1,
            grid=(OUT_TILES + UP_TILES,),
            in_specs=[
                pl.BlockSpec((LEN, SPLIT), lambda i, s: (0, 0)),
                pl.BlockSpec((LEN, ATT - SPLIT), lambda i, s: (0, 0)),
                pl.BlockSpec((LEN, TILE), lambda i, s: (0, jnp.minimum(i, OUT_TILES - 1))),
                pl.BlockSpec((LEN, D), lambda i, s: (0, 0)),
                pl.BlockSpec((LEN, TILE), lambda i, s: (0, jnp.maximum(i - OUT_TILES, 0))),
            ],
            out_specs=[out, out],
            scratch_shapes=[pltpu.VMEM((D, TILE), F32)],
        ),
        compiler_params=params(30),
        cost_estimate=cost(17),
        name="up_term",
    )(sc, ctx0, ctx1, agrad, nlow, pgrad)


def qterm_kernel(last, pieces, sc, x_ref, *rest):
    g_refs = rest[:pieces]
    sums_ref, usum_ref, qv_in_ref, *rest = rest[pieces:]
    if last:
        keep_ref, send_ref, acc_ref, qv_ref = rest
    else:
        keep_ref, send_ref, qv_ref, acc_ref = rest
    tile = pl.program_id(0)

    @pl.when(tile < 3)
    def _():
        x = x_ref[...]
        x = jnp.where(iota(x.shape, 1) < sc[1], x, jnp.zeros_like(x))
        g = jnp.concatenate([g_ref[0] for g_ref in g_refs], axis=1)
        acc_ref[...] = mm(x, g, TN)
        column = jnp.sum(g.astype(F32), axis=0, keepdims=True)
        for third in (0, 2):

            @pl.when(tile == third)
            def _():
                qv_ref[third // 2] = column

    if last:

        @pl.when(tile == 3)
        def _():
            high = lax.Precision.HIGHEST
            rows = sums_ref[...]
            pick = iota((8, D), 0)
            for k in range(2):
                row = jnp.concatenate([qv_in_ref[k], qv_ref[k]], axis=1)
                rows = jnp.where(pick == k, row, rows)
            shape = (UNITS, 8, D)
            start = iota(shape, 0) * ROWS
            lane = iota(shape, 2)
            mine = (lane >= start) & (lane < start + ROWS)
            wide = jnp.where(mine, rows[None], 0.0).reshape(UNITS * 8, D)
            small = mm(wide, spread(EXTRA, ROWS, D), NT, high).reshape(UNITS, 8, EXTRA)
            start = iota((UNITS, FF), 0) * FROWS
            lane = iota((UNITS, FF), 1)
            mine = (lane >= start) & (lane < start + FROWS)
            up = mm(jnp.where(mine, usum_ref[...], 0.0), spread(EXTRA, FROWS, FF), NT, high)
            acc_ref[...] = jnp.zeros_like(acc_ref)
            for unit in range(UNITS):
                acc_ref[unit * ROWS : unit * ROWS + 8, 0:EXTRA] = small[unit]
                acc_ref[unit * ROWS + 8 : unit * ROWS + 9, 0:EXTRA] = up[unit : unit + 1]

    place(acc_ref, keep_ref, send_ref, sc[0], ROWS)


def qterm_call(sc, hidden, grads, sums, usum, qv=None):
    last = qv is not None
    width = sum(g.shape[2] for g in grads)
    out = pl.BlockSpec((CHIPS, ROWS, width), lambda i, s: (0, 0, i))
    shape = jax.ShapeDtypeStruct((2, 1, width), F32)
    if not last:
        qv = jnp.zeros(shape.shape, F32)
    cols = width * (4 if last else 3)
    return pl.pallas_call(
        functools.partial(qterm_kernel, last, len(grads)),
        out_shape=(
            jax.ShapeDtypeStruct((CHIPS, ROWS, cols), KEEP),
            jax.ShapeDtypeStruct((CHIPS, ROWS, cols), SEND),
        )
        + (() if last else (shape,)),
        grid_spec=pltpu.PrefetchScalarGridSpec(
            num_scalar_prefetch=1,
            grid=(cols // width,),
            in_specs=[pl.BlockSpec((LEN, D), lambda i, s: (0, 0))]
            + [
                pl.BlockSpec((1, LEN, g.shape[2]), lambda i, s: (jnp.minimum(i, 2), 0, 0))
                for g in grads
            ]
            + [
                pl.BlockSpec((8, D), lambda i, s: (0, 0)),
                pl.BlockSpec((1, FF), lambda i, s: (0, 0)),
                whole_spec(*qv.shape),
            ],
            out_specs=[out, out] + ([] if last else [whole_spec(*shape.shape)]),
            scratch_shapes=[pltpu.VMEM((D, width), F32)]
            + ([pltpu.VMEM((2, 1, width), F32)] if last else []),
        ),
        compiler_params=params(22),
        cost_estimate=cost(7),
        name="qkv_term",
    )(sc, hidden, *grads, sums, usum, qv)


BWD_BLOCK = 256


def attend_back_kernel(
    first, sc, q_ref, k_ref, v_ref, do_ref, o_ref, e_ref, inv_ref, g_ref, dk_acc, dv_acc
):
    k = k_ref[...]
    v = v_ref[...]
    lane = iota((LEN, 128), 1)
    keys = [jnp.where((lane // HDIM) == h, k, jnp.zeros_like(k)) for h in range(2)]
    lane_q = iota((BWD_BLOCK, 128), 1)
    on = iota((1, 128), 1) + (first + pl.program_id(0)) * 128 < sc[2]
    for b in range(LEN // BWD_BLOCK):
        rows = slice(b * BWD_BLOCK, (b + 1) * BWD_BLOCK)
        q = q_ref[rows, :]
        do = (do_ref[rows, :].astype(F32) * inv_ref[rows, :]).astype(BF)
        both = do.astype(F32) * o_ref[rows, :].astype(F32)
        dq = None
        for h in range(2):
            mine = (lane_q // HDIM) == h
            doh = jnp.where(mine, do, jnp.zeros_like(do))
            qh = jnp.where(mine, q, jnp.zeros_like(q))
            delta = jnp.sum(jnp.where(mine, both, 0.0), axis=1, keepdims=True)
            dp = mm(doh, v, NT)
            e = e_ref[h, rows, :]
            ds = (e.astype(F32) * (dp - delta)).astype(BF)
            part = mm(ds, keys[h], NN)
            dq = part if dq is None else dq + part
            dk = mm(ds, qh, TN)
            dv = mm(e, doh, TN)
            if b == 0 and h == 0:
                dk_acc[...] = dk
                dv_acc[...] = dv
            else:
                dk_acc[...] += dk
                dv_acc[...] += dv
        g_ref[0, rows, :] = jnp.where(on, dq * HDIM ** (-0.5), 0.0).astype(BF)
    g_ref[1] = jnp.where(on, dk_acc[...], 0.0).astype(BF)
    g_ref[2] = jnp.where(on, dv_acc[...], 0.0).astype(BF)


def attend_back_call(sc, qkv, cgrad, part, skip, pairs):
    first, ctx, e, inv = part
    first += skip

    def spec(offset):
        return pl.BlockSpec((LEN, 128), lambda i, s: (0, offset + first + i))

    own = pl.BlockSpec((LEN, 128), lambda i, s: (0, skip + i))
    return pl.pallas_call(
        functools.partial(attend_back_kernel, first),
        out_shape=jax.ShapeDtypeStruct((3, LEN, pairs * 128), BF),
        grid_spec=pltpu.PrefetchScalarGridSpec(
            num_scalar_prefetch=1,
            grid=(pairs,),
            in_specs=[
                spec(0),
                spec(PAIRS),
                spec(2 * PAIRS),
                spec(0),
                own,
                pl.BlockSpec((2, LEN, LEN), lambda i, s: (skip + i, 0, 0)),
                own,
            ],
            out_specs=pl.BlockSpec((3, LEN, 128), lambda i, s: (0, 0, i)),
            scratch_shapes=[pltpu.VMEM((LEN, 128), F32)] * 2,
        ),
        compiler_params=params(28),
        cost_estimate=cost(6 * pairs),
        name="attend_back",
    )(sc, qkv, qkv, qkv, cgrad, ctx, e, inv)


def input_kernel(sc, *refs):
    *parts, own, other, first_ref, out_ref, w_ref, sem = refs

    @pl.when(pl.program_id(0) == 0)
    def _():
        copies = qkv_copies(sc[0], own, other, w_ref, sem)
        for copy in copies:
            copy.start()
        for copy in copies:
            copy.wait()

    total = first_ref[...]
    for third in range(3):
        grads = jnp.concatenate([g_ref[third] for g_ref in parts], axis=1)
        total = total + mm(grads, w_ref[:, third * ATT : (third + 1) * ATT], NT)
    on = iota((1, D), 1) < sc[1]
    out_ref[...] = jnp.where(on, 0.1 * total, 0.0).astype(BF)


def input_call(sc, parts, own, other, first_grad):
    block = 512
    return pl.pallas_call(
        input_kernel,
        out_shape=jax.ShapeDtypeStruct((LEN, D), BF),
        grid_spec=pltpu.PrefetchScalarGridSpec(
            num_scalar_prefetch=1,
            grid=(LEN // block,),
            in_specs=[
                pl.BlockSpec((3, block, g.shape[2]), lambda i, s: (0, i, 0)) for g in parts
            ]
            + [pl.BlockSpec(memory_space=pl.ANY)] * 2
            + [pl.BlockSpec((block, D), lambda i, s: (i, 0))],
            out_specs=pl.BlockSpec((block, D), lambda i, s: (i, 0)),
            scratch_shapes=[pltpu.VMEM((D, QCOLS), BF), pltpu.SemaphoreType.DMA((UNITS,))],
        ),
        compiler_params=params(20),
        cost_estimate=cost(9),
        name="input_grad",
    )(sc, *parts, own, other, first_grad)


def outputs_kernel(keep, r0, r1, r2, qkv_ref, qv_ref, gains_ref, biases_ref, upb_ref):
    total = keep[0]
    for r in (r0, r1, r2):
        total = total + r[0].astype(F32)
    col = 0
    for first, pairs in zip((0, PARTS[0]), PARTS):
        for third in range(3):
            to = third * ATT + first * 128
            qkv_ref[:, to : to + pairs * 128] = total[:, col : col + pairs * 128]
            col += pairs * 128
    extra = total[:, col : col + EXTRA]
    qv_ref[...] = extra[0:2, :ROWS]
    gains_ref[...] = extra[2:4, :ROWS]
    biases_ref[...] = extra[4:8, :ROWS]
    upb_ref[...] = extra[8:9, :FROWS]


def outputs_call(keep, recvs):
    return pl.pallas_call(
        outputs_kernel,
        out_shape=tuple(
            jax.ShapeDtypeStruct(shape, F32)
            for shape in ((ROWS, 3 * ATT), (2, ROWS), (2, ROWS), (4, ROWS), (1, FROWS))
        ),
        compiler_params=params(16),
        cost_estimate=cost(2),
        name="outputs",
    )(keep, *recvs)


def make_local(groups, members):
    fine = groups * members == UNITS
    axes = ("grp", "dp") if fine else ("grp",)

    def swap(x, even, odd=None):
        pair = (even, even if odd is None else odd)
        return lax.ppermute(x, axes, [(i, i ^ pair[i & 1]) for i in range(UNITS)])

    along_z = ((Z2, Z2), (Z1, Z1), (Z1 ^ Z2, Z1 ^ Z2))
    gather_hops = tuple((hop,) for hop in zip(*GATHER)) + (((CORE, CORE),),)
    scatter_hops = (
        (((CORE, CORE),),) + tuple((hop,) for hop in zip(*SCATTER))[:1:-1] + (along_z,)
    )

    class Gather:
        def __init__(self, x):
            self.state, self.stage = [x[None]], 0

        def start(self):
            self.recv = [swap(self.state[0], *hop) for hop in gather_hops[self.stage]]
            self.stage += 1

        def finish(self, *beside):
            if beside:
                self.recv = after(*self.recv, *beside)[: len(self.recv)]
            if self.stage == len(gather_hops):
                return self.state[0], self.recv[0]
            self.state = [jnp.concatenate([self.state[0], *self.recv], axis=0)]

    class Scatter:
        def __init__(self, keep, send):
            self.state, self.stage = [keep, send], 0

        def start(self):
            hops = scatter_hops[self.stage]
            self.recv = [swap(x, *hop) for x, hop in zip(self.state[1:], hops)]
            self.stage += 1

        def finish(self, *beside):
            if beside:
                self.recv = after(*self.recv, *beside)[: len(self.recv)]
            kept = self.state[0]
            if self.stage == len(scatter_hops):
                total = kept[0]
                for recv in self.recv:
                    total = total + recv[0].astype(F32)
                return total
            parts = len(scatter_hops[self.stage]) + 1
            n = kept.shape[0] // parts
            sums = [
                kept[p * n : (p + 1) * n].astype(F32) + self.recv[0][p * n : (p + 1) * n].astype(F32)
                for p in range(parts)
            ]
            self.state = sums[:1] + [x.astype(SEND) for x in sums[1:]]

    def tie(x, *movers):
        x, *flat = after(x, *(a for m in movers for a in m.state))
        for m in movers:
            m.state, flat = flat[: len(m.state)], flat[len(m.state) :]
        return x

    def local(
        hidden,
        lengths,
        subnet,
        qkv_weight,
        qv_bias,
        out_weight,
        up_weight,
        up_bias,
        down_weight,
        norm_gains,
        bias_rows,
        cotangent,
    ):
        group = lax.axis_index("grp")
        me = group * members + lax.axis_index("dp") if fine else group
        if not fine:
            qkv_weight, out_weight, up_weight, up_bias, down_weight = (
                lax.all_gather(w, "dp", axis=0, tiled=True)
                for w in (qkv_weight, out_weight, up_weight, up_bias, down_weight)
            )
            qv_bias, norm_gains, bias_rows = (
                lax.all_gather(w, "dp", axis=1, tiled=True)
                for w in (qv_bias, norm_gains, bias_rows)
            )
        picks = lax.dynamic_index_in_dim(subnet, group, 0, keepdims=False)
        width = D - (2 - picks[0]) * (D // 6)
        heads = HEADS - (2 - picks[1]) * (HEADS // 6)
        inner = width * (6 + picks[2]) // 2
        sc = jnp.stack([me.astype(jnp.int32), width, heads * HDIM, inner, lengths[0]])

        rows = jnp.concatenate([qv_bias, norm_gains, bias_rows], axis=0)
        extra = jnp.concatenate(
            [
                jnp.pad(rows, ((0, 0), (0, EXTRA - ROWS))),
                jnp.pad(up_bias[None], ((0, ROWS - 9), (0, EXTRA - FROWS))),
            ],
            axis=0,
        )
        side = me & 1

        def pair(shard, *beside):
            n = shard.shape[1] // 2
            mine = lax.dynamic_slice_in_dim(shard, side * n, n, 1)
            recv = swap(lax.dynamic_slice_in_dim(shard, (1 - side) * n, n, 1), CORE)
            ordered = [jnp.where(side == 0, mine, recv), jnp.where(side == 0, recv, mine)]
            return jnp.concatenate(ordered, axis=0)

        extra = jnp.pad(extra, ((0, 0), (0, EXTRA)))
        q = pair(jnp.concatenate([qkv_weight, extra], axis=1))
        half = PAIRS // 2
        q = Gather(q)
        q.start()
        q.finish()
        u = pair(jnp.concatenate([tie(out_weight, q), up_weight], axis=1))
        q.start()
        q.finish()
        u = Gather(tie(u, q))
        q.start()
        u.start()
        q.finish()
        u.finish()
        u.state = [tie(u.state[0], q)]
        q.start()
        u.start()
        q.finish()
        u.finish()
        u.state = [tie(u.state[0], q)]
        q.start()
        u.start()
        d = Gather(tie(down_weight, u))
        d.start()
        q0, q1 = q.finish()
        qkv, small, upb = qkv_call(sc, hidden, q0, q1)
        u.finish(small)
        d.finish(small)
        qkv = tie(qkv, u, d)
        u.start()
        d.start()
        ctx0, e0, inv0 = attend_call(sc, qkv, 0, PARTS[0])
        u.finish(inv0)
        d.finish(inv0)
        qkv = tie(qkv, u, d)
        u.start()
        d.start()
        ctx1, e1, inv1 = attend_call(sc, qkv, PARTS[0], PARTS[1])
        d.finish(inv1)
        ctx1 = tie(ctx1, d)
        d.start()
        u0, u1 = u.finish(inv1)
        first, nlow, act, slope = rise_call(sc, ctx0, ctx1, hidden, small, upb, u0, u1)
        d.finish(first)
        d.start()
        d0, d1 = d.finish()
        output, fgrad, pgrad, agrad, first_grad, cgrad, sums, usum = fall_call(
            sc, first, act, slope, cotangent, small, u0, u1, d0, d1
        )

        def step(beside, *movers):
            for m in movers:
                m.finish(beside)
                m.start()

        part0, part1 = (0, ctx0, e0, inv0), (PARTS[0], ctx1, e1, inv1)
        dn = Scatter(*down_call(sc, act, fgrad))
        dn.start()
        uk, us = up_call(sc, ctx0, ctx1, agrad, nlow, tie(pgrad, dn))
        up = Scatter(uk, us)
        step(uk, dn)
        up.start()
        g0 = attend_back_call(sc, qkv, tie(cgrad, dn, up), part0, 0, 2)
        step(g0, dn, up)
        g1 = attend_back_call(sc, qkv, tie(cgrad, dn, up), part0, 2, 2)
        step(g1, dn)
        qk, qs, qv = qterm_call(sc, hidden, (g0, tie(g1, dn)), sums, usum)
        qa = Scatter(qk, qs)
        step(qv, up)
        qa.start()
        g2 = attend_back_call(sc, qkv, tie(cgrad, qa, up), part1, 0, PARTS[1])
        step(g2, up, qa)
        down = dn.finish(g2)
        g2, down = after(tie(g2, up, qa), down)
        qk, qs = qterm_call(sc, hidden, (g2,), sums, usum, qv)
        qb = Scatter(qk, qs)
        qb.start()
        step(qk, qa)
        qb.finish(qa.state[1])
        qb.start()
        grad_hidden = input_call(sc, (g0, g1, g2), q0, q1, tie(first_grad, qb, qa))
        step(grad_hidden, qb)
        qa.finish(qb.state[1])
        up = up.finish(qa.state[1])
        qb.finish()
        both = Scatter(None, None)
        both.state = [jnp.concatenate(x, axis=2) for x in zip(qa.state, qb.state)]
        both.state[0], up = after(both.state[0], up)
        both.stage = qa.stage
        both.start()
        qkv_sum, qv_sum, gains_sum, biases_sum, upb_sum = outputs_call(both.state[0], both.recv)
        grads = (
            qkv_sum,
            qv_sum,
            up[:, :D],
            up[:, D:],
            upb_sum.reshape(FROWS),
            down,
            gains_sum,
            biases_sum,
        )
        if not fine:
            dims = (0, 1, 0, 0, 0, 0, 1, 1)
            grads = tuple(
                lax.psum_scatter(g, "dp", scatter_dimension=d, tiled=True)
                for g, d in zip(grads, dims)
            )
        return (output, grad_hidden) + grads

    return local


def solution(mesh):
    both = ("grp", "dp")
    row, col, flat = P(both, None), P(None, both), P(both)
    placed = (row, flat, P(), row, col, row, row, flat, row, col, col, row)
    return jax.shard_map(
        make_local(mesh.shape["grp"], mesh.shape["dp"]),
        mesh=mesh,
        in_specs=placed,
        out_specs=(row, row, row, col, row, row, flat, row, col, col),
        check_vma=False,
    )
```

```python
import functools

import jax
import jax.numpy as jnp
from jax import lax
from jax.experimental import pallas as pl
from jax.experimental.pallas import tpu as pltpu
from jax.sharding import PartitionSpec as P

D = 768
HEADS = 12
HDIM = 64
FF = 3072
LEN = 1024
ATT = 768
PAIRS = HEADS // 2
PARTS = (4, 2)
SPLIT = PARTS[0] * 128

EPSILON = 1e-05
NEGATIVE = -1e30

UNITS = 32
ROWS = D // UNITS
FROWS = FF // UNITS
PAIR = 2 * ROWS
CHIPS = UNITS // 2
EXTRA = 128
QCOLS = 3 * ATT + 2 * EXTRA
UCOLS = D + FF

BF = jnp.bfloat16
F32 = jnp.float32
SEND = jnp.bfloat16
KEEP = jnp.bfloat16

NN = (((1,), (0,)), ((), ()))
NT = (((1,), (1,)), ((), ()))
TN = (((0,), (0,)), ((), ()))

CORE, AX, AY, Z1, Z2 = 1, 2, 4, 8, 16


def mm(a, b, dims, precision=None):
    return lax.dot_general(a, b, dims, precision=precision, preferred_element_type=F32)


def params(megabytes):
    return pltpu.CompilerParams(vmem_limit_bytes=megabytes << 20)


def cost(micros):
    return pl.CostEstimate(
        flops=int(micros * 1.1e9), transcendentals=0, bytes_accessed=int(micros * 1e6)
    )


def owner(position, masks):
    offset = 0
    for bit, mask in enumerate(masks):
        if (position >> bit) & 1:
            offset ^= mask
    return offset


GATHER = ((Z2, Z1, AX, AY), (Z2, Z1, AY, AX))
SCATTER = ((Z2, Z1, AY, AX), (Z2, Z1, AX, AY))


def held(me, position, orders, sibling=False):
    even, odd = owner(position, orders[0]), owner(position, orders[1])
    parity = me & 1
    if sibling:
        me, parity = me ^ CORE, 1 - parity
    return me ^ jnp.where(parity == 0, even, odd)


def after(x, *others):
    return lax.optimization_barrier((x,) + others)


def iota(shape, axis):
    return lax.broadcasted_iota(jnp.int32, shape, axis)


def spread(width, period, columns):
    col = iota((width, columns), 1)
    turn = jnp.floor((col.astype(F32) + 0.5) * (1.0 / period)).astype(jnp.int32)
    return jnp.where(col - turn * period == iota((width, columns), 0), 1.0, 0.0)


QKV_BLOCK = 512


def qkv_copies(me, own, other, w_ref, sem):
    copies = []
    half = QCOLS // 2
    for source, sibling in ((own, False), (other, True)):
        side = (me & 1) ^ 1 if sibling else me & 1
        col = pl.multiple_of(side * half, 128)
        for position in range(CHIPS):
            chip = held(me, position, GATHER, sibling) >> 1
            row = pl.multiple_of(chip * PAIR, 16)
            copies.append(
                pltpu.make_async_copy(
                    source.at[position],
                    w_ref.at[pl.ds(row, PAIR), pl.ds(col, half)],
                    sem.at[len(copies)],
                )
            )
    return copies


def qkv_kernel(sc, x_ref, own, other, qkv_ref, small_ref, upb_ref, w_ref, sem):
    me, width, att = sc[0], sc[1], sc[2]

    @pl.when(pl.program_id(0) == 0)
    def _():
        copies = qkv_copies(me, own, other, w_ref, sem)
        for copy in copies:
            copy.start()
        for copy in copies:
            copy.wait()
        extra = w_ref[:, 3 * ATT : 3 * ATT + EXTRA]
        wide = mm(extra, spread(EXTRA, ROWS, D).astype(BF), NN).reshape(UNITS, ROWS, D)
        shape = (UNITS, ROWS, D)
        start = iota(shape, 0) * ROWS
        lane = iota(shape, 2)
        mine = (lane >= start) & (lane < start + ROWS)
        small_ref[...] = jnp.sum(jnp.where(mine, wide, 0.0), axis=0)
        row8 = extra.reshape(UNITS, ROWS, EXTRA)[:, 8, :]
        wide = mm(row8, spread(EXTRA, FROWS, FF).astype(BF), NN)
        start = iota((UNITS, FF), 0) * FROWS
        lane = iota((UNITS, FF), 1)
        mine = (lane >= start) & (lane < start + FROWS)
        upb_ref[...] = jnp.sum(jnp.where(mine, wide, 0.0), axis=0, keepdims=True)

    x = x_ref[...]
    x = jnp.where(iota(x.shape, 1) < width, x, jnp.zeros_like(x))
    on = iota((1, ATT), 1) < att
    for third in range(3):
        part = mm(x, w_ref[:, third * ATT : (third + 1) * ATT], NN)
        if third == 0:
            part = part + small_ref[0:1, :]
        if third == 2:
            part = part + small_ref[1:2, :]
        part = jnp.where(on, part, 0.0).astype(BF)
        if third == 0:
            part = part * jnp.asarray(HDIM ** (-0.5), BF)
        qkv_ref[:, third * ATT : (third + 1) * ATT] = part


def qkv_call(sc, hidden, own, other):
    hbm = pl.BlockSpec(memory_space=pl.ANY)
    return pl.pallas_call(
        qkv_kernel,
        out_shape=(
            jax.ShapeDtypeStruct((LEN, 3 * ATT), BF),
            jax.ShapeDtypeStruct((ROWS, D), F32),
            jax.ShapeDtypeStruct((1, FF), F32),
        ),
        grid_spec=pltpu.PrefetchScalarGridSpec(
            num_scalar_prefetch=1,
            grid=(LEN // QKV_BLOCK,),
            in_specs=[pl.BlockSpec((QKV_BLOCK, D), lambda i, s: (i, 0)), hbm, hbm],
            out_specs=[
                pl.BlockSpec((QKV_BLOCK, 3 * ATT), lambda i, s: (i, 0)),
                pl.BlockSpec((ROWS, D), lambda i, s: (0, 0)),
                pl.BlockSpec((1, FF), lambda i, s: (0, 0)),
            ],
            scratch_shapes=[pltpu.VMEM((D, QCOLS), BF), pltpu.SemaphoreType.DMA((UNITS,))],
        ),
        compiler_params=params(24),
        cost_estimate=cost(10),
        name="qkv",
    )(sc, hidden, own, other)


FWD_BLOCK = 512


def attend_kernel(sc, q_ref, k_ref, v_ref, o_ref, e_ref, inv_ref):
    length = sc[4]
    half = LEN // 2
    lane = iota((LEN, 128), 1)
    edge = jnp.where(iota((1, half), 1) + half < length, 0.0, NEGATIVE)
    k = k_ref[...]
    v = v_ref[...]
    heads = []
    for h in range(2):
        mine = (lane // HDIM) == h
        heads.append(
            (jnp.where(mine, k, jnp.zeros_like(k)), jnp.where(mine, v, jnp.ones_like(v)))
        )
    left = iota((FWD_BLOCK, 128), 1) < HDIM
    for b in range(LEN // FWD_BLOCK):
        rows = slice(b * FWD_BLOCK, (b + 1) * FWD_BLOCK)
        q = q_ref[rows, :]
        outs, invs = [], []
        for h in range(2):
            keys, values = heads[h]
            scores = mm(q, keys, NT)
            sa = scores[:, :half]
            sb = scores[:, half:] + edge
            top = jnp.maximum(
                jnp.max(sa, axis=1, keepdims=True), jnp.max(sb, axis=1, keepdims=True)
            )
            ea = jnp.exp(sa - top).astype(BF)
            eb = jnp.exp(sb - top).astype(BF)
            e_ref[h, rows, :half] = ea
            e_ref[h, rows, half:] = eb
            o = mm(ea, values[:half], NN) + mm(eb, values[half:], NN)
            inv = 1.0 / pltpu.roll(o, HDIM, 1)
            outs.append(o * inv)
            invs.append(inv)
        o_ref[rows, :] = jnp.where(left, outs[0], outs[1]).astype(BF)
        inv_ref[rows, :] = jnp.where(left, invs[0], invs[1])


def attend_call(sc, qkv, first, pairs):
    def spec(offset):
        return pl.BlockSpec((LEN, 128), lambda i, s: (0, offset + first + i))

    out = pl.BlockSpec((LEN, 128), lambda i, s: (0, i))

    return pl.pallas_call(
        attend_kernel,
        out_shape=(
            jax.ShapeDtypeStruct((LEN, pairs * 128), BF),
            jax.ShapeDtypeStruct((2 * pairs, LEN, LEN), BF),
            jax.ShapeDtypeStruct((LEN, pairs * 128), F32),
        ),
        grid_spec=pltpu.PrefetchScalarGridSpec(
            num_scalar_prefetch=1,
            grid=(pairs,),
            in_specs=[spec(0), spec(PAIRS), spec(2 * PAIRS)],
            out_specs=[out, pl.BlockSpec((2, LEN, LEN), lambda i, s: (i, 0, 0)), out],
        ),
        compiler_params=params(56),
        cost_estimate=cost(4 * pairs),
        name="attend",
    )(sc, qkv, qkv, qkv)


CHAIN_BLOCK = 256
CHUNK = 768


def normal_parts(x):
    t = 1.0 / (jnp.abs(x) + 4.317008465)
    gauss = jnp.exp2((x * x) * -0.7213475204444817)
    poly = t * (
        0.5500507529
        + t * (-2.651020542 + t * (57.17935007 + t * (-252.3554320 + t * 795.7301438)))
    )
    tail = poly * gauss
    return jnp.where(x >= 0, 1.0 - tail, tail), gauss * 0.3989422804014327


def normalise(v, cm, count):
    mean = jnp.sum(v, axis=1, keepdims=True) / count
    centred = (v - mean) * cm
    var = jnp.sum(centred * centred, axis=1, keepdims=True) / count
    r = lax.rsqrt(var + EPSILON)
    return centred * r, r


def normalise_back(e, yhat, r, gain, cm, count):
    t = e * gain * cm
    s1 = jnp.sum(t, axis=1, keepdims=True) / count
    s2 = jnp.sum(t * yhat, axis=1, keepdims=True) / count
    return r * cm * (t - s1 - yhat * s2)


def width_mask(width):
    return jnp.where(iota((1, D), 1) < width, 1.0, 0.0)


def column_sum(x):
    return jnp.sum(x.astype(F32), axis=0, keepdims=True)


def up_copies(me, own, other, w_ref, sem):
    copies = []
    half = UCOLS // 2
    for source, sibling in ((own, False), (other, True)):
        side = (me & 1) ^ 1 if sibling else me & 1
        col = pl.multiple_of(side * half, 128)
        for position in range(CHIPS):
            chip = held(me, position, GATHER, sibling) >> 1
            row = pl.multiple_of(chip * PAIR, 16)
            copies.append(
                pltpu.make_async_copy(
                    source.at[position],
                    w_ref.at[pl.ds(row, PAIR), pl.ds(col, half)],
                    sem.at[len(copies)],
                )
            )
    return copies


def down_copies(me, own, other, w_ref, sem):
    copies = []
    for source, sibling in ((own, False), (other, True)):
        for position in range(CHIPS):
            unit = held(me, position, GATHER, sibling)
            row = pl.multiple_of(unit * FROWS, 16)
            copies.append(
                pltpu.make_async_copy(
                    source.at[position],
                    w_ref.at[pl.ds(row, FROWS), :],
                    sem.at[len(copies)],
                )
            )
    return copies


def rise_kernel(
    sc,
    ctx0_ref,
    ctx1_ref,
    hid_ref,
    small_ref,
    upb_ref,
    u0,
    u1,
    first_ref,
    nlow_ref,
    act_ref,
    slope_ref,
    wu_ref,
    sem,
):
    me, width, inner = sc[0], sc[1], sc[3]

    @pl.when(pl.program_id(0) == 0)
    def _():
        copies = up_copies(me, u0, u1, wu_ref, sem)
        for copy in copies:
            copy.start()
        for copy in copies:
            copy.wait()

    cm = width_mask(width)
    gain1, bias0, shift1 = small_ref[2:3, :], small_ref[4:5, :], small_ref[5:6, :]
    x = hid_ref[...].astype(F32) * cm
    projected = mm(ctx0_ref[...], wu_ref[:SPLIT, :D], NN) + mm(
        ctx1_ref[...], wu_ref[SPLIT:, :D], NN
    )
    first = x + (projected + bias0) * cm
    first_ref[...] = first
    yhat, _ = normalise(first, cm, width.astype(F32))
    nlow = ((yhat * gain1 + shift1) * cm).astype(BF)
    nlow_ref[...] = nlow
    for j in range(FF // CHUNK):
        cols = slice(j * CHUNK, (j + 1) * CHUNK)
        up_cols = slice(D + j * CHUNK, D + (j + 1) * CHUNK)
        fm = jnp.where(iota((1, CHUNK), 1) + j * CHUNK < inner, 1.0, 0.0)
        pre = (mm(nlow, wu_ref[:, up_cols], NN) + upb_ref[:, cols]) * fm
        cdf, pdf = normal_parts(pre)
        act_ref[:, cols] = (pre * cdf).astype(BF)
        slope_ref[:, cols] = (cdf + pre * pdf).astype(BF)


def row_spec(cols):
    return pl.BlockSpec((CHAIN_BLOCK, cols), lambda i, s: (i, 0))


def whole_spec(*shape):
    return pl.BlockSpec(shape, lambda i, s: (0,) * len(shape))


def row_shape(cols, dtype=BF):
    return jax.ShapeDtypeStruct((LEN, cols), dtype)


def rise_call(sc, ctx0, ctx1, hidden, small, upb, u0, u1):
    hbm = pl.BlockSpec(memory_space=pl.ANY)
    return pl.pallas_call(
        rise_kernel,
        out_shape=(
            row_shape(D, F32),
            row_shape(D),
            row_shape(FF),
            row_shape(FF),
        ),
        grid_spec=pltpu.PrefetchScalarGridSpec(
            num_scalar_prefetch=1,
            grid=(LEN // CHAIN_BLOCK,),
            in_specs=[row_spec(SPLIT), row_spec(ATT - SPLIT)]
            + [row_spec(D), whole_spec(ROWS, D), whole_spec(1, FF), hbm, hbm],
            out_specs=[
                row_spec(D),
                row_spec(D),
                row_spec(FF),
                row_spec(FF),
            ],
            scratch_shapes=[pltpu.VMEM((D, UCOLS), BF), pltpu.SemaphoreType.DMA((UNITS,))],
        ),
        compiler_params=params(44),
        cost_estimate=cost(18),
        name="rise",
    )(sc, ctx0, ctx1, hidden, small, upb, u0, u1)


def fall_kernel(
    sc,
    first_ref,
    act_ref,
    slope_ref,
    cot_ref,
    small_ref,
    u0,
    u1,
    d0,
    d1,
    out_ref,
    fgrad_ref,
    pgrad_ref,
    agrad_ref,
    igrad_ref,
    cgrad_ref,
    sums_ref,
    usum_ref,
    wu_ref,
    wd_ref,
    usem,
    dsem,
):
    me, width, inner, length = sc[0], sc[1], sc[3], sc[4]
    step = pl.program_id(0)

    @pl.when(step == 0)
    def _():
        down = down_copies(me, d0, d1, wd_ref, dsem)
        for copy in down + up_copies(me, u0, u1, wu_ref, usem):
            copy.start()
        sums_ref[...] = jnp.zeros_like(sums_ref)
        usum_ref[...] = jnp.zeros_like(usum_ref)
        for copy in down:
            copy.wait()

    cm = width_mask(width)
    count = width.astype(F32)
    rowpos = step * CHAIN_BLOCK + iota((CHAIN_BLOCK, 1), 0)
    rm = jnp.where(rowpos < length, 1.0, 0.0)
    gain1, gain2 = small_ref[2:3, :], small_ref[3:4, :]
    shift1, bias2, shift3 = small_ref[5:6, :], small_ref[6:7, :], small_ref[7:8, :]

    yhat1, r1 = normalise(first_ref[...], cm, count)
    normed1 = (yhat1 * gain1 + shift1) * cm
    second = normed1 + (mm(act_ref[...], wd_ref[...], NN) + bias2) * cm
    yhat2, r2 = normalise(second, cm, count)
    out_ref[...] = ((yhat2 * gain2 + shift3) * cm * rm).astype(BF)
    e2 = cot_ref[...].astype(F32) * rm
    sums_ref[3:4, :] += column_sum(e2 * yhat2)
    sums_ref[7:8, :] += column_sum(e2 * cm)
    second_grad = normalise_back(e2, yhat2, r2, gain2, cm, count)
    fgrad = second_grad.astype(BF)
    fgrad_ref[...] = fgrad
    sums_ref[6:7, :] += column_sum(fgrad)
    @pl.when(step == 0)
    def _():
        for copy in up_copies(me, u0, u1, wu_ref, usem):
            copy.wait()

    total = second_grad
    for j in range(FF // CHUNK):
        cols = slice(j * CHUNK, (j + 1) * CHUNK)
        up_cols = slice(D + j * CHUNK, D + (j + 1) * CHUNK)
        fm = jnp.where(iota((1, CHUNK), 1) + j * CHUNK < inner, 1.0, 0.0).astype(BF)
        slope = (slope_ref[:, cols] * fm).astype(F32)
        pgrad = (mm(fgrad, wd_ref[cols, :], NT) * slope).astype(BF)
        pgrad_ref[:, cols] = pgrad
        usum_ref[:, cols] += column_sum(pgrad)
        total = total + mm(pgrad, wu_ref[:, up_cols], NT)
    sums_ref[2:3, :] += column_sum(total * yhat1)
    sums_ref[5:6, :] += column_sum(total * cm)
    first_grad = normalise_back(total, yhat1, r1, gain1, cm, count)
    igrad_ref[...] = first_grad
    agrad = first_grad.astype(BF)
    agrad_ref[...] = agrad
    sums_ref[4:5, :] += column_sum(agrad)
    cgrad_ref[...] = mm(agrad, wu_ref[:, :D], NT).astype(BF)


def fall_call(sc, first, act, slope, cotangent, small, u0, u1, d0, d1):
    hbm = pl.BlockSpec(memory_space=pl.ANY)
    return pl.pallas_call(
        fall_kernel,
        out_shape=(
            row_shape(D),
            row_shape(D),
            row_shape(FF),
            row_shape(D),
            row_shape(D, F32),
            row_shape(ATT),
            jax.ShapeDtypeStruct((8, D), F32),
            jax.ShapeDtypeStruct((1, FF), F32),
        ),
        grid_spec=pltpu.PrefetchScalarGridSpec(
            num_scalar_prefetch=1,
            grid=(LEN // CHAIN_BLOCK,),
            in_specs=[
                row_spec(D),
                row_spec(FF),
                row_spec(FF),
                row_spec(D),
                whole_spec(ROWS, D),
                hbm,
                hbm,
                hbm,
                hbm,
            ],
            out_specs=[
                row_spec(D),
                row_spec(D),
                row_spec(FF),
                row_spec(D),
                row_spec(D),
                row_spec(ATT),
                whole_spec(8, D),
                whole_spec(1, FF),
            ],
            scratch_shapes=[
                pltpu.VMEM((D, UCOLS), BF),
                pltpu.VMEM((FF, D), BF),
                pltpu.SemaphoreType.DMA((UNITS,)),
                pltpu.SemaphoreType.DMA((UNITS,)),
            ],
        ),
        compiler_params=params(58),
        cost_estimate=cost(30),
        name="fall",
    )(sc, first, act, slope, cotangent, small, u0, u1, d0, d1)


def place(acc_ref, keep_ref, send_ref, me, rows):
    for ref, sibling in ((keep_ref, False), (send_ref, True)):
        for position in range(CHIPS):
            unit = held(me, position, SCATTER, sibling)
            row = pl.multiple_of(unit * rows, 8)
            ref[position] = acc_ref[pl.ds(row, rows), :].astype(ref.dtype)


PLANE = 8
DOWN_ROWS = FF // 4


def down_kernel(sc, act_ref, g_ref, keep_ref, send_ref, acc_ref):
    acc_ref[...] = mm(act_ref[...], g_ref[...], TN)
    for ref, sibling in ((keep_ref, False), (send_ref, True)):
        for high in range(4):
            unit = held(sc[0], high * 4, SCATTER, sibling) & (PLANE - 1)
            row = pl.multiple_of(unit * FROWS, 8)
            ref[high, 0] = acc_ref[pl.ds(row, FROWS), :].astype(ref.dtype)


def down_call(sc, act, fgrad):
    def where(i, s):
        z = i ^ (s[0] // PLANE)
        return (0, (z & 1) * 2 + (z >> 1), 0, 0)

    out = pl.BlockSpec((4, 1, FROWS, D), where)
    keep, send = pl.pallas_call(
        down_kernel,
        out_shape=(
            jax.ShapeDtypeStruct((4, 4, FROWS, D), KEEP),
            jax.ShapeDtypeStruct((4, 4, FROWS, D), SEND),
        ),
        grid_spec=pltpu.PrefetchScalarGridSpec(
            num_scalar_prefetch=1,
            grid=(4,),
            in_specs=[
                pl.BlockSpec((LEN, DOWN_ROWS), lambda i, s: (0, i)),
                pl.BlockSpec((LEN, D), lambda i, s: (0, 0)),
            ],
            out_specs=[out, out],
            scratch_shapes=[pltpu.VMEM((DOWN_ROWS, D), F32)],
        ),
        compiler_params=params(24),
        cost_estimate=cost(14),
        name="down_term",
    )(sc, act, fgrad)
    return keep.reshape(CHIPS, FROWS, D), send.reshape(CHIPS, FROWS, D)


TILE = 768
OUT_TILES = D // TILE
UP_TILES = FF // TILE


def up_kernel(sc, ctx0_ref, ctx1_ref, ag_ref, nlow_ref, pg_ref, keep_ref, send_ref, acc_ref):
    tile = pl.program_id(0)

    @pl.when(tile < OUT_TILES)
    def _():
        acc_ref[:SPLIT, :] = mm(ctx0_ref[...], ag_ref[...], TN)
        acc_ref[SPLIT:, :] = mm(ctx1_ref[...], ag_ref[...], TN)

    @pl.when(tile >= OUT_TILES)
    def _():
        acc_ref[...] = mm(nlow_ref[...], pg_ref[...], TN)

    place(acc_ref, keep_ref, send_ref, sc[0], ROWS)


def up_call(sc, ctx0, ctx1, agrad, nlow, pgrad):
    out = pl.BlockSpec((16, ROWS, TILE), lambda i, s: (0, 0, i))
    cols = D + FF
    return pl.pallas_call(
        up_kernel,
        out_shape=(
            jax.ShapeDtypeStruct((16, ROWS, cols), KEEP),
            jax.ShapeDtypeStruct((16, ROWS, cols), SEND),
        ),
        grid_spec=pltpu.PrefetchScalarGridSpec(
            num_scalar_prefetch=1,
            grid=(OUT_TILES + UP_TILES,),
            in_specs=[
                pl.BlockSpec((LEN, SPLIT), lambda i, s: (0, 0)),
                pl.BlockSpec((LEN, ATT - SPLIT), lambda i, s: (0, 0)),
                pl.BlockSpec((LEN, TILE), lambda i, s: (0, jnp.minimum(i, OUT_TILES - 1))),
                pl.BlockSpec((LEN, D), lambda i, s: (0, 0)),
                pl.BlockSpec((LEN, TILE), lambda i, s: (0, jnp.maximum(i - OUT_TILES, 0))),
            ],
            out_specs=[out, out],
            scratch_shapes=[pltpu.VMEM((D, TILE), F32)],
        ),
        compiler_params=params(30),
        cost_estimate=cost(17),
        name="up_term",
    )(sc, ctx0, ctx1, agrad, nlow, pgrad)


def qterm_kernel(last, pieces, sc, x_ref, *rest):
    g_refs = rest[:pieces]
    sums_ref, usum_ref, qv_in_ref, *rest = rest[pieces:]
    if last:
        keep_ref, send_ref, acc_ref, qv_ref = rest
    else:
        keep_ref, send_ref, qv_ref, acc_ref = rest
    tile = pl.program_id(0)

    @pl.when(tile < 3)
    def _():
        x = x_ref[...]
        x = jnp.where(iota(x.shape, 1) < sc[1], x, jnp.zeros_like(x))
        g = jnp.concatenate([g_ref[0] for g_ref in g_refs], axis=1)
        acc_ref[...] = mm(x, g, TN)
        column = jnp.sum(g.astype(F32), axis=0, keepdims=True)
        for third in (0, 2):

            @pl.when(tile == third)
            def _():
                qv_ref[third // 2] = column

    if last:

        @pl.when(tile == 3)
        def _():
            high = lax.Precision.HIGHEST
            rows = sums_ref[...]
            pick = iota((8, D), 0)
            for k in range(2):
                row = jnp.concatenate([qv_in_ref[k], qv_ref[k]], axis=1)
                rows = jnp.where(pick == k, row, rows)
            shape = (UNITS, 8, D)
            start = iota(shape, 0) * ROWS
            lane = iota(shape, 2)
            mine = (lane >= start) & (lane < start + ROWS)
            wide = jnp.where(mine, rows[None], 0.0).reshape(UNITS * 8, D)
            small = mm(wide, spread(EXTRA, ROWS, D), NT, high).reshape(UNITS, 8, EXTRA)
            start = iota((UNITS, FF), 0) * FROWS
            lane = iota((UNITS, FF), 1)
            mine = (lane >= start) & (lane < start + FROWS)
            up = mm(jnp.where(mine, usum_ref[...], 0.0), spread(EXTRA, FROWS, FF), NT, high)
            acc_ref[...] = jnp.zeros_like(acc_ref)
            for unit in range(UNITS):
                acc_ref[unit * ROWS : unit * ROWS + 8, 0:EXTRA] = small[unit]
                acc_ref[unit * ROWS + 8 : unit * ROWS + 9, 0:EXTRA] = up[unit : unit + 1]

    place(acc_ref, keep_ref, send_ref, sc[0], ROWS)


def qterm_call(sc, hidden, grads, sums, usum, qv=None):
    last = qv is not None
    width = sum(g.shape[2] for g in grads)
    out = pl.BlockSpec((CHIPS, ROWS, width), lambda i, s: (0, 0, i))
    shape = jax.ShapeDtypeStruct((2, 1, width), F32)
    if not last:
        qv = jnp.zeros(shape.shape, F32)
    cols = width * (4 if last else 3)
    return pl.pallas_call(
        functools.partial(qterm_kernel, last, len(grads)),
        out_shape=(
            jax.ShapeDtypeStruct((CHIPS, ROWS, cols), KEEP),
            jax.ShapeDtypeStruct((CHIPS, ROWS, cols), SEND),
        )
        + (() if last else (shape,)),
        grid_spec=pltpu.PrefetchScalarGridSpec(
            num_scalar_prefetch=1,
            grid=(cols // width,),
            in_specs=[pl.BlockSpec((LEN, D), lambda i, s: (0, 0))]
            + [
                pl.BlockSpec((1, LEN, g.shape[2]), lambda i, s: (jnp.minimum(i, 2), 0, 0))
                for g in grads
            ]
            + [
                pl.BlockSpec((8, D), lambda i, s: (0, 0)),
                pl.BlockSpec((1, FF), lambda i, s: (0, 0)),
                whole_spec(*qv.shape),
            ],
            out_specs=[out, out] + ([] if last else [whole_spec(*shape.shape)]),
            scratch_shapes=[pltpu.VMEM((D, width), F32)]
            + ([pltpu.VMEM((2, 1, width), F32)] if last else []),
        ),
        compiler_params=params(22),
        cost_estimate=cost(7),
        name="qkv_term",
    )(sc, hidden, *grads, sums, usum, qv)


BWD_BLOCK = 256


def attend_back_kernel(
    first, sc, q_ref, k_ref, v_ref, do_ref, o_ref, e_ref, inv_ref, g_ref, dk_acc, dv_acc
):
    k = k_ref[...]
    v = v_ref[...]
    lane = iota((LEN, 128), 1)
    keys = [jnp.where((lane // HDIM) == h, k, jnp.zeros_like(k)) for h in range(2)]
    lane_q = iota((BWD_BLOCK, 128), 1)
    on = iota((1, 128), 1) + (first + pl.program_id(0)) * 128 < sc[2]
    for b in range(LEN // BWD_BLOCK):
        rows = slice(b * BWD_BLOCK, (b + 1) * BWD_BLOCK)
        q = q_ref[rows, :]
        do = (do_ref[rows, :].astype(F32) * inv_ref[rows, :]).astype(BF)
        both = do.astype(F32) * o_ref[rows, :].astype(F32)
        dq = None
        for h in range(2):
            mine = (lane_q // HDIM) == h
            doh = jnp.where(mine, do, jnp.zeros_like(do))
            qh = jnp.where(mine, q, jnp.zeros_like(q))
            delta = jnp.sum(jnp.where(mine, both, 0.0), axis=1, keepdims=True)
            dp = mm(doh, v, NT)
            e = e_ref[h, rows, :]
            ds = (e.astype(F32) * (dp - delta)).astype(BF)
            part = mm(ds, keys[h], NN)
            dq = part if dq is None else dq + part
            dk = mm(ds, qh, TN)
            dv = mm(e, doh, TN)
            if b == 0 and h == 0:
                dk_acc[...] = dk
                dv_acc[...] = dv
            else:
                dk_acc[...] += dk
                dv_acc[...] += dv
        g_ref[0, rows, :] = jnp.where(on, dq * HDIM ** (-0.5), 0.0).astype(BF)
    g_ref[1] = jnp.where(on, dk_acc[...], 0.0).astype(BF)
    g_ref[2] = jnp.where(on, dv_acc[...], 0.0).astype(BF)


def attend_back_call(sc, qkv, cgrad, part, skip, pairs):
    first, ctx, e, inv = part
    first += skip

    def spec(offset):
        return pl.BlockSpec((LEN, 128), lambda i, s: (0, offset + first + i))

    own = pl.BlockSpec((LEN, 128), lambda i, s: (0, skip + i))
    return pl.pallas_call(
        functools.partial(attend_back_kernel, first),
        out_shape=jax.ShapeDtypeStruct((3, LEN, pairs * 128), BF),
        grid_spec=pltpu.PrefetchScalarGridSpec(
            num_scalar_prefetch=1,
            grid=(pairs,),
            in_specs=[
                spec(0),
                spec(PAIRS),
                spec(2 * PAIRS),
                spec(0),
                own,
                pl.BlockSpec((2, LEN, LEN), lambda i, s: (skip + i, 0, 0)),
                own,
            ],
            out_specs=pl.BlockSpec((3, LEN, 128), lambda i, s: (0, 0, i)),
            scratch_shapes=[pltpu.VMEM((LEN, 128), F32)] * 2,
        ),
        compiler_params=params(28),
        cost_estimate=cost(6 * pairs),
        name="attend_back",
    )(sc, qkv, qkv, qkv, cgrad, ctx, e, inv)


def input_kernel(sc, *refs):
    *parts, own, other, first_ref, out_ref, w_ref, sem = refs

    @pl.when(pl.program_id(0) == 0)
    def _():
        copies = qkv_copies(sc[0], own, other, w_ref, sem)
        for copy in copies:
            copy.start()
        for copy in copies:
            copy.wait()

    total = first_ref[...]
    for third in range(3):
        grads = jnp.concatenate([g_ref[third] for g_ref in parts], axis=1)
        total = total + mm(grads, w_ref[:, third * ATT : (third + 1) * ATT], NT)
    on = iota((1, D), 1) < sc[1]
    out_ref[...] = jnp.where(on, 0.1 * total, 0.0).astype(BF)


def input_call(sc, parts, own, other, first_grad):
    block = 512
    return pl.pallas_call(
        input_kernel,
        out_shape=jax.ShapeDtypeStruct((LEN, D), BF),
        grid_spec=pltpu.PrefetchScalarGridSpec(
            num_scalar_prefetch=1,
            grid=(LEN // block,),
            in_specs=[
                pl.BlockSpec((3, block, g.shape[2]), lambda i, s: (0, i, 0)) for g in parts
            ]
            + [pl.BlockSpec(memory_space=pl.ANY)] * 2
            + [pl.BlockSpec((block, D), lambda i, s: (i, 0))],
            out_specs=pl.BlockSpec((block, D), lambda i, s: (i, 0)),
            scratch_shapes=[pltpu.VMEM((D, QCOLS), BF), pltpu.SemaphoreType.DMA((UNITS,))],
        ),
        compiler_params=params(20),
        cost_estimate=cost(9),
        name="input_grad",
    )(sc, *parts, own, other, first_grad)


def outputs_kernel(keep, r0, r1, r2, qkv_ref, qv_ref, gains_ref, biases_ref, upb_ref):
    total = keep[0]
    for r in (r0, r1, r2):
        total = total + r[0].astype(F32)
    col = 0
    for first, pairs in zip((0, PARTS[0]), PARTS):
        for third in range(3):
            to = third * ATT + first * 128
            qkv_ref[:, to : to + pairs * 128] = total[:, col : col + pairs * 128]
            col += pairs * 128
    extra = total[:, col : col + EXTRA]
    qv_ref[...] = extra[0:2, :ROWS]
    gains_ref[...] = extra[2:4, :ROWS]
    biases_ref[...] = extra[4:8, :ROWS]
    upb_ref[...] = extra[8:9, :FROWS]


def outputs_call(keep, recvs):
    return pl.pallas_call(
        outputs_kernel,
        out_shape=tuple(
            jax.ShapeDtypeStruct(shape, F32)
            for shape in ((ROWS, 3 * ATT), (2, ROWS), (2, ROWS), (4, ROWS), (1, FROWS))
        ),
        compiler_params=params(16),
        cost_estimate=cost(2),
        name="outputs",
    )(keep, *recvs)


def make_local(groups, members):
    fine = groups * members == UNITS
    axes = ("grp", "dp") if fine else ("grp",)

    def swap(x, even, odd=None):
        pair = (even, even if odd is None else odd)
        return lax.ppermute(x, axes, [(i, i ^ pair[i & 1]) for i in range(UNITS)])

    along_z = ((Z2, Z2), (Z1, Z1), (Z1 ^ Z2, Z1 ^ Z2))
    gather_hops = tuple((hop,) for hop in zip(*GATHER)) + (((CORE, CORE),),)
    scatter_hops = (
        (((CORE, CORE),),) + tuple((hop,) for hop in zip(*SCATTER))[:1:-1] + (along_z,)
    )

    class Gather:
        def __init__(self, x):
            self.state, self.stage = [x[None]], 0

        def start(self):
            self.recv = [swap(self.state[0], *hop) for hop in gather_hops[self.stage]]
            self.stage += 1

        def finish(self, *beside):
            if beside:
                self.recv = after(*self.recv, *beside)[: len(self.recv)]
            if self.stage == len(gather_hops):
                return self.state[0], self.recv[0]
            self.state = [jnp.concatenate([self.state[0], *self.recv], axis=0)]

    class Scatter:
        def __init__(self, keep, send):
            self.state, self.stage = [keep, send], 0

        def start(self):
            hops = scatter_hops[self.stage]
            self.recv = [swap(x, *hop) for x, hop in zip(self.state[1:], hops)]
            self.stage += 1

        def finish(self, *beside):
            if beside:
                self.recv = after(*self.recv, *beside)[: len(self.recv)]
            kept = self.state[0]
            if self.stage == len(scatter_hops):
                total = kept[0]
                for recv in self.recv:
                    total = total + recv[0].astype(F32)
                return total
            parts = len(scatter_hops[self.stage]) + 1
            n = kept.shape[0] // parts
            sums = [
                kept[p * n : (p + 1) * n].astype(F32) + self.recv[0][p * n : (p + 1) * n].astype(F32)
                for p in range(parts)
            ]
            self.state = sums[:1] + [x.astype(SEND) for x in sums[1:]]

    def tie(x, *movers):
        x, *flat = after(x, *(a for m in movers for a in m.state))
        for m in movers:
            m.state, flat = flat[: len(m.state)], flat[len(m.state) :]
        return x

    def local(
        hidden,
        lengths,
        subnet,
        qkv_weight,
        qv_bias,
        out_weight,
        up_weight,
        up_bias,
        down_weight,
        norm_gains,
        bias_rows,
        cotangent,
    ):
        group = lax.axis_index("grp")
        me = group * members + lax.axis_index("dp") if fine else group
        if not fine:
            qkv_weight, out_weight, up_weight, up_bias, down_weight = (
                lax.all_gather(w, "dp", axis=0, tiled=True)
                for w in (qkv_weight, out_weight, up_weight, up_bias, down_weight)
            )
            qv_bias, norm_gains, bias_rows = (
                lax.all_gather(w, "dp", axis=1, tiled=True)
                for w in (qv_bias, norm_gains, bias_rows)
            )
        picks = lax.dynamic_index_in_dim(subnet, group, 0, keepdims=False)
        width = D - (2 - picks[0]) * (D // 6)
        heads = HEADS - (2 - picks[1]) * (HEADS // 6)
        inner = width * (6 + picks[2]) // 2
        sc = jnp.stack([me.astype(jnp.int32), width, heads * HDIM, inner, lengths[0]])

        rows = jnp.concatenate([qv_bias, norm_gains, bias_rows], axis=0)
        extra = jnp.concatenate(
            [
                jnp.pad(rows, ((0, 0), (0, EXTRA - ROWS))),
                jnp.pad(up_bias[None], ((0, ROWS - 9), (0, EXTRA - FROWS))),
            ],
            axis=0,
        )
        side = me & 1

        def pair(shard, *beside):
            n = shard.shape[1] // 2
            mine = lax.dynamic_slice_in_dim(shard, side * n, n, 1)
            recv = swap(lax.dynamic_slice_in_dim(shard, (1 - side) * n, n, 1), CORE)
            ordered = [jnp.where(side == 0, mine, recv), jnp.where(side == 0, recv, mine)]
            return jnp.concatenate(ordered, axis=0)

        extra = jnp.pad(extra, ((0, 0), (0, EXTRA)))
        q = pair(jnp.concatenate([qkv_weight, extra], axis=1))
        half = PAIRS // 2
        q = Gather(q)
        q.start()
        q.finish()
        u = pair(jnp.concatenate([tie(out_weight, q), up_weight], axis=1))
        q.start()
        q.finish()
        u = Gather(tie(u, q))
        q.start()
        u.start()
        q.finish()
        u.finish()
        u.state = [tie(u.state[0], q)]
        q.start()
        u.start()
        q.finish()
        u.finish()
        u.state = [tie(u.state[0], q)]
        q.start()
        u.start()
        d = Gather(tie(down_weight, u))
        d.start()
        q0, q1 = q.finish()
        qkv, small, upb = qkv_call(sc, hidden, q0, q1)
        u.finish(small)
        d.finish(small)
        qkv = tie(qkv, u, d)
        u.start()
        d.start()
        ctx0, e0, inv0 = attend_call(sc, qkv, 0, PARTS[0])
        u.finish(inv0)
        d.finish(inv0)
        qkv = tie(qkv, u, d)
        u.start()
        d.start()
        ctx1, e1, inv1 = attend_call(sc, qkv, PARTS[0], PARTS[1])
        d.finish(inv1)
        ctx1 = tie(ctx1, d)
        d.start()
        u0, u1 = u.finish(inv1)
        first, nlow, act, slope = rise_call(sc, ctx0, ctx1, hidden, small, upb, u0, u1)
        d.finish(first)
        d.start()
        d0, d1 = d.finish()
        output, fgrad, pgrad, agrad, first_grad, cgrad, sums, usum = fall_call(
            sc, first, act, slope, cotangent, small, u0, u1, d0, d1
        )

        def step(beside, *movers):
            for m in movers:
                m.finish(beside)
                m.start()

        part0, part1 = (0, ctx0, e0, inv0), (PARTS[0], ctx1, e1, inv1)
        dn = Scatter(*down_call(sc, act, fgrad))
        dn.start()
        uk, us = up_call(sc, ctx0, ctx1, agrad, nlow, tie(pgrad, dn))
        up = Scatter(uk, us)
        step(uk, dn)
        up.start()
        g0 = attend_back_call(sc, qkv, tie(cgrad, dn, up), part0, 0, 2)
        step(g0, dn, up)
        g1 = attend_back_call(sc, qkv, tie(cgrad, dn, up), part0, 2, 2)
        step(g1, dn)
        qk, qs, qv = qterm_call(sc, hidden, (g0, tie(g1, dn)), sums, usum)
        qa = Scatter(qk, qs)
        step(qv, up)
        qa.start()
        g2 = attend_back_call(sc, qkv, tie(cgrad, qa, up), part1, 0, PARTS[1])
        step(g2, up, qa)
        down = dn.finish(g2)
        g2, down = after(tie(g2, up, qa), down)
        qk, qs = qterm_call(sc, hidden, (g2,), sums, usum, qv)
        qb = Scatter(qk, qs)
        qb.start()
        step(qk, qa)
        qb.finish(qa.state[1])
        qb.start()
        grad_hidden = input_call(sc, (g0, g1, g2), q0, q1, tie(first_grad, qb, qa))
        step(grad_hidden, qb)
        qa.finish(qb.state[1])
        up = up.finish(qa.state[1])
        qb.finish()
        both = Scatter(None, None)
        both.state = [jnp.concatenate(x, axis=2) for x in zip(qa.state, qb.state)]
        both.state[0], up = after(both.state[0], up)
        both.stage = qa.stage
        both.start()
        qkv_sum, qv_sum, gains_sum, biases_sum, upb_sum = outputs_call(both.state[0], both.recv)
        grads = (
            qkv_sum,
            qv_sum,
            up[:, :D],
            up[:, D:],
            upb_sum.reshape(FROWS),
            down,
            gains_sum,
            biases_sum,
        )
        if not fine:
            dims = (0, 1, 0, 0, 0, 0, 1, 1)
            grads = tuple(
                lax.psum_scatter(g, "dp", scatter_dimension=d, tiled=True)
                for g, d in zip(grads, dims)
            )
        return (output, grad_hidden) + grads

    return local


def solution(mesh):
    both = ("grp", "dp")
    row, col, flat = P(both, None), P(None, both), P(both)
    placed = (row, flat, P(), row, col, row, row, flat, row, col, col, row)
    return jax.shard_map(
        make_local(mesh.shape["grp"], mesh.shape["dp"]),
        mesh=mesh,
        in_specs=placed,
        out_specs=(row, row, row, col, row, row, flat, row, col, col),
        check_vma=False,
    )
```

```python
import functools

import jax
import jax.numpy as jnp
from jax import lax
from jax.experimental import pallas as pl
from jax.experimental.pallas import tpu as pltpu
from jax.sharding import PartitionSpec as P

D = 768
HEADS = 12
HDIM = 64
FF = 3072
LEN = 1024
ATT = 768
PAIRS = HEADS // 2
PARTS = (4, 2)
SPLIT = PARTS[0] * 128

EPSILON = 1e-05
NEGATIVE = -1e30

UNITS = 32
ROWS = D // UNITS
FROWS = FF // UNITS
PAIR = 2 * ROWS
CHIPS = UNITS // 2
EXTRA = 128
QCOLS = 3 * ATT + 2 * EXTRA
UCOLS = D + FF

BF = jnp.bfloat16
F32 = jnp.float32
SEND = jnp.bfloat16
KEEP = jnp.bfloat16

NN = (((1,), (0,)), ((), ()))
NT = (((1,), (1,)), ((), ()))
TN = (((0,), (0,)), ((), ()))

CORE, AX, AY, Z1, Z2 = 1, 2, 4, 8, 16


def mm(a, b, dims, precision=None):
    return lax.dot_general(a, b, dims, precision=precision, preferred_element_type=F32)


def params(megabytes):
    return pltpu.CompilerParams(vmem_limit_bytes=megabytes << 20)


def cost(micros):
    return pl.CostEstimate(
        flops=int(micros * 1.1e9), transcendentals=0, bytes_accessed=int(micros * 1e6)
    )


def owner(position, masks):
    offset = 0
    for bit, mask in enumerate(masks):
        if (position >> bit) & 1:
            offset ^= mask
    return offset


GATHER = ((Z2, Z1, AX, AY), (Z2, Z1, AY, AX))
SCATTER = ((Z2, Z1, AY, AX), (Z2, Z1, AX, AY))


def held(me, position, orders, sibling=False):
    even, odd = owner(position, orders[0]), owner(position, orders[1])
    parity = me & 1
    if sibling:
        me, parity = me ^ CORE, 1 - parity
    return me ^ jnp.where(parity == 0, even, odd)


def after(x, *others):
    return lax.optimization_barrier((x,) + others)


def iota(shape, axis):
    return lax.broadcasted_iota(jnp.int32, shape, axis)


def spread(width, period, columns):
    col = iota((width, columns), 1)
    turn = jnp.floor((col.astype(F32) + 0.5) * (1.0 / period)).astype(jnp.int32)
    return jnp.where(col - turn * period == iota((width, columns), 0), 1.0, 0.0)


QKV_BLOCK = 512


def qkv_copies(me, own, other, w_ref, sem):
    copies = []
    half = QCOLS // 2
    for source, sibling in ((own, False), (other, True)):
        side = (me & 1) ^ 1 if sibling else me & 1
        col = pl.multiple_of(side * half, 128)
        for position in range(CHIPS):
            chip = held(me, position, GATHER, sibling) >> 1
            row = pl.multiple_of(chip * PAIR, 16)
            copies.append(
                pltpu.make_async_copy(
                    source.at[position],
                    w_ref.at[pl.ds(row, PAIR), pl.ds(col, half)],
                    sem.at[len(copies)],
                )
            )
    return copies


def qkv_kernel(sc, x_ref, own, other, qkv_ref, small_ref, upb_ref, w_ref, sem):
    me, width, att = sc[0], sc[1], sc[2]

    @pl.when(pl.program_id(0) == 0)
    def _():
        copies = qkv_copies(me, own, other, w_ref, sem)
        for copy in copies:
            copy.start()
        for copy in copies:
            copy.wait()
        extra = w_ref[:, 3 * ATT : 3 * ATT + EXTRA]
        wide = mm(extra, spread(EXTRA, ROWS, D).astype(BF), NN).reshape(UNITS, ROWS, D)
        shape = (UNITS, ROWS, D)
        start = iota(shape, 0) * ROWS
        lane = iota(shape, 2)
        mine = (lane >= start) & (lane < start + ROWS)
        small_ref[...] = jnp.sum(jnp.where(mine, wide, 0.0), axis=0)
        row8 = extra.reshape(UNITS, ROWS, EXTRA)[:, 8, :]
        wide = mm(row8, spread(EXTRA, FROWS, FF).astype(BF), NN)
        start = iota((UNITS, FF), 0) * FROWS
        lane = iota((UNITS, FF), 1)
        mine = (lane >= start) & (lane < start + FROWS)
        upb_ref[...] = jnp.sum(jnp.where(mine, wide, 0.0), axis=0, keepdims=True)

    x = x_ref[...]
    x = jnp.where(iota(x.shape, 1) < width, x, jnp.zeros_like(x))
    on = iota((1, ATT), 1) < att
    for third in range(3):
        part = mm(x, w_ref[:, third * ATT : (third + 1) * ATT], NN)
        if third == 0:
            part = part + small_ref[0:1, :]
        if third == 2:
            part = part + small_ref[1:2, :]
        part = jnp.where(on, part, 0.0).astype(BF)
        if third == 0:
            part = part * jnp.asarray(HDIM ** (-0.5), BF)
        qkv_ref[:, third * ATT : (third + 1) * ATT] = part


def qkv_call(sc, hidden, own, other):
    hbm = pl.BlockSpec(memory_space=pl.ANY)
    return pl.pallas_call(
        qkv_kernel,
        out_shape=(
            jax.ShapeDtypeStruct((LEN, 3 * ATT), BF),
            jax.ShapeDtypeStruct((ROWS, D), F32),
            jax.ShapeDtypeStruct((1, FF), F32),
        ),
        grid_spec=pltpu.PrefetchScalarGridSpec(
            num_scalar_prefetch=1,
            grid=(LEN // QKV_BLOCK,),
            in_specs=[pl.BlockSpec((QKV_BLOCK, D), lambda i, s: (i, 0)), hbm, hbm],
            out_specs=[
                pl.BlockSpec((QKV_BLOCK, 3 * ATT), lambda i, s: (i, 0)),
                pl.BlockSpec((ROWS, D), lambda i, s: (0, 0)),
                pl.BlockSpec((1, FF), lambda i, s: (0, 0)),
            ],
            scratch_shapes=[pltpu.VMEM((D, QCOLS), BF), pltpu.SemaphoreType.DMA((UNITS,))],
        ),
        compiler_params=params(24),
        cost_estimate=cost(10),
        name="qkv",
    )(sc, hidden, own, other)


FWD_BLOCK = 512


def attend_kernel(sc, q_ref, k_ref, v_ref, o_ref, e_ref, inv_ref):
    length = sc[4]
    half = LEN // 2
    lane = iota((LEN, 128), 1)
    edge = jnp.where(iota((1, half), 1) + half < length, 0.0, NEGATIVE)
    k = k_ref[...]
    v = v_ref[...]
    heads = []
    for h in range(2):
        mine = (lane // HDIM) == h
        heads.append(
            (jnp.where(mine, k, jnp.zeros_like(k)), jnp.where(mine, v, jnp.ones_like(v)))
        )
    left = iota((FWD_BLOCK, 128), 1) < HDIM
    for b in range(LEN // FWD_BLOCK):
        rows = slice(b * FWD_BLOCK, (b + 1) * FWD_BLOCK)
        q = q_ref[rows, :]
        outs, invs = [], []
        for h in range(2):
            keys, values = heads[h]
            scores = mm(q, keys, NT)
            sa = scores[:, :half]
            sb = scores[:, half:] + edge
            top = jnp.maximum(
                jnp.max(sa, axis=1, keepdims=True), jnp.max(sb, axis=1, keepdims=True)
            )
            ea = jnp.exp(sa - top).astype(BF)
            eb = jnp.exp(sb - top).astype(BF)
            e_ref[h, rows, :half] = ea
            e_ref[h, rows, half:] = eb
            o = mm(ea, values[:half], NN) + mm(eb, values[half:], NN)
            inv = 1.0 / pltpu.roll(o, HDIM, 1)
            outs.append(o * inv)
            invs.append(inv)
        o_ref[rows, :] = jnp.where(left, outs[0], outs[1]).astype(BF)
        inv_ref[rows, :] = jnp.where(left, invs[0], invs[1])


def attend_call(sc, qkv, first, pairs):
    def spec(offset):
        return pl.BlockSpec((LEN, 128), lambda i, s: (0, offset + first + i))

    out = pl.BlockSpec((LEN, 128), lambda i, s: (0, i))

    return pl.pallas_call(
        attend_kernel,
        out_shape=(
            jax.ShapeDtypeStruct((LEN, pairs * 128), BF),
            jax.ShapeDtypeStruct((2 * pairs, LEN, LEN), BF),
            jax.ShapeDtypeStruct((LEN, pairs * 128), F32),
        ),
        grid_spec=pltpu.PrefetchScalarGridSpec(
            num_scalar_prefetch=1,
            grid=(pairs,),
            in_specs=[spec(0), spec(PAIRS), spec(2 * PAIRS)],
            out_specs=[out, pl.BlockSpec((2, LEN, LEN), lambda i, s: (i, 0, 0)), out],
        ),
        compiler_params=params(56),
        cost_estimate=cost(4 * pairs),
        name="attend",
    )(sc, qkv, qkv, qkv)


CHAIN_BLOCK = 256
CHUNK = 768


def normal_parts(x):
    t = 1.0 / (jnp.abs(x) + 4.317008465)
    gauss = jnp.exp2((x * x) * -0.7213475204444817)
    poly = t * (
        0.5500507529
        + t * (-2.651020542 + t * (57.17935007 + t * (-252.3554320 + t * 795.7301438)))
    )
    tail = poly * gauss
    return jnp.where(x >= 0, 1.0 - tail, tail), gauss * 0.3989422804014327


def normalise(v, cm, count):
    mean = jnp.sum(v, axis=1, keepdims=True) / count
    centred = (v - mean) * cm
    var = jnp.sum(centred * centred, axis=1, keepdims=True) / count
    r = lax.rsqrt(var + EPSILON)
    return centred * r, r


def normalise_back(e, yhat, r, gain, cm, count):
    t = e * gain * cm
    s1 = jnp.sum(t, axis=1, keepdims=True) / count
    s2 = jnp.sum(t * yhat, axis=1, keepdims=True) / count
    return r * cm * (t - s1 - yhat * s2)


def width_mask(width):
    return jnp.where(iota((1, D), 1) < width, 1.0, 0.0)


def column_sum(x):
    return jnp.sum(x.astype(F32), axis=0, keepdims=True)


def up_copies(me, own, other, w_ref, sem):
    copies = []
    half = UCOLS // 2
    for source, sibling in ((own, False), (other, True)):
        side = (me & 1) ^ 1 if sibling else me & 1
        col = pl.multiple_of(side * half, 128)
        for position in range(CHIPS):
            chip = held(me, position, GATHER, sibling) >> 1
            row = pl.multiple_of(chip * PAIR, 16)
            copies.append(
                pltpu.make_async_copy(
                    source.at[position],
                    w_ref.at[pl.ds(row, PAIR), pl.ds(col, half)],
                    sem.at[len(copies)],
                )
            )
    return copies


def down_copies(me, own, other, w_ref, sem):
    copies = []
    for source, sibling in ((own, False), (other, True)):
        for position in range(CHIPS):
            unit = held(me, position, GATHER, sibling)
            row = pl.multiple_of(unit * FROWS, 16)
            copies.append(
                pltpu.make_async_copy(
                    source.at[position],
                    w_ref.at[pl.ds(row, FROWS), :],
                    sem.at[len(copies)],
                )
            )
    return copies


def rise_kernel(
    sc,
    ctx0_ref,
    ctx1_ref,
    hid_ref,
    small_ref,
    upb_ref,
    u0,
    u1,
    first_ref,
    nlow_ref,
    act_ref,
    slope_ref,
    wu_ref,
    sem,
):
    me, width, inner = sc[0], sc[1], sc[3]

    @pl.when(pl.program_id(0) == 0)
    def _():
        copies = up_copies(me, u0, u1, wu_ref, sem)
        for copy in copies:
            copy.start()
        for copy in copies:
            copy.wait()

    cm = width_mask(width)
    gain1, bias0, shift1 = small_ref[2:3, :], small_ref[4:5, :], small_ref[5:6, :]
    x = hid_ref[...].astype(F32) * cm
    projected = mm(ctx0_ref[...], wu_ref[:SPLIT, :D], NN) + mm(
        ctx1_ref[...], wu_ref[SPLIT:, :D], NN
    )
    first = x + (projected + bias0) * cm
    first_ref[...] = first
    yhat, _ = normalise(first, cm, width.astype(F32))
    nlow = ((yhat * gain1 + shift1) * cm).astype(BF)
    nlow_ref[...] = nlow
    for j in range(FF // CHUNK):
        cols = slice(j * CHUNK, (j + 1) * CHUNK)
        up_cols = slice(D + j * CHUNK, D + (j + 1) * CHUNK)
        fm = jnp.where(iota((1, CHUNK), 1) + j * CHUNK < inner, 1.0, 0.0)
        pre = (mm(nlow, wu_ref[:, up_cols], NN) + upb_ref[:, cols]) * fm
        cdf, pdf = normal_parts(pre)
        act_ref[:, cols] = (pre * cdf).astype(BF)
        slope_ref[:, cols] = (cdf + pre * pdf).astype(BF)


def row_spec(cols):
    return pl.BlockSpec((CHAIN_BLOCK, cols), lambda i, s: (i, 0))


def whole_spec(*shape):
    return pl.BlockSpec(shape, lambda i, s: (0,) * len(shape))


def row_shape(cols, dtype=BF):
    return jax.ShapeDtypeStruct((LEN, cols), dtype)


def rise_call(sc, ctx0, ctx1, hidden, small, upb, u0, u1):
    hbm = pl.BlockSpec(memory_space=pl.ANY)
    return pl.pallas_call(
        rise_kernel,
        out_shape=(
            row_shape(D, F32),
            row_shape(D),
            row_shape(FF),
            row_shape(FF),
        ),
        grid_spec=pltpu.PrefetchScalarGridSpec(
            num_scalar_prefetch=1,
            grid=(LEN // CHAIN_BLOCK,),
            in_specs=[row_spec(SPLIT), row_spec(ATT - SPLIT)]
            + [row_spec(D), whole_spec(ROWS, D), whole_spec(1, FF), hbm, hbm],
            out_specs=[
                row_spec(D),
                row_spec(D),
                row_spec(FF),
                row_spec(FF),
            ],
            scratch_shapes=[pltpu.VMEM((D, UCOLS), BF), pltpu.SemaphoreType.DMA((UNITS,))],
        ),
        compiler_params=params(44),
        cost_estimate=cost(18),
        name="rise",
    )(sc, ctx0, ctx1, hidden, small, upb, u0, u1)


def fall_kernel(
    sc,
    first_ref,
    act_ref,
    slope_ref,
    cot_ref,
    small_ref,
    u0,
    u1,
    d0,
    d1,
    out_ref,
    fgrad_ref,
    pgrad_ref,
    agrad_ref,
    igrad_ref,
    cgrad_ref,
    sums_ref,
    usum_ref,
    wu_ref,
    wd_ref,
    usem,
    dsem,
):
    me, width, inner, length = sc[0], sc[1], sc[3], sc[4]
    step = pl.program_id(0)

    @pl.when(step == 0)
    def _():
        down = down_copies(me, d0, d1, wd_ref, dsem)
        for copy in down + up_copies(me, u0, u1, wu_ref, usem):
            copy.start()
        sums_ref[...] = jnp.zeros_like(sums_ref)
        usum_ref[...] = jnp.zeros_like(usum_ref)
        for copy in down:
            copy.wait()

    cm = width_mask(width)
    count = width.astype(F32)
    rowpos = step * CHAIN_BLOCK + iota((CHAIN_BLOCK, 1), 0)
    rm = jnp.where(rowpos < length, 1.0, 0.0)
    gain1, gain2 = small_ref[2:3, :], small_ref[3:4, :]
    shift1, bias2, shift3 = small_ref[5:6, :], small_ref[6:7, :], small_ref[7:8, :]

    yhat1, r1 = normalise(first_ref[...], cm, count)
    normed1 = (yhat1 * gain1 + shift1) * cm
    second = normed1 + (mm(act_ref[...], wd_ref[...], NN) + bias2) * cm
    yhat2, r2 = normalise(second, cm, count)
    out_ref[...] = ((yhat2 * gain2 + shift3) * cm * rm).astype(BF)
    e2 = cot_ref[...].astype(F32) * rm
    sums_ref[3:4, :] += column_sum(e2 * yhat2)
    sums_ref[7:8, :] += column_sum(e2 * cm)
    second_grad = normalise_back(e2, yhat2, r2, gain2, cm, count)
    fgrad = second_grad.astype(BF)
    fgrad_ref[...] = fgrad
    sums_ref[6:7, :] += column_sum(fgrad)
    @pl.when(step == 0)
    def _():
        for copy in up_copies(me, u0, u1, wu_ref, usem):
            copy.wait()

    total = second_grad
    for j in range(FF // CHUNK):
        cols = slice(j * CHUNK, (j + 1) * CHUNK)
        up_cols = slice(D + j * CHUNK, D + (j + 1) * CHUNK)
        fm = jnp.where(iota((1, CHUNK), 1) + j * CHUNK < inner, 1.0, 0.0).astype(BF)
        slope = (slope_ref[:, cols] * fm).astype(F32)
        pgrad = (mm(fgrad, wd_ref[cols, :], NT) * slope).astype(BF)
        pgrad_ref[:, cols] = pgrad
        usum_ref[:, cols] += column_sum(pgrad)
        total = total + mm(pgrad, wu_ref[:, up_cols], NT)
    sums_ref[2:3, :] += column_sum(total * yhat1)
    sums_ref[5:6, :] += column_sum(total * cm)
    first_grad = normalise_back(total, yhat1, r1, gain1, cm, count)
    igrad_ref[...] = first_grad
    agrad = first_grad.astype(BF)
    agrad_ref[...] = agrad
    sums_ref[4:5, :] += column_sum(agrad)
    cgrad_ref[...] = mm(agrad, wu_ref[:, :D], NT).astype(BF)


def fall_call(sc, first, act, slope, cotangent, small, u0, u1, d0, d1):
    hbm = pl.BlockSpec(memory_space=pl.ANY)
    return pl.pallas_call(
        fall_kernel,
        out_shape=(
            row_shape(D),
            row_shape(D),
            row_shape(FF),
            row_shape(D),
            row_shape(D, F32),
            row_shape(ATT),
            jax.ShapeDtypeStruct((8, D), F32),
            jax.ShapeDtypeStruct((1, FF), F32),
        ),
        grid_spec=pltpu.PrefetchScalarGridSpec(
            num_scalar_prefetch=1,
            grid=(LEN // CHAIN_BLOCK,),
            in_specs=[
                row_spec(D),
                row_spec(FF),
                row_spec(FF),
                row_spec(D),
                whole_spec(ROWS, D),
                hbm,
                hbm,
                hbm,
                hbm,
            ],
            out_specs=[
                row_spec(D),
                row_spec(D),
                row_spec(FF),
                row_spec(D),
                row_spec(D),
                row_spec(ATT),
                whole_spec(8, D),
                whole_spec(1, FF),
            ],
            scratch_shapes=[
                pltpu.VMEM((D, UCOLS), BF),
                pltpu.VMEM((FF, D), BF),
                pltpu.SemaphoreType.DMA((UNITS,)),
                pltpu.SemaphoreType.DMA((UNITS,)),
            ],
        ),
        compiler_params=params(58),
        cost_estimate=cost(30),
        name="fall",
    )(sc, first, act, slope, cotangent, small, u0, u1, d0, d1)


def place(acc_ref, keep_ref, send_ref, me, rows):
    for ref, sibling in ((keep_ref, False), (send_ref, True)):
        for position in range(CHIPS):
            unit = held(me, position, SCATTER, sibling)
            row = pl.multiple_of(unit * rows, 8)
            ref[position] = acc_ref[pl.ds(row, rows), :].astype(ref.dtype)


PLANE = 8
DOWN_ROWS = FF // 4


def down_kernel(sc, act_ref, g_ref, keep_ref, send_ref, acc_ref):
    acc_ref[...] = mm(act_ref[...], g_ref[...], TN)
    for ref, sibling in ((keep_ref, False), (send_ref, True)):
        for high in range(4):
            unit = held(sc[0], high * 4, SCATTER, sibling) & (PLANE - 1)
            row = pl.multiple_of(unit * FROWS, 8)
            ref[high, 0] = acc_ref[pl.ds(row, FROWS), :].astype(ref.dtype)


def down_call(sc, act, fgrad):
    def where(i, s):
        z = i ^ (s[0] // PLANE)
        return (0, (z & 1) * 2 + (z >> 1), 0, 0)

    out = pl.BlockSpec((4, 1, FROWS, D), where)
    keep, send = pl.pallas_call(
        down_kernel,
        out_shape=(
            jax.ShapeDtypeStruct((4, 4, FROWS, D), KEEP),
            jax.ShapeDtypeStruct((4, 4, FROWS, D), SEND),
        ),
        grid_spec=pltpu.PrefetchScalarGridSpec(
            num_scalar_prefetch=1,
            grid=(4,),
            in_specs=[
                pl.BlockSpec((LEN, DOWN_ROWS), lambda i, s: (0, i)),
                pl.BlockSpec((LEN, D), lambda i, s: (0, 0)),
            ],
            out_specs=[out, out],
            scratch_shapes=[pltpu.VMEM((DOWN_ROWS, D), F32)],
        ),
        compiler_params=params(24),
        cost_estimate=cost(14),
        name="down_term",
    )(sc, act, fgrad)
    return keep.reshape(CHIPS, FROWS, D), send.reshape(CHIPS, FROWS, D)


TILE = 768
OUT_TILES = D // TILE
UP_TILES = FF // TILE


def up_kernel(sc, ctx0_ref, ctx1_ref, ag_ref, nlow_ref, pg_ref, keep_ref, send_ref, acc_ref):
    tile = pl.program_id(0)

    @pl.when(tile < OUT_TILES)
    def _():
        acc_ref[:SPLIT, :] = mm(ctx0_ref[...], ag_ref[...], TN)
        acc_ref[SPLIT:, :] = mm(ctx1_ref[...], ag_ref[...], TN)

    @pl.when(tile >= OUT_TILES)
    def _():
        acc_ref[...] = mm(nlow_ref[...], pg_ref[...], TN)

    place(acc_ref, keep_ref, send_ref, sc[0], ROWS)


def up_call(sc, ctx0, ctx1, agrad, nlow, pgrad):
    out = pl.BlockSpec((16, ROWS, TILE), lambda i, s: (0, 0, i))
    cols = D + FF
    return pl.pallas_call(
        up_kernel,
        out_shape=(
            jax.ShapeDtypeStruct((16, ROWS, cols), KEEP),
            jax.ShapeDtypeStruct((16, ROWS, cols), SEND),
        ),
        grid_spec=pltpu.PrefetchScalarGridSpec(
            num_scalar_prefetch=1,
            grid=(OUT_TILES + UP_TILES,),
            in_specs=[
                pl.BlockSpec((LEN, SPLIT), lambda i, s: (0, 0)),
                pl.BlockSpec((LEN, ATT - SPLIT), lambda i, s: (0, 0)),
                pl.BlockSpec((LEN, TILE), lambda i, s: (0, jnp.minimum(i, OUT_TILES - 1))),
                pl.BlockSpec((LEN, D), lambda i, s: (0, 0)),
                pl.BlockSpec((LEN, TILE), lambda i, s: (0, jnp.maximum(i - OUT_TILES, 0))),
            ],
            out_specs=[out, out],
            scratch_shapes=[pltpu.VMEM((D, TILE), F32)],
        ),
        compiler_params=params(30),
        cost_estimate=cost(17),
        name="up_term",
    )(sc, ctx0, ctx1, agrad, nlow, pgrad)


def qterm_kernel(last, pieces, sc, x_ref, *rest):
    g_refs = rest[:pieces]
    sums_ref, usum_ref, qv_in_ref, *rest = rest[pieces:]
    if last:
        keep_ref, send_ref, acc_ref, qv_ref = rest
    else:
        keep_ref, send_ref, qv_ref, acc_ref = rest
    tile = pl.program_id(0)

    @pl.when(tile < 3)
    def _():
        x = x_ref[...]
        x = jnp.where(iota(x.shape, 1) < sc[1], x, jnp.zeros_like(x))
        g = jnp.concatenate([g_ref[0] for g_ref in g_refs], axis=1)
        acc_ref[...] = mm(x, g, TN)
        column = jnp.sum(g.astype(F32), axis=0, keepdims=True)
        for third in (0, 2):

            @pl.when(tile == third)
            def _():
                qv_ref[third // 2] = column

    if last:

        @pl.when(tile == 3)
        def _():
            high = lax.Precision.HIGHEST
            rows = sums_ref[...]
            pick = iota((8, D), 0)
            for k in range(2):
                row = jnp.concatenate([qv_in_ref[k], qv_ref[k]], axis=1)
                rows = jnp.where(pick == k, row, rows)
            shape = (UNITS, 8, D)
            start = iota(shape, 0) * ROWS
            lane = iota(shape, 2)
            mine = (lane >= start) & (lane < start + ROWS)
            wide = jnp.where(mine, rows[None], 0.0).reshape(UNITS * 8, D)
            small = mm(wide, spread(EXTRA, ROWS, D), NT, high).reshape(UNITS, 8, EXTRA)
            start = iota((UNITS, FF), 0) * FROWS
            lane = iota((UNITS, FF), 1)
            mine = (lane >= start) & (lane < start + FROWS)
            up = mm(jnp.where(mine, usum_ref[...], 0.0), spread(EXTRA, FROWS, FF), NT, high)
            acc_ref[...] = jnp.zeros_like(acc_ref)
            for unit in range(UNITS):
                acc_ref[unit * ROWS : unit * ROWS + 8, 0:EXTRA] = small[unit]
                acc_ref[unit * ROWS + 8 : unit * ROWS + 9, 0:EXTRA] = up[unit : unit + 1]

    place(acc_ref, keep_ref, send_ref, sc[0], ROWS)


def qterm_call(sc, hidden, grads, sums, usum, qv=None):
    last = qv is not None
    width = sum(g.shape[2] for g in grads)
    out = pl.BlockSpec((CHIPS, ROWS, width), lambda i, s: (0, 0, i))
    shape = jax.ShapeDtypeStruct((2, 1, width), F32)
    if not last:
        qv = jnp.zeros(shape.shape, F32)
    cols = width * (4 if last else 3)
    return pl.pallas_call(
        functools.partial(qterm_kernel, last, len(grads)),
        out_shape=(
            jax.ShapeDtypeStruct((CHIPS, ROWS, cols), KEEP),
            jax.ShapeDtypeStruct((CHIPS, ROWS, cols), SEND),
        )
        + (() if last else (shape,)),
        grid_spec=pltpu.PrefetchScalarGridSpec(
            num_scalar_prefetch=1,
            grid=(cols // width,),
            in_specs=[pl.BlockSpec((LEN, D), lambda i, s: (0, 0))]
            + [
                pl.BlockSpec((1, LEN, g.shape[2]), lambda i, s: (jnp.minimum(i, 2), 0, 0))
                for g in grads
            ]
            + [
                pl.BlockSpec((8, D), lambda i, s: (0, 0)),
                pl.BlockSpec((1, FF), lambda i, s: (0, 0)),
                whole_spec(*qv.shape),
            ],
            out_specs=[out, out] + ([] if last else [whole_spec(*shape.shape)]),
            scratch_shapes=[pltpu.VMEM((D, width), F32)]
            + ([pltpu.VMEM((2, 1, width), F32)] if last else []),
        ),
        compiler_params=params(30),
        cost_estimate=cost(7),
        name="qkv_term",
    )(sc, hidden, *grads, sums, usum, qv)


BWD_BLOCK = 256


def attend_back_kernel(
    first, sc, q_ref, k_ref, v_ref, do_ref, o_ref, e_ref, inv_ref, g_ref, dk_acc, dv_acc
):
    k = k_ref[...]
    v = v_ref[...]
    lane = iota((LEN, 128), 1)
    keys = [jnp.where((lane // HDIM) == h, k, jnp.zeros_like(k)) for h in range(2)]
    lane_q = iota((BWD_BLOCK, 128), 1)
    on = iota((1, 128), 1) + (first + pl.program_id(0)) * 128 < sc[2]
    for b in range(LEN // BWD_BLOCK):
        rows = slice(b * BWD_BLOCK, (b + 1) * BWD_BLOCK)
        q = q_ref[rows, :]
        do = (do_ref[rows, :].astype(F32) * inv_ref[rows, :]).astype(BF)
        both = do.astype(F32) * o_ref[rows, :].astype(F32)
        dq = None
        for h in range(2):
            mine = (lane_q // HDIM) == h
            doh = jnp.where(mine, do, jnp.zeros_like(do))
            qh = jnp.where(mine, q, jnp.zeros_like(q))
            delta = jnp.sum(jnp.where(mine, both, 0.0), axis=1, keepdims=True)
            dp = mm(doh, v, NT)
            e = e_ref[h, rows, :]
            ds = (e.astype(F32) * (dp - delta)).astype(BF)
            part = mm(ds, keys[h], NN)
            dq = part if dq is None else dq + part
            dk = mm(ds, qh, TN)
            dv = mm(e, doh, TN)
            if b == 0 and h == 0:
                dk_acc[...] = dk
                dv_acc[...] = dv
            else:
                dk_acc[...] += dk
                dv_acc[...] += dv
        g_ref[0, rows, :] = jnp.where(on, dq * HDIM ** (-0.5), 0.0).astype(BF)
    g_ref[1] = jnp.where(on, dk_acc[...], 0.0).astype(BF)
    g_ref[2] = jnp.where(on, dv_acc[...], 0.0).astype(BF)


def attend_back_call(sc, qkv, cgrad, part, skip, pairs):
    first, ctx, e, inv = part
    first += skip

    def spec(offset):
        return pl.BlockSpec((LEN, 128), lambda i, s: (0, offset + first + i))

    own = pl.BlockSpec((LEN, 128), lambda i, s: (0, skip + i))
    return pl.pallas_call(
        functools.partial(attend_back_kernel, first),
        out_shape=jax.ShapeDtypeStruct((3, LEN, pairs * 128), BF),
        grid_spec=pltpu.PrefetchScalarGridSpec(
            num_scalar_prefetch=1,
            grid=(pairs,),
            in_specs=[
                spec(0),
                spec(PAIRS),
                spec(2 * PAIRS),
                spec(0),
                own,
                pl.BlockSpec((2, LEN, LEN), lambda i, s: (skip + i, 0, 0)),
                own,
            ],
            out_specs=pl.BlockSpec((3, LEN, 128), lambda i, s: (0, 0, i)),
            scratch_shapes=[pltpu.VMEM((LEN, 128), F32)] * 2,
        ),
        compiler_params=params(28 if first < PARTS[0] else 40),
        cost_estimate=cost(6 * pairs),
        name="attend_back",
    )(sc, qkv, qkv, qkv, cgrad, ctx, e, inv)


def input_kernel(sc, *refs):
    *parts, own, other, first_ref, out_ref, w_ref, sem = refs

    @pl.when(pl.program_id(0) == 0)
    def _():
        copies = qkv_copies(sc[0], own, other, w_ref, sem)
        for copy in copies:
            copy.start()
        for copy in copies:
            copy.wait()

    total = first_ref[...]
    for third in range(3):
        grads = jnp.concatenate([g_ref[third] for g_ref in parts], axis=1)
        total = total + mm(grads, w_ref[:, third * ATT : (third + 1) * ATT], NT)
    on = iota((1, D), 1) < sc[1]
    out_ref[...] = jnp.where(on, 0.1 * total, 0.0).astype(BF)


def input_call(sc, parts, own, other, first_grad):
    block = 512
    return pl.pallas_call(
        input_kernel,
        out_shape=jax.ShapeDtypeStruct((LEN, D), BF),
        grid_spec=pltpu.PrefetchScalarGridSpec(
            num_scalar_prefetch=1,
            grid=(LEN // block,),
            in_specs=[
                pl.BlockSpec((3, block, g.shape[2]), lambda i, s: (0, i, 0)) for g in parts
            ]
            + [pl.BlockSpec(memory_space=pl.ANY)] * 2
            + [pl.BlockSpec((block, D), lambda i, s: (i, 0))],
            out_specs=pl.BlockSpec((block, D), lambda i, s: (i, 0)),
            scratch_shapes=[pltpu.VMEM((D, QCOLS), BF), pltpu.SemaphoreType.DMA((UNITS,))],
        ),
        compiler_params=params(20),
        cost_estimate=cost(9),
        name="input_grad",
    )(sc, *parts, own, other, first_grad)


def outputs_kernel(keep, r0, r1, r2, qkv_ref, qv_ref, gains_ref, biases_ref, upb_ref):
    total = keep[0]
    for r in (r0, r1, r2):
        total = total + r[0].astype(F32)
    col = 0
    for first, pairs in zip((0, PARTS[0]), PARTS):
        for third in range(3):
            to = third * ATT + first * 128
            qkv_ref[:, to : to + pairs * 128] = total[:, col : col + pairs * 128]
            col += pairs * 128
    extra = total[:, col : col + EXTRA]
    qv_ref[...] = extra[0:2, :ROWS]
    gains_ref[...] = extra[2:4, :ROWS]
    biases_ref[...] = extra[4:8, :ROWS]
    upb_ref[...] = extra[8:9, :FROWS]


def outputs_call(keep, recvs):
    return pl.pallas_call(
        outputs_kernel,
        out_shape=tuple(
            jax.ShapeDtypeStruct(shape, F32)
            for shape in ((ROWS, 3 * ATT), (2, ROWS), (2, ROWS), (4, ROWS), (1, FROWS))
        ),
        compiler_params=params(16),
        cost_estimate=cost(2),
        name="outputs",
    )(keep, *recvs)


def make_local(groups, members):
    fine = groups * members == UNITS
    axes = ("grp", "dp") if fine else ("grp",)

    def swap(x, even, odd=None):
        pair = (even, even if odd is None else odd)
        return lax.ppermute(x, axes, [(i, i ^ pair[i & 1]) for i in range(UNITS)])

    along_z = ((Z2, Z2), (Z1, Z1), (Z1 ^ Z2, Z1 ^ Z2))
    gather_hops = tuple((hop,) for hop in zip(*GATHER)) + (((CORE, CORE),),)
    scatter_hops = (
        (((CORE, CORE),),) + tuple((hop,) for hop in zip(*SCATTER))[:1:-1] + (along_z,)
    )

    class Gather:
        def __init__(self, x):
            self.state, self.stage = [x[None]], 0

        def start(self):
            self.recv = [swap(self.state[0], *hop) for hop in gather_hops[self.stage]]
            self.stage += 1

        def finish(self, *beside):
            if beside:
                self.recv = after(*self.recv, *beside)[: len(self.recv)]
            if self.stage == len(gather_hops):
                return self.state[0], self.recv[0]
            self.state = [jnp.concatenate([self.state[0], *self.recv], axis=0)]

    class Scatter:
        def __init__(self, keep, send):
            self.state, self.stage = [keep, send], 0

        def start(self):
            hops = scatter_hops[self.stage]
            self.recv = [swap(x, *hop) for x, hop in zip(self.state[1:], hops)]
            self.stage += 1

        def finish(self, *beside):
            if beside:
                self.recv = after(*self.recv, *beside)[: len(self.recv)]
            kept = self.state[0]
            if self.stage == len(scatter_hops):
                total = kept[0]
                for recv in self.recv:
                    total = total + recv[0].astype(F32)
                return total
            parts = len(scatter_hops[self.stage]) + 1
            n = kept.shape[0] // parts
            sums = [
                kept[p * n : (p + 1) * n].astype(F32) + self.recv[0][p * n : (p + 1) * n].astype(F32)
                for p in range(parts)
            ]
            self.state = sums[:1] + [x.astype(SEND) for x in sums[1:]]

    def tie(x, *movers):
        x, *flat = after(x, *(a for m in movers for a in m.state))
        for m in movers:
            m.state, flat = flat[: len(m.state)], flat[len(m.state) :]
        return x

    def local(
        hidden,
        lengths,
        subnet,
        qkv_weight,
        qv_bias,
        out_weight,
        up_weight,
        up_bias,
        down_weight,
        norm_gains,
        bias_rows,
        cotangent,
    ):
        group = lax.axis_index("grp")
        me = group * members + lax.axis_index("dp") if fine else group
        if not fine:
            qkv_weight, out_weight, up_weight, up_bias, down_weight = (
                lax.all_gather(w, "dp", axis=0, tiled=True)
                for w in (qkv_weight, out_weight, up_weight, up_bias, down_weight)
            )
            qv_bias, norm_gains, bias_rows = (
                lax.all_gather(w, "dp", axis=1, tiled=True)
                for w in (qv_bias, norm_gains, bias_rows)
            )
        picks = lax.dynamic_index_in_dim(subnet, group, 0, keepdims=False)
        width = D - (2 - picks[0]) * (D // 6)
        heads = HEADS - (2 - picks[1]) * (HEADS // 6)
        inner = width * (6 + picks[2]) // 2
        sc = jnp.stack([me.astype(jnp.int32), width, heads * HDIM, inner, lengths[0]])

        rows = jnp.concatenate([qv_bias, norm_gains, bias_rows], axis=0)
        extra = jnp.concatenate(
            [
                jnp.pad(rows, ((0, 0), (0, EXTRA - ROWS))),
                jnp.pad(up_bias[None], ((0, ROWS - 9), (0, EXTRA - FROWS))),
            ],
            axis=0,
        )
        side = me & 1

        def pair(shard, *beside):
            n = shard.shape[1] // 2
            mine = lax.dynamic_slice_in_dim(shard, side * n, n, 1)
            recv = swap(lax.dynamic_slice_in_dim(shard, (1 - side) * n, n, 1), CORE)
            ordered = [jnp.where(side == 0, mine, recv), jnp.where(side == 0, recv, mine)]
            return jnp.concatenate(ordered, axis=0)

        extra = jnp.pad(extra, ((0, 0), (0, EXTRA)))
        q = pair(jnp.concatenate([qkv_weight, extra], axis=1))
        half = PAIRS // 2
        q = Gather(q)
        q.start()
        q.finish()
        u = pair(jnp.concatenate([tie(out_weight, q), up_weight], axis=1))
        q.start()
        q.finish()
        u = Gather(tie(u, q))
        q.start()
        u.start()
        q.finish()
        u.finish()
        u.state = [tie(u.state[0], q)]
        q.start()
        u.start()
        q.finish()
        u.finish()
        u.state = [tie(u.state[0], q)]
        q.start()
        u.start()
        d = Gather(tie(down_weight, u))
        d.start()
        q0, q1 = q.finish()
        qkv, small, upb = qkv_call(sc, hidden, q0, q1)
        u.finish(small)
        d.finish(small)
        qkv = tie(qkv, u, d)
        u.start()
        d.start()
        ctx0, e0, inv0 = attend_call(sc, qkv, 0, PARTS[0])
        u.finish(inv0)
        d.finish(inv0)
        qkv = tie(qkv, u, d)
        u.start()
        d.start()
        ctx1, e1, inv1 = attend_call(sc, qkv, PARTS[0], PARTS[1])
        d.finish(inv1)
        ctx1 = tie(ctx1, d)
        d.start()
        u0, u1 = u.finish(inv1)
        first, nlow, act, slope = rise_call(sc, ctx0, ctx1, hidden, small, upb, u0, u1)
        d.finish(first)
        d.start()
        d0, d1 = d.finish()
        output, fgrad, pgrad, agrad, first_grad, cgrad, sums, usum = fall_call(
            sc, first, act, slope, cotangent, small, u0, u1, d0, d1
        )

        def step(beside, *movers):
            for m in movers:
                m.finish(beside)
                m.start()

        part0, part1 = (0, ctx0, e0, inv0), (PARTS[0], ctx1, e1, inv1)
        dn = Scatter(*down_call(sc, act, fgrad))
        dn.start()
        uk, us = up_call(sc, ctx0, ctx1, agrad, nlow, tie(pgrad, dn))
        up = Scatter(uk, us)
        step(uk, dn)
        up.start()
        g0 = attend_back_call(sc, qkv, tie(cgrad, dn, up), part0, 0, 2)
        step(g0, dn, up)
        g1 = attend_back_call(sc, qkv, tie(cgrad, dn, up), part0, 2, 2)
        step(g1, dn)
        qk, qs, qv = qterm_call(sc, hidden, (g0, tie(g1, dn)), sums, usum)
        qa = Scatter(qk, qs)
        step(qv, up)
        qa.start()
        g2 = attend_back_call(sc, qkv, tie(cgrad, qa, up), part1, 0, PARTS[1])
        step(g2, up, qa)
        down = dn.finish(g2)
        g2, down = after(tie(g2, up, qa), down)
        qk, qs = qterm_call(sc, hidden, (g2,), sums, usum, qv)
        qb = Scatter(qk, qs)
        qb.start()
        step(qk, qa)
        qb.finish(qa.state[1])
        qb.start()
        grad_hidden = input_call(sc, (g0, g1, g2), q0, q1, tie(first_grad, qb, qa))
        step(grad_hidden, qb)
        qa.finish(qb.state[1])
        up = up.finish(qa.state[1])
        qb.finish()
        both = Scatter(None, None)
        both.state = [jnp.concatenate(x, axis=2) for x in zip(qa.state, qb.state)]
        both.state[0], up = after(both.state[0], up)
        both.stage = qa.stage
        both.start()
        qkv_sum, qv_sum, gains_sum, biases_sum, upb_sum = outputs_call(both.state[0], both.recv)
        grads = (
            qkv_sum,
            qv_sum,
            up[:, :D],
            up[:, D:],
            upb_sum.reshape(FROWS),
            down,
            gains_sum,
            biases_sum,
        )
        if not fine:
            dims = (0, 1, 0, 0, 0, 0, 1, 1)
            grads = tuple(
                lax.psum_scatter(g, "dp", scatter_dimension=d, tiled=True)
                for g, d in zip(grads, dims)
            )
        return (output, grad_hidden) + grads

    return local


def solution(mesh):
    both = ("grp", "dp")
    row, col, flat = P(both, None), P(None, both), P(both)
    placed = (row, flat, P(), row, col, row, row, flat, row, col, col, row)
    return jax.shard_map(
        make_local(mesh.shape["grp"], mesh.shape["dp"]),
        mesh=mesh,
        in_specs=placed,
        out_specs=(row, row, row, col, row, row, flat, row, col, col),
        check_vma=False,
    )
```

```python
import functools

import jax
import jax.numpy as jnp
from jax import lax
from jax.experimental import pallas as pl
from jax.experimental.pallas import tpu as pltpu
from jax.sharding import PartitionSpec as P

D = 768
HEADS = 12
HDIM = 64
FF = 3072
LEN = 1024
ATT = 768
PAIRS = HEADS // 2
PARTS = (4, 2)
SPLIT = PARTS[0] * 128

EPSILON = 1e-05
NEGATIVE = -1e30

UNITS = 32
ROWS = D // UNITS
FROWS = FF // UNITS
PAIR = 2 * ROWS
CHIPS = UNITS // 2
EXTRA = 128
QCOLS = 3 * ATT + 2 * EXTRA
UCOLS = D + FF

BF = jnp.bfloat16
F32 = jnp.float32
SEND = jnp.bfloat16
KEEP = jnp.bfloat16

NN = (((1,), (0,)), ((), ()))
NT = (((1,), (1,)), ((), ()))
TN = (((0,), (0,)), ((), ()))

CORE, AX, AY, Z1, Z2 = 1, 2, 4, 8, 16


def mm(a, b, dims, precision=None):
    return lax.dot_general(a, b, dims, precision=precision, preferred_element_type=F32)


def params(megabytes):
    return pltpu.CompilerParams(vmem_limit_bytes=megabytes << 20)


def cost(micros):
    return pl.CostEstimate(
        flops=int(micros * 1.1e9), transcendentals=0, bytes_accessed=int(micros * 1e6)
    )


def owner(position, masks):
    offset = 0
    for bit, mask in enumerate(masks):
        if (position >> bit) & 1:
            offset ^= mask
    return offset


GATHER = ((Z2, Z1, AX, AY), (Z2, Z1, AY, AX))
SCATTER = ((Z2, Z1, AY, AX), (Z2, Z1, AX, AY))


def held(me, position, orders, sibling=False):
    even, odd = owner(position, orders[0]), owner(position, orders[1])
    parity = me & 1
    if sibling:
        me, parity = me ^ CORE, 1 - parity
    return me ^ jnp.where(parity == 0, even, odd)


def after(x, *others):
    return lax.optimization_barrier((x,) + others)


def iota(shape, axis):
    return lax.broadcasted_iota(jnp.int32, shape, axis)


def spread(width, period, columns):
    col = iota((width, columns), 1)
    turn = jnp.floor((col.astype(F32) + 0.5) * (1.0 / period)).astype(jnp.int32)
    return jnp.where(col - turn * period == iota((width, columns), 0), 1.0, 0.0)


QKV_BLOCK = 512


def qkv_copies(me, own, other, w_ref, sem):
    copies = []
    half = QCOLS // 2
    for source, sibling in ((own, False), (other, True)):
        side = (me & 1) ^ 1 if sibling else me & 1
        col = pl.multiple_of(side * half, 128)
        for position in range(CHIPS):
            chip = held(me, position, GATHER, sibling) >> 1
            row = pl.multiple_of(chip * PAIR, 16)
            copies.append(
                pltpu.make_async_copy(
                    source.at[position],
                    w_ref.at[pl.ds(row, PAIR), pl.ds(col, half)],
                    sem.at[len(copies)],
                )
            )
    return copies


def qkv_kernel(sc, x_ref, own, other, qkv_ref, small_ref, upb_ref, w_ref, sem):
    me, width, att = sc[0], sc[1], sc[2]

    @pl.when(pl.program_id(0) == 0)
    def _():
        copies = qkv_copies(me, own, other, w_ref, sem)
        for copy in copies:
            copy.start()
        for copy in copies:
            copy.wait()
        extra = w_ref[:, 3 * ATT : 3 * ATT + EXTRA]
        wide = mm(extra, spread(EXTRA, ROWS, D).astype(BF), NN).reshape(UNITS, ROWS, D)
        shape = (UNITS, ROWS, D)
        start = iota(shape, 0) * ROWS
        lane = iota(shape, 2)
        mine = (lane >= start) & (lane < start + ROWS)
        small_ref[...] = jnp.sum(jnp.where(mine, wide, 0.0), axis=0)
        row8 = extra.reshape(UNITS, ROWS, EXTRA)[:, 8, :]
        wide = mm(row8, spread(EXTRA, FROWS, FF).astype(BF), NN)
        start = iota((UNITS, FF), 0) * FROWS
        lane = iota((UNITS, FF), 1)
        mine = (lane >= start) & (lane < start + FROWS)
        upb_ref[...] = jnp.sum(jnp.where(mine, wide, 0.0), axis=0, keepdims=True)

    x = x_ref[...]
    x = jnp.where(iota(x.shape, 1) < width, x, jnp.zeros_like(x))
    on = iota((1, ATT), 1) < att
    for third in range(3):
        part = mm(x, w_ref[:, third * ATT : (third + 1) * ATT], NN)
        if third == 0:
            part = part + small_ref[0:1, :]
        if third == 2:
            part = part + small_ref[1:2, :]
        part = jnp.where(on, part, 0.0).astype(BF)
        if third == 0:
            part = part * jnp.asarray(HDIM ** (-0.5), BF)
        qkv_ref[:, third * ATT : (third + 1) * ATT] = part


def qkv_call(sc, hidden, own, other):
    hbm = pl.BlockSpec(memory_space=pl.ANY)
    return pl.pallas_call(
        qkv_kernel,
        out_shape=(
            jax.ShapeDtypeStruct((LEN, 3 * ATT), BF),
            jax.ShapeDtypeStruct((ROWS, D), F32),
            jax.ShapeDtypeStruct((1, FF), F32),
        ),
        grid_spec=pltpu.PrefetchScalarGridSpec(
            num_scalar_prefetch=1,
            grid=(LEN // QKV_BLOCK,),
            in_specs=[pl.BlockSpec((QKV_BLOCK, D), lambda i, s: (i, 0)), hbm, hbm],
            out_specs=[
                pl.BlockSpec((QKV_BLOCK, 3 * ATT), lambda i, s: (i, 0)),
                pl.BlockSpec((ROWS, D), lambda i, s: (0, 0)),
                pl.BlockSpec((1, FF), lambda i, s: (0, 0)),
            ],
            scratch_shapes=[pltpu.VMEM((D, QCOLS), BF), pltpu.SemaphoreType.DMA((UNITS,))],
        ),
        compiler_params=params(24),
        cost_estimate=cost(10),
        name="qkv",
    )(sc, hidden, own, other)


FWD_BLOCK = 512


def attend_kernel(sc, q_ref, k_ref, v_ref, o_ref, e_ref, inv_ref):
    length = sc[4]
    half = LEN // 2
    lane = iota((LEN, 128), 1)
    edge = jnp.where(iota((1, half), 1) + half < length, 0.0, NEGATIVE)
    k = k_ref[...]
    v = v_ref[...]
    heads = []
    for h in range(2):
        mine = (lane // HDIM) == h
        heads.append(
            (jnp.where(mine, k, jnp.zeros_like(k)), jnp.where(mine, v, jnp.ones_like(v)))
        )
    left = iota((FWD_BLOCK, 128), 1) < HDIM
    for b in range(LEN // FWD_BLOCK):
        rows = slice(b * FWD_BLOCK, (b + 1) * FWD_BLOCK)
        q = q_ref[rows, :]
        outs, invs = [], []
        for h in range(2):
            keys, values = heads[h]
            scores = mm(q, keys, NT)
            sa = scores[:, :half]
            sb = scores[:, half:] + edge
            top = jnp.maximum(
                jnp.max(sa, axis=1, keepdims=True), jnp.max(sb, axis=1, keepdims=True)
            )
            ea = jnp.exp(sa - top).astype(BF)
            eb = jnp.exp(sb - top).astype(BF)
            e_ref[h, rows, :half] = ea
            e_ref[h, rows, half:] = eb
            o = mm(ea, values[:half], NN) + mm(eb, values[half:], NN)
            inv = 1.0 / pltpu.roll(o, HDIM, 1)
            outs.append(o * inv)
            invs.append(inv)
        o_ref[rows, :] = jnp.where(left, outs[0], outs[1]).astype(BF)
        inv_ref[rows, :] = jnp.where(left, invs[0], invs[1])


def attend_call(sc, qkv, first, pairs):
    def spec(offset):
        return pl.BlockSpec((LEN, 128), lambda i, s: (0, offset + first + i))

    out = pl.BlockSpec((LEN, 128), lambda i, s: (0, i))

    return pl.pallas_call(
        attend_kernel,
        out_shape=(
            jax.ShapeDtypeStruct((LEN, pairs * 128), BF),
            jax.ShapeDtypeStruct((2 * pairs, LEN, LEN), BF),
            jax.ShapeDtypeStruct((LEN, pairs * 128), F32),
        ),
        grid_spec=pltpu.PrefetchScalarGridSpec(
            num_scalar_prefetch=1,
            grid=(pairs,),
            in_specs=[spec(0), spec(PAIRS), spec(2 * PAIRS)],
            out_specs=[out, pl.BlockSpec((2, LEN, LEN), lambda i, s: (i, 0, 0)), out],
        ),
        compiler_params=params(56),
        cost_estimate=cost(4 * pairs),
        name="attend",
    )(sc, qkv, qkv, qkv)


CHAIN_BLOCK = 256
CHUNK = 768


def normal_parts(x):
    t = 1.0 / (jnp.abs(x) + 4.317008465)
    gauss = jnp.exp2((x * x) * -0.7213475204444817)
    poly = t * (
        0.5500507529
        + t * (-2.651020542 + t * (57.17935007 + t * (-252.3554320 + t * 795.7301438)))
    )
    tail = poly * gauss
    return jnp.where(x >= 0, 1.0 - tail, tail), gauss * 0.3989422804014327


def normalise(v, cm, count):
    mean = jnp.sum(v, axis=1, keepdims=True) / count
    centred = (v - mean) * cm
    var = jnp.sum(centred * centred, axis=1, keepdims=True) / count
    r = lax.rsqrt(var + EPSILON)
    return centred * r, r


def normalise_back(e, yhat, r, gain, cm, count):
    t = e * gain * cm
    s1 = jnp.sum(t, axis=1, keepdims=True) / count
    s2 = jnp.sum(t * yhat, axis=1, keepdims=True) / count
    return r * cm * (t - s1 - yhat * s2)


def width_mask(width):
    return jnp.where(iota((1, D), 1) < width, 1.0, 0.0)


def column_sum(x):
    return jnp.sum(x.astype(F32), axis=0, keepdims=True)


def up_copies(me, own, other, w_ref, sem):
    copies = []
    half = UCOLS // 2
    for source, sibling in ((own, False), (other, True)):
        side = (me & 1) ^ 1 if sibling else me & 1
        col = pl.multiple_of(side * half, 128)
        for position in range(CHIPS):
            chip = held(me, position, GATHER, sibling) >> 1
            row = pl.multiple_of(chip * PAIR, 16)
            copies.append(
                pltpu.make_async_copy(
                    source.at[position],
                    w_ref.at[pl.ds(row, PAIR), pl.ds(col, half)],
                    sem.at[len(copies)],
                )
            )
    return copies


def down_copies(me, own, other, w_ref, sem):
    copies = []
    for source, sibling in ((own, False), (other, True)):
        for position in range(CHIPS):
            unit = held(me, position, GATHER, sibling)
            row = pl.multiple_of(unit * FROWS, 16)
            copies.append(
                pltpu.make_async_copy(
                    source.at[position],
                    w_ref.at[pl.ds(row, FROWS), :],
                    sem.at[len(copies)],
                )
            )
    return copies


def rise_kernel(
    sc,
    ctx0_ref,
    ctx1_ref,
    hid_ref,
    small_ref,
    upb_ref,
    u0,
    u1,
    first_ref,
    nlow_ref,
    act_ref,
    slope_ref,
    wu_ref,
    sem,
):
    me, width, inner = sc[0], sc[1], sc[3]

    @pl.when(pl.program_id(0) == 0)
    def _():
        copies = up_copies(me, u0, u1, wu_ref, sem)
        for copy in copies:
            copy.start()
        for copy in copies:
            copy.wait()

    cm = width_mask(width)
    gain1, bias0, shift1 = small_ref[2:3, :], small_ref[4:5, :], small_ref[5:6, :]
    x = hid_ref[...].astype(F32) * cm
    projected = mm(ctx0_ref[...], wu_ref[:SPLIT, :D], NN) + mm(
        ctx1_ref[...], wu_ref[SPLIT:, :D], NN
    )
    first = x + (projected + bias0) * cm
    first_ref[...] = first
    yhat, _ = normalise(first, cm, width.astype(F32))
    nlow = ((yhat * gain1 + shift1) * cm).astype(BF)
    nlow_ref[...] = nlow
    for j in range(FF // CHUNK):
        cols = slice(j * CHUNK, (j + 1) * CHUNK)
        up_cols = slice(D + j * CHUNK, D + (j + 1) * CHUNK)
        fm = jnp.where(iota((1, CHUNK), 1) + j * CHUNK < inner, 1.0, 0.0)
        pre = (mm(nlow, wu_ref[:, up_cols], NN) + upb_ref[:, cols]) * fm
        cdf, pdf = normal_parts(pre)
        act_ref[:, cols] = (pre * cdf).astype(BF)
        slope_ref[:, cols] = (cdf + pre * pdf).astype(BF)


def row_spec(cols):
    return pl.BlockSpec((CHAIN_BLOCK, cols), lambda i, s: (i, 0))


def whole_spec(*shape):
    return pl.BlockSpec(shape, lambda i, s: (0,) * len(shape))


def row_shape(cols, dtype=BF):
    return jax.ShapeDtypeStruct((LEN, cols), dtype)


def rise_call(sc, ctx0, ctx1, hidden, small, upb, u0, u1):
    hbm = pl.BlockSpec(memory_space=pl.ANY)
    return pl.pallas_call(
        rise_kernel,
        out_shape=(
            row_shape(D, F32),
            row_shape(D),
            row_shape(FF),
            row_shape(FF),
        ),
        grid_spec=pltpu.PrefetchScalarGridSpec(
            num_scalar_prefetch=1,
            grid=(LEN // CHAIN_BLOCK,),
            in_specs=[row_spec(SPLIT), row_spec(ATT - SPLIT)]
            + [row_spec(D), whole_spec(ROWS, D), whole_spec(1, FF), hbm, hbm],
            out_specs=[
                row_spec(D),
                row_spec(D),
                row_spec(FF),
                row_spec(FF),
            ],
            scratch_shapes=[pltpu.VMEM((D, UCOLS), BF), pltpu.SemaphoreType.DMA((UNITS,))],
        ),
        compiler_params=params(44),
        cost_estimate=cost(18),
        name="rise",
    )(sc, ctx0, ctx1, hidden, small, upb, u0, u1)


def fall_kernel(
    sc,
    first_ref,
    act_ref,
    slope_ref,
    cot_ref,
    small_ref,
    u0,
    u1,
    d0,
    d1,
    out_ref,
    fgrad_ref,
    pgrad_ref,
    agrad_ref,
    igrad_ref,
    cgrad_ref,
    sums_ref,
    usum_ref,
    wu_ref,
    wd_ref,
    usem,
    dsem,
):
    me, width, inner, length = sc[0], sc[1], sc[3], sc[4]
    step = pl.program_id(0)

    @pl.when(step == 0)
    def _():
        down = down_copies(me, d0, d1, wd_ref, dsem)
        for copy in down + up_copies(me, u0, u1, wu_ref, usem):
            copy.start()
        sums_ref[...] = jnp.zeros_like(sums_ref)
        usum_ref[...] = jnp.zeros_like(usum_ref)
        for copy in down:
            copy.wait()

    cm = width_mask(width)
    count = width.astype(F32)
    rowpos = step * CHAIN_BLOCK + iota((CHAIN_BLOCK, 1), 0)
    rm = jnp.where(rowpos < length, 1.0, 0.0)
    gain1, gain2 = small_ref[2:3, :], small_ref[3:4, :]
    shift1, bias2, shift3 = small_ref[5:6, :], small_ref[6:7, :], small_ref[7:8, :]

    yhat1, r1 = normalise(first_ref[...], cm, count)
    normed1 = (yhat1 * gain1 + shift1) * cm
    second = normed1 + (mm(act_ref[...], wd_ref[...], NN) + bias2) * cm
    yhat2, r2 = normalise(second, cm, count)
    out_ref[...] = ((yhat2 * gain2 + shift3) * cm * rm).astype(BF)
    e2 = cot_ref[...].astype(F32) * rm
    sums_ref[3:4, :] += column_sum(e2 * yhat2)
    sums_ref[7:8, :] += column_sum(e2 * cm)
    second_grad = normalise_back(e2, yhat2, r2, gain2, cm, count)
    fgrad = second_grad.astype(BF)
    fgrad_ref[...] = fgrad
    sums_ref[6:7, :] += column_sum(fgrad)
    @pl.when(step == 0)
    def _():
        for copy in up_copies(me, u0, u1, wu_ref, usem):
            copy.wait()

    total = second_grad
    for j in range(FF // CHUNK):
        cols = slice(j * CHUNK, (j + 1) * CHUNK)
        up_cols = slice(D + j * CHUNK, D + (j + 1) * CHUNK)
        fm = jnp.where(iota((1, CHUNK), 1) + j * CHUNK < inner, 1.0, 0.0).astype(BF)
        slope = (slope_ref[:, cols] * fm).astype(F32)
        pgrad = (mm(fgrad, wd_ref[cols, :], NT) * slope).astype(BF)
        pgrad_ref[:, cols] = pgrad
        usum_ref[:, cols] += column_sum(pgrad)
        total = total + mm(pgrad, wu_ref[:, up_cols], NT)
    sums_ref[2:3, :] += column_sum(total * yhat1)
    sums_ref[5:6, :] += column_sum(total * cm)
    first_grad = normalise_back(total, yhat1, r1, gain1, cm, count)
    igrad_ref[...] = first_grad
    agrad = first_grad.astype(BF)
    agrad_ref[...] = agrad
    sums_ref[4:5, :] += column_sum(agrad)
    cgrad_ref[...] = mm(agrad, wu_ref[:, :D], NT).astype(BF)


def fall_call(sc, first, act, slope, cotangent, small, u0, u1, d0, d1):
    hbm = pl.BlockSpec(memory_space=pl.ANY)
    return pl.pallas_call(
        fall_kernel,
        out_shape=(
            row_shape(D),
            row_shape(D),
            row_shape(FF),
            row_shape(D),
            row_shape(D, F32),
            row_shape(ATT),
            jax.ShapeDtypeStruct((8, D), F32),
            jax.ShapeDtypeStruct((1, FF), F32),
        ),
        grid_spec=pltpu.PrefetchScalarGridSpec(
            num_scalar_prefetch=1,
            grid=(LEN // CHAIN_BLOCK,),
            in_specs=[
                row_spec(D),
                row_spec(FF),
                row_spec(FF),
                row_spec(D),
                whole_spec(ROWS, D),
                hbm,
                hbm,
                hbm,
                hbm,
            ],
            out_specs=[
                row_spec(D),
                row_spec(D),
                row_spec(FF),
                row_spec(D),
                row_spec(D),
                row_spec(ATT),
                whole_spec(8, D),
                whole_spec(1, FF),
            ],
            scratch_shapes=[
                pltpu.VMEM((D, UCOLS), BF),
                pltpu.VMEM((FF, D), BF),
                pltpu.SemaphoreType.DMA((UNITS,)),
                pltpu.SemaphoreType.DMA((UNITS,)),
            ],
        ),
        compiler_params=params(58),
        cost_estimate=cost(30),
        name="fall",
    )(sc, first, act, slope, cotangent, small, u0, u1, d0, d1)


def place(acc_ref, keep_ref, send_ref, me, rows):
    for ref, sibling in ((keep_ref, False), (send_ref, True)):
        for position in range(CHIPS):
            unit = held(me, position, SCATTER, sibling)
            row = pl.multiple_of(unit * rows, 8)
            ref[position] = acc_ref[pl.ds(row, rows), :].astype(ref.dtype)


PLANE = 8
DOWN_ROWS = FF // 4


def down_kernel(sc, act_ref, g_ref, keep_ref, send_ref, acc_ref):
    acc_ref[...] = mm(act_ref[...], g_ref[...], TN)
    for ref, sibling in ((keep_ref, False), (send_ref, True)):
        for high in range(4):
            unit = held(sc[0], high * 4, SCATTER, sibling) & (PLANE - 1)
            row = pl.multiple_of(unit * FROWS, 8)
            ref[high, 0] = acc_ref[pl.ds(row, FROWS), :].astype(ref.dtype)


def down_call(sc, act, fgrad):
    def where(i, s):
        z = i ^ (s[0] // PLANE)
        return (0, (z & 1) * 2 + (z >> 1), 0, 0)

    out = pl.BlockSpec((4, 1, FROWS, D), where)
    keep, send = pl.pallas_call(
        down_kernel,
        out_shape=(
            jax.ShapeDtypeStruct((4, 4, FROWS, D), KEEP),
            jax.ShapeDtypeStruct((4, 4, FROWS, D), SEND),
        ),
        grid_spec=pltpu.PrefetchScalarGridSpec(
            num_scalar_prefetch=1,
            grid=(4,),
            in_specs=[
                pl.BlockSpec((LEN, DOWN_ROWS), lambda i, s: (0, i)),
                pl.BlockSpec((LEN, D), lambda i, s: (0, 0)),
            ],
            out_specs=[out, out],
            scratch_shapes=[pltpu.VMEM((DOWN_ROWS, D), F32)],
        ),
        compiler_params=params(24),
        cost_estimate=cost(14),
        name="down_term",
    )(sc, act, fgrad)
    return keep.reshape(CHIPS, FROWS, D), send.reshape(CHIPS, FROWS, D)


TILE = 768
OUT_TILES = D // TILE
UP_TILES = FF // TILE


def up_kernel(sc, ctx0_ref, ctx1_ref, ag_ref, nlow_ref, pg_ref, keep_ref, send_ref, acc_ref):
    tile = pl.program_id(0)

    @pl.when(tile < OUT_TILES)
    def _():
        acc_ref[:SPLIT, :] = mm(ctx0_ref[...], ag_ref[...], TN)
        acc_ref[SPLIT:, :] = mm(ctx1_ref[...], ag_ref[...], TN)

    @pl.when(tile >= OUT_TILES)
    def _():
        acc_ref[...] = mm(nlow_ref[...], pg_ref[...], TN)

    place(acc_ref, keep_ref, send_ref, sc[0], ROWS)


def up_call(sc, ctx0, ctx1, agrad, nlow, pgrad):
    out = pl.BlockSpec((16, ROWS, TILE), lambda i, s: (0, 0, i))
    cols = D + FF
    return pl.pallas_call(
        up_kernel,
        out_shape=(
            jax.ShapeDtypeStruct((16, ROWS, cols), KEEP),
            jax.ShapeDtypeStruct((16, ROWS, cols), SEND),
        ),
        grid_spec=pltpu.PrefetchScalarGridSpec(
            num_scalar_prefetch=1,
            grid=(OUT_TILES + UP_TILES,),
            in_specs=[
                pl.BlockSpec((LEN, SPLIT), lambda i, s: (0, 0)),
                pl.BlockSpec((LEN, ATT - SPLIT), lambda i, s: (0, 0)),
                pl.BlockSpec((LEN, TILE), lambda i, s: (0, jnp.minimum(i, OUT_TILES - 1))),
                pl.BlockSpec((LEN, D), lambda i, s: (0, 0)),
                pl.BlockSpec((LEN, TILE), lambda i, s: (0, jnp.maximum(i - OUT_TILES, 0))),
            ],
            out_specs=[out, out],
            scratch_shapes=[pltpu.VMEM((D, TILE), F32)],
        ),
        compiler_params=params(30),
        cost_estimate=cost(17),
        name="up_term",
    )(sc, ctx0, ctx1, agrad, nlow, pgrad)


def qterm_kernel(last, pieces, sc, x_ref, *rest):
    g_refs = rest[:pieces]
    sums_ref, usum_ref, qv_in_ref, *rest = rest[pieces:]
    if last:
        keep_ref, send_ref, acc_ref, qv_ref = rest
    else:
        keep_ref, send_ref, qv_ref, acc_ref = rest
    tile = pl.program_id(0)

    @pl.when(tile < 3)
    def _():
        x = x_ref[...]
        x = jnp.where(iota(x.shape, 1) < sc[1], x, jnp.zeros_like(x))
        g = jnp.concatenate([g_ref[0] for g_ref in g_refs], axis=1)
        acc_ref[...] = mm(x, g, TN)
        column = jnp.sum(g.astype(F32), axis=0, keepdims=True)
        for third in (0, 2):

            @pl.when(tile == third)
            def _():
                qv_ref[third // 2] = column

    if last:

        @pl.when(tile == 3)
        def _():
            high = lax.Precision.HIGHEST
            rows = sums_ref[...]
            pick = iota((8, D), 0)
            for k in range(2):
                row = jnp.concatenate([qv_in_ref[k], qv_ref[k]], axis=1)
                rows = jnp.where(pick == k, row, rows)
            shape = (UNITS, 8, D)
            start = iota(shape, 0) * ROWS
            lane = iota(shape, 2)
            mine = (lane >= start) & (lane < start + ROWS)
            wide = jnp.where(mine, rows[None], 0.0).reshape(UNITS * 8, D)
            small = mm(wide, spread(EXTRA, ROWS, D), NT, high).reshape(UNITS, 8, EXTRA)
            start = iota((UNITS, FF), 0) * FROWS
            lane = iota((UNITS, FF), 1)
            mine = (lane >= start) & (lane < start + FROWS)
            up = mm(jnp.where(mine, usum_ref[...], 0.0), spread(EXTRA, FROWS, FF), NT, high)
            acc_ref[...] = jnp.zeros_like(acc_ref)
            for unit in range(UNITS):
                acc_ref[unit * ROWS : unit * ROWS + 8, 0:EXTRA] = small[unit]
                acc_ref[unit * ROWS + 8 : unit * ROWS + 9, 0:EXTRA] = up[unit : unit + 1]

    place(acc_ref, keep_ref, send_ref, sc[0], ROWS)


def qterm_call(sc, hidden, grads, sums, usum, qv=None):
    last = qv is not None
    width = sum(g.shape[2] for g in grads)
    out = pl.BlockSpec((CHIPS, ROWS, width), lambda i, s: (0, 0, i))
    shape = jax.ShapeDtypeStruct((2, 1, width), F32)
    if not last:
        qv = jnp.zeros(shape.shape, F32)
    cols = width * (4 if last else 3)
    return pl.pallas_call(
        functools.partial(qterm_kernel, last, len(grads)),
        out_shape=(
            jax.ShapeDtypeStruct((CHIPS, ROWS, cols), KEEP),
            jax.ShapeDtypeStruct((CHIPS, ROWS, cols), SEND),
        )
        + (() if last else (shape,)),
        grid_spec=pltpu.PrefetchScalarGridSpec(
            num_scalar_prefetch=1,
            grid=(cols // width,),
            in_specs=[pl.BlockSpec((LEN, D), lambda i, s: (0, 0))]
            + [
                pl.BlockSpec((1, LEN, g.shape[2]), lambda i, s: (jnp.minimum(i, 2), 0, 0))
                for g in grads
            ]
            + [
                pl.BlockSpec((8, D), lambda i, s: (0, 0)),
                pl.BlockSpec((1, FF), lambda i, s: (0, 0)),
                whole_spec(*qv.shape),
            ],
            out_specs=[out, out] + ([] if last else [whole_spec(*shape.shape)]),
            scratch_shapes=[pltpu.VMEM((D, width), F32)]
            + ([pltpu.VMEM((2, 1, width), F32)] if last else []),
        ),
        compiler_params=params(30),
        cost_estimate=cost(7),
        name="qkv_term",
    )(sc, hidden, *grads, sums, usum, qv)


BWD_BLOCK = 256


def attend_back_kernel(
    first, sc, q_ref, k_ref, v_ref, do_ref, o_ref, e_ref, inv_ref, g_ref, dk_acc, dv_acc
):
    k = k_ref[...]
    v = v_ref[...]
    lane = iota((LEN, 128), 1)
    keys = [jnp.where((lane // HDIM) == h, k, jnp.zeros_like(k)) for h in range(2)]
    lane_q = iota((BWD_BLOCK, 128), 1)
    on = iota((1, 128), 1) + (first + pl.program_id(0)) * 128 < sc[2]
    for b in range(LEN // BWD_BLOCK):
        rows = slice(b * BWD_BLOCK, (b + 1) * BWD_BLOCK)
        q = q_ref[rows, :]
        do = (do_ref[rows, :].astype(F32) * inv_ref[rows, :]).astype(BF)
        both = do.astype(F32) * o_ref[rows, :].astype(F32)
        dq = None
        for h in range(2):
            mine = (lane_q // HDIM) == h
            doh = jnp.where(mine, do, jnp.zeros_like(do))
            qh = jnp.where(mine, q, jnp.zeros_like(q))
            delta = jnp.sum(jnp.where(mine, both, 0.0), axis=1, keepdims=True)
            dp = mm(doh, v, NT)
            e = e_ref[h, rows, :]
            ds = (e.astype(F32) * (dp - delta)).astype(BF)
            part = mm(ds, keys[h], NN)
            dq = part if dq is None else dq + part
            dk = mm(ds, qh, TN)
            dv = mm(e, doh, TN)
            if b == 0 and h == 0:
                dk_acc[...] = dk
                dv_acc[...] = dv
            else:
                dk_acc[...] += dk
                dv_acc[...] += dv
        g_ref[0, rows, :] = jnp.where(on, dq * HDIM ** (-0.5), 0.0).astype(BF)
    g_ref[1] = jnp.where(on, dk_acc[...], 0.0).astype(BF)
    g_ref[2] = jnp.where(on, dv_acc[...], 0.0).astype(BF)


def attend_back_call(sc, qkv, cgrad, part, skip, pairs):
    first, ctx, e, inv = part
    first += skip

    def spec(offset):
        return pl.BlockSpec((LEN, 128), lambda i, s: (0, offset + first + i))

    own = pl.BlockSpec((LEN, 128), lambda i, s: (0, skip + i))
    return pl.pallas_call(
        functools.partial(attend_back_kernel, first),
        out_shape=jax.ShapeDtypeStruct((3, LEN, pairs * 128), BF),
        grid_spec=pltpu.PrefetchScalarGridSpec(
            num_scalar_prefetch=1,
            grid=(pairs,),
            in_specs=[
                spec(0),
                spec(PAIRS),
                spec(2 * PAIRS),
                spec(0),
                own,
                pl.BlockSpec((2, LEN, LEN), lambda i, s: (skip + i, 0, 0)),
                own,
            ],
            out_specs=pl.BlockSpec((3, LEN, 128), lambda i, s: (0, 0, i)),
            scratch_shapes=[pltpu.VMEM((LEN, 128), F32)] * 2,
        ),
        compiler_params=params(28 if first < PARTS[0] else 40),
        cost_estimate=cost(6 * pairs),
        name="attend_back",
    )(sc, qkv, qkv, qkv, cgrad, ctx, e, inv)


def input_kernel(sc, *refs):
    *parts, own, other, first_ref, out_ref, w_ref, sem = refs

    @pl.when(pl.program_id(0) == 0)
    def _():
        copies = qkv_copies(sc[0], own, other, w_ref, sem)
        for copy in copies:
            copy.start()
        for copy in copies:
            copy.wait()

    total = first_ref[...]
    for third in range(3):
        grads = jnp.concatenate([g_ref[third] for g_ref in parts], axis=1)
        total = total + mm(grads, w_ref[:, third * ATT : (third + 1) * ATT], NT)
    on = iota((1, D), 1) < sc[1]
    out_ref[...] = jnp.where(on, 0.1 * total, 0.0).astype(BF)


def input_call(sc, parts, own, other, first_grad):
    block = 512
    return pl.pallas_call(
        input_kernel,
        out_shape=jax.ShapeDtypeStruct((LEN, D), BF),
        grid_spec=pltpu.PrefetchScalarGridSpec(
            num_scalar_prefetch=1,
            grid=(LEN // block,),
            in_specs=[
                pl.BlockSpec((3, block, g.shape[2]), lambda i, s: (0, i, 0)) for g in parts
            ]
            + [pl.BlockSpec(memory_space=pl.ANY)] * 2
            + [pl.BlockSpec((block, D), lambda i, s: (i, 0))],
            out_specs=pl.BlockSpec((block, D), lambda i, s: (i, 0)),
            scratch_shapes=[pltpu.VMEM((D, QCOLS), BF), pltpu.SemaphoreType.DMA((UNITS,))],
        ),
        compiler_params=params(30),
        cost_estimate=cost(9),
        name="input_grad",
    )(sc, *parts, own, other, first_grad)


def outputs_kernel(keep, r0, r1, r2, qkv_ref, qv_ref, gains_ref, biases_ref, upb_ref):
    total = keep[0]
    for r in (r0, r1, r2):
        total = total + r[0].astype(F32)
    col = 0
    for first, pairs in zip((0, PARTS[0]), PARTS):
        for third in range(3):
            to = third * ATT + first * 128
            qkv_ref[:, to : to + pairs * 128] = total[:, col : col + pairs * 128]
            col += pairs * 128
    extra = total[:, col : col + EXTRA]
    qv_ref[...] = extra[0:2, :ROWS]
    gains_ref[...] = extra[2:4, :ROWS]
    biases_ref[...] = extra[4:8, :ROWS]
    upb_ref[...] = extra[8:9, :FROWS]


def outputs_call(keep, recvs):
    return pl.pallas_call(
        outputs_kernel,
        out_shape=tuple(
            jax.ShapeDtypeStruct(shape, F32)
            for shape in ((ROWS, 3 * ATT), (2, ROWS), (2, ROWS), (4, ROWS), (1, FROWS))
        ),
        compiler_params=params(16),
        cost_estimate=cost(2),
        name="outputs",
    )(keep, *recvs)


def make_local(groups, members):
    fine = groups * members == UNITS
    axes = ("grp", "dp") if fine else ("grp",)

    def swap(x, even, odd=None):
        pair = (even, even if odd is None else odd)
        return lax.ppermute(x, axes, [(i, i ^ pair[i & 1]) for i in range(UNITS)])

    along_z = ((Z2, Z2), (Z1, Z1), (Z1 ^ Z2, Z1 ^ Z2))
    gather_hops = tuple((hop,) for hop in zip(*GATHER)) + (((CORE, CORE),),)
    scatter_hops = (
        (((CORE, CORE),),) + tuple((hop,) for hop in zip(*SCATTER))[:1:-1] + (along_z,)
    )

    class Gather:
        def __init__(self, x):
            self.state, self.stage = [x[None]], 0

        def start(self):
            self.recv = [swap(self.state[0], *hop) for hop in gather_hops[self.stage]]
            self.stage += 1

        def finish(self, *beside):
            if beside:
                self.recv = after(*self.recv, *beside)[: len(self.recv)]
            if self.stage == len(gather_hops):
                return self.state[0], self.recv[0]
            self.state = [jnp.concatenate([self.state[0], *self.recv], axis=0)]

    class Scatter:
        def __init__(self, keep, send):
            self.state, self.stage = [keep, send], 0

        def start(self):
            hops = scatter_hops[self.stage]
            self.recv = [swap(x, *hop) for x, hop in zip(self.state[1:], hops)]
            self.stage += 1

        def finish(self, *beside):
            if beside:
                self.recv = after(*self.recv, *beside)[: len(self.recv)]
            kept = self.state[0]
            if self.stage == len(scatter_hops):
                total = kept[0]
                for recv in self.recv:
                    total = total + recv[0].astype(F32)
                return total
            parts = len(scatter_hops[self.stage]) + 1
            n = kept.shape[0] // parts
            sums = [
                kept[p * n : (p + 1) * n].astype(F32) + self.recv[0][p * n : (p + 1) * n].astype(F32)
                for p in range(parts)
            ]
            self.state = sums[:1] + [x.astype(SEND) for x in sums[1:]]

    def tie(x, *movers):
        x, *flat = after(x, *(a for m in movers for a in m.state))
        for m in movers:
            m.state, flat = flat[: len(m.state)], flat[len(m.state) :]
        return x

    def local(
        hidden,
        lengths,
        subnet,
        qkv_weight,
        qv_bias,
        out_weight,
        up_weight,
        up_bias,
        down_weight,
        norm_gains,
        bias_rows,
        cotangent,
    ):
        group = lax.axis_index("grp")
        me = group * members + lax.axis_index("dp") if fine else group
        if not fine:
            qkv_weight, out_weight, up_weight, up_bias, down_weight = (
                lax.all_gather(w, "dp", axis=0, tiled=True)
                for w in (qkv_weight, out_weight, up_weight, up_bias, down_weight)
            )
            qv_bias, norm_gains, bias_rows = (
                lax.all_gather(w, "dp", axis=1, tiled=True)
                for w in (qv_bias, norm_gains, bias_rows)
            )
        picks = lax.dynamic_index_in_dim(subnet, group, 0, keepdims=False)
        width = D - (2 - picks[0]) * (D // 6)
        heads = HEADS - (2 - picks[1]) * (HEADS // 6)
        inner = width * (6 + picks[2]) // 2
        sc = jnp.stack([me.astype(jnp.int32), width, heads * HDIM, inner, lengths[0]])

        rows = jnp.concatenate([qv_bias, norm_gains, bias_rows], axis=0)
        extra = jnp.concatenate(
            [
                jnp.pad(rows, ((0, 0), (0, EXTRA - ROWS))),
                jnp.pad(up_bias[None], ((0, ROWS - 9), (0, EXTRA - FROWS))),
            ],
            axis=0,
        )
        side = me & 1

        def pair(shard, *beside):
            n = shard.shape[1] // 2
            mine = lax.dynamic_slice_in_dim(shard, side * n, n, 1)
            recv = swap(lax.dynamic_slice_in_dim(shard, (1 - side) * n, n, 1), CORE)
            ordered = [jnp.where(side == 0, mine, recv), jnp.where(side == 0, recv, mine)]
            return jnp.concatenate(ordered, axis=0)

        extra = jnp.pad(extra, ((0, 0), (0, EXTRA)))
        q = pair(jnp.concatenate([qkv_weight, extra], axis=1))
        half = PAIRS // 2
        q = Gather(q)
        q.start()
        q.finish()
        u = pair(jnp.concatenate([tie(out_weight, q), up_weight], axis=1))
        q.start()
        q.finish()
        u = Gather(tie(u, q))
        q.start()
        u.start()
        q.finish()
        u.finish()
        u.state = [tie(u.state[0], q)]
        q.start()
        u.start()
        q.finish()
        u.finish()
        u.state = [tie(u.state[0], q)]
        q.start()
        u.start()
        d = Gather(tie(down_weight, u))
        d.start()
        q0, q1 = q.finish()
        qkv, small, upb = qkv_call(sc, hidden, q0, q1)
        u.finish(small)
        d.finish(small)
        qkv = tie(qkv, u, d)
        u.start()
        d.start()
        ctx0, e0, inv0 = attend_call(sc, qkv, 0, PARTS[0])
        u.finish(inv0)
        d.finish(inv0)
        qkv = tie(qkv, u, d)
        u.start()
        d.start()
        ctx1, e1, inv1 = attend_call(sc, qkv, PARTS[0], PARTS[1])
        d.finish(inv1)
        ctx1 = tie(ctx1, d)
        d.start()
        u0, u1 = u.finish(inv1)
        first, nlow, act, slope = rise_call(sc, ctx0, ctx1, hidden, small, upb, u0, u1)
        d.finish(first)
        d.start()
        d0, d1 = d.finish()
        output, fgrad, pgrad, agrad, first_grad, cgrad, sums, usum = fall_call(
            sc, first, act, slope, cotangent, small, u0, u1, d0, d1
        )

        def step(beside, *movers):
            for m in movers:
                m.finish(beside)
                m.start()

        part0, part1 = (0, ctx0, e0, inv0), (PARTS[0], ctx1, e1, inv1)
        dn = Scatter(*down_call(sc, act, fgrad))
        dn.start()
        uk, us = up_call(sc, ctx0, ctx1, agrad, nlow, tie(pgrad, dn))
        up = Scatter(uk, us)
        step(uk, dn)
        up.start()
        g0 = attend_back_call(sc, qkv, tie(cgrad, dn, up), part0, 0, 2)
        step(g0, dn, up)
        g1 = attend_back_call(sc, qkv, tie(cgrad, dn, up), part0, 2, 2)
        step(g1, dn)
        qk, qs, qv = qterm_call(sc, hidden, (g0, tie(g1, dn)), sums, usum)
        qa = Scatter(qk, qs)
        step(qv, up)
        qa.start()
        g2 = attend_back_call(sc, qkv, tie(cgrad, qa, up), part1, 0, PARTS[1])
        step(g2, up, qa)
        down = dn.finish(g2)
        g2, down = after(tie(g2, up, qa), down)
        qk, qs = qterm_call(sc, hidden, (g2,), sums, usum, qv)
        qb = Scatter(qk, qs)
        qb.start()
        step(qk, qa)
        qb.finish(qa.state[1])
        qb.start()
        grad_hidden = input_call(sc, (g0, g1, g2), q0, q1, tie(first_grad, qb, qa))
        step(grad_hidden, qb)
        qa.finish(qb.state[1])
        up = up.finish(qa.state[1])
        qb.finish()
        both = Scatter(None, None)
        both.state = [jnp.concatenate(x, axis=2) for x in zip(qa.state, qb.state)]
        both.state[0], up = after(both.state[0], up)
        both.stage = qa.stage
        both.start()
        qkv_sum, qv_sum, gains_sum, biases_sum, upb_sum = outputs_call(both.state[0], both.recv)
        grads = (
            qkv_sum,
            qv_sum,
            up[:, :D],
            up[:, D:],
            upb_sum.reshape(FROWS),
            down,
            gains_sum,
            biases_sum,
        )
        if not fine:
            dims = (0, 1, 0, 0, 0, 0, 1, 1)
            grads = tuple(
                lax.psum_scatter(g, "dp", scatter_dimension=d, tiled=True)
                for g, d in zip(grads, dims)
            )
        return (output, grad_hidden) + grads

    return local


def solution(mesh):
    both = ("grp", "dp")
    row, col, flat = P(both, None), P(None, both), P(both)
    placed = (row, flat, P(), row, col, row, row, flat, row, col, col, row)
    return jax.shard_map(
        make_local(mesh.shape["grp"], mesh.shape["dp"]),
        mesh=mesh,
        in_specs=placed,
        out_specs=(row, row, row, col, row, row, flat, row, col, col),
        check_vma=False,
    )
```
